32 devices in a mesh: fsdp: 2 (over y), ctx: 8 (over z, core), tp: 2 (over x).
Axes of the slice: x: 2, y: 2, z: 4, core: 2. Of those that a mesh axis runs over, the one named last changes fastest.
Arguments:
- byte_ids: int32 [4096], P(('fsdp', 'ctx')), may hold values from 0 to 258
- seq_tokens: int32 [2, 4], replicated, may hold values from 16 to 512, as said below
- pad_bytes: int32 [2, 4], replicated, may hold values from 0 to 24, as said below
- deal_targets: int32 [2, 8, 8], replicated, may hold values from 0 to 7, each once within a row
- rel_buckets: int32 [257], replicated, may hold values from 0 to 31
- embedding: bfloat16 [259, 768], P(None, 'fsdp'), may hold values from -6 to 6
- conv_weight: bfloat16 [4, 768], P(None, 'fsdp'), may hold values from -3 to 3
- conv_bias: bfloat16 [768], P('fsdp'), may hold values from -3 to 3
- score_weight: bfloat16 [768], P('fsdp'), may hold values from -0.59765625 to 0.59765625
- attn_gain: bfloat16 [768], P('fsdp'), may hold values from 0.5 to 1.5
- query_weight: bfloat16 [768, 768], P('fsdp', 'tp'), may hold values from -0.21875 to 0.21875
- key_weight: bfloat16 [768, 768], P('fsdp', 'tp'), may hold values from -0.21875 to 0.21875
- value_weight: bfloat16 [768, 768], P('fsdp', 'tp'), may hold values from -0.21875 to 0.21875
- rel_bias: bfloat16 [32, 12], P('fsdp', 'tp'), may hold values from -4 to 4
- out_weight: bfloat16 [768, 768], P('tp', 'fsdp'), may hold values from -1.75 to 1.75
- mlp_gain: bfloat16 [768], P('fsdp'), may hold values from 0.5 to 1.5
- gate_weight: bfloat16 [768, 2048], P('fsdp', 'tp'), may hold values from -0.21875 to 0.21875
- up_weight: bfloat16 [768, 2048], P('fsdp', 'tp'), may hold values from -0.21875 to 0.21875
- down_weight: bfloat16 [2048, 768], P('tp', 'fsdp'), may hold values from -0.1875 to 0.1875
- teacher: bfloat16 [2048, 768], P(('fsdp', 'ctx')), may hold values from -6 to 6
Outputs:
- output: bfloat16 [2048, 768], P(('fsdp', 'ctx'), 'tp')
- embedding_grad: float32 [259, 768], P(None, 'fsdp')
- conv_weight_grad: float32 [4, 768], P(None, 'fsdp')
- conv_bias_grad: float32 [768], P('fsdp')
- score_weight_grad: float32 [768], P('fsdp')
- attn_gain_grad: float32 [768], P('fsdp')
- query_weight_grad: float32 [768, 768], P('fsdp', 'tp')
- key_weight_grad: float32 [768, 768], P('fsdp', 'tp')
- value_weight_grad: float32 [768, 768], P('fsdp', 'tp')
- rel_bias_grad: float32 [32, 12], P('fsdp', 'tp')
- out_weight_grad: float32 [768, 768], P('tp', 'fsdp')
- mlp_gain_grad: float32 [768], P('fsdp')
- gate_weight_grad: float32 [768, 2048], P('fsdp', 'tp')
- up_weight_grad: float32 [768, 2048], P('fsdp', 'tp')
- down_weight_grad: float32 [2048, 768], P('tp', 'fsdp')
- loss: float32 [], replicated
The draws below stay inside these ranges and needn't reach their ends.
Inputs may be any that keep to these rules, and one draw needn't show every extreme that they name: `seq_tokens`: row f lists the token lengths of the 4 sequences packed in order into pack f; a row sums to 1024 and its largest entry is exactly 512. `pad_bytes`: padding bytes that end each sequence's 2 seq_tokens bytes; every row has an entry equal to 24. deal_targets[f, d, s] is the device along ctx that receives block s of 16 tokens of device d in pack f; each device receives one block from every device of its pack.
All inputs are finite; a program needn't handle non-finite values.
Results may differ from the reference program's by a relative error of at most 0.013.
Values may be sent and summed in bfloat16 or wider, within the bound.
No kernel may reach another device: no remote copies, remote signals or barrier semaphores. Data moves between devices by JAX's collectives and lax.ppermute only.
A program may use at most 256 MiB of HBM per device.

```python
import math
import jax
import jax.numpy as jnp
import numpy as np
from jax import lax

D = 768
H = 12
DH = 64
FF = 2048
VOCAB = 259
NB = 32
RMAX = 128
CONV = 4
BLOCKS = 4
SEQS = 4
MINSPAN = 16
PADMAX = 24
TOK_DEV = 128
UNIT = 16
TOK_PACK = 1024
TOKENS = 2048
BYTES = 4096
N_FSDP = 2
N_CTX = 8


def pack_layout(key):
    spread_key = jax.random.fold_in(key, 11)
    order_key = jax.random.fold_in(key, 12)
    padding_key = jax.random.fold_in(key, 13)
    choice_key = jax.random.fold_in(key, 14)
    largest = TOK_PACK // 2
    remain = TOK_PACK - largest
    shares_raw = jax.random.randint(spread_key, (N_FSDP, SEQS - 1), 1, 9)
    spare = remain - (SEQS - 1) * MINSPAN
    shares = MINSPAN + spare * shares_raw // jnp.sum(shares_raw, axis=1, keepdims=True)
    closing = remain - jnp.sum(shares[:, :-1], axis=1)
    pieces = jnp.concatenate([jnp.full((N_FSDP, 1), largest, jnp.int32), shares[:, :-1].astype(jnp.int32), closing[:, None].astype(jnp.int32)], axis=1)
    ranks = jax.random.randint(order_key, (N_FSDP, SEQS), 0, 1024) * SEQS + jnp.arange(SEQS, dtype=jnp.int32)[None, :]
    order = jnp.argsort(ranks, axis=1)
    lengths = jnp.take_along_axis(pieces, order, axis=1)
    padding = jax.random.randint(padding_key, (N_FSDP, SEQS), 0, PADMAX + 1)
    chosen = jax.random.randint(choice_key, (N_FSDP, 1), 0, SEQS)
    padding = jnp.where(jnp.arange(SEQS, dtype=jnp.int32)[None, :] == chosen, PADMAX, padding)
    return (lengths.astype(jnp.int32), padding.astype(jnp.int32))


def draw_seq_tokens(key, part):
    lengths, padding = pack_layout(key)
    return lengths


def draw_pad_bytes(key, part):
    lengths, padding = pack_layout(key)
    return padding


def set_ends(values, stream_key, low, high):
    extent = values.shape
    spot = [jax.random.randint(jax.random.fold_in(stream_key, axis), (), 0, extent[axis]) for axis in range(len(extent))]
    values = values.at[tuple(spot)].set(low)
    longest = extent.index(max(extent))
    spot[longest] = (spot[longest] + 1) % extent[longest]
    return values.at[tuple(spot)].set(high)


def steps_of(own_key, shape, split, low, top_value):
    level = 1.0
    for axis_at, shards_of in split:
        steps = jax.random.uniform(jax.random.fold_in(jax.random.fold_in(own_key, 6), axis_at), (shards_of,), jnp.float32, low / len(split), top_value / len(split))
        level = level * jnp.repeat(jnp.exp(steps), shape[axis_at] // shards_of).reshape((-1,) + (1,) * (len(shape) - 1 - axis_at))
    return level


def cumulative_ranks(amount, slope):
    loads = [(1 << 20) // math.isqrt(rank ** slope) + 1 for rank in range(1, amount + 1)]
    deviation = 1 + sum(loads) // (1 << 30)
    return np.cumsum(np.array([max(1, weight // deviation) for weight in loads]))


def ranked(key, dims, number_of, lean):
    table = cumulative_ranks(number_of, lean)
    pick = jax.random.randint(jax.random.fold_in(key, 1), dims, 0, int(table[number_of - 1]))
    grade = jnp.searchsorted(jnp.asarray(table, jnp.int32), pick, side="right")
    return jax.random.permutation(jax.random.fold_in(key, 2), number_of)[grade].astype(jnp.int32)


def centred(rng, shape, deviation, reach, cuts=(), kind=jnp.bfloat16):
    entries = deviation * jax.random.normal(rng, shape, jnp.float32)
    if cuts:
        entries = entries * steps_of(rng, shape, cuts, -0.22, 0.18)
    return jnp.clip(entries, -reach, reach).astype(kind)


def setup_inputs(seed: int = 0) -> dict:
    key_list = jax.random.split(jax.random.key(seed), 21)
    return {
        "byte_ids": set_ends(ranked(key_list[0], (BYTES,), VOCAB, 1), jax.random.fold_in(key_list[0], 3), 0, VOCAB - 1).astype(jnp.int32),
        "seq_tokens": draw_seq_tokens(jax.random.fold_in(key_list[20], 71), 0),
        "pad_bytes": draw_pad_bytes(jax.random.fold_in(key_list[20], 71), 0),
        "deal_targets": jax.vmap(lambda own: jax.random.permutation(own, N_CTX))(jax.random.split(key_list[3], N_FSDP * N_CTX)).reshape((N_FSDP, N_CTX, N_CTX)).astype(jnp.int32),
        "rel_buckets": set_ends(jax.random.randint(key_list[4], (2 * RMAX + 1,), 0, NB), jax.random.fold_in(key_list[4], 1), 0, NB - 1).astype(jnp.int32),
        "embedding": centred(key_list[5], (VOCAB, D), 1.0, 6.0, ((1, 2),)),
        "conv_weight": centred(key_list[6], (CONV, D), CONV ** -0.5, 3.0, ((1, 2),)),
        "conv_bias": centred(key_list[7], (D,), 0.5, 3.0, ((0, 2),)),
        "score_weight": centred(key_list[8], (D,), 0.1, 0.59765625, ((0, 2),)),
        "attn_gain": jnp.clip(1.0 + 0.1 * jax.random.normal(key_list[9], (D,), jnp.float32), 0.5, 1.5).astype(jnp.bfloat16),
        "query_weight": centred(key_list[10], (D, D), D ** -0.5, 0.21875, ((0, 2), (1, 2))),
        "key_weight": centred(key_list[11], (D, D), D ** -0.5, 0.21875, ((0, 2), (1, 2))),
        "value_weight": centred(key_list[12], (D, D), D ** -0.5, 0.21875, ((0, 2), (1, 2))),
        "rel_bias": centred(key_list[13], (NB, H), 1.0, 4.0, ((0, 2), (1, 2))),
        "out_weight": centred(key_list[14], (D, D), (D // 64) ** -0.5, 1.75, ((0, 2), (1, 2))),
        "mlp_gain": jnp.clip(1.0 + 0.1 * jax.random.normal(key_list[15], (D,), jnp.float32), 0.5, 1.5).astype(jnp.bfloat16),
        "gate_weight": centred(key_list[16], (D, FF), D ** -0.5, 0.21875, ((0, 2), (1, 2))),
        "up_weight": centred(key_list[17], (D, FF), D ** -0.5, 0.21875, ((0, 2), (1, 2))),
        "down_weight": centred(key_list[18], (FF, D), (FF // 2) ** -0.5, 0.1875, ((0, 2), (1, 2))),
        "teacher": centred(key_list[19], (TOKENS, D), 1.0, 6.0, ((0, 16),)),
    }


eps_norm = 1e-06
neg_fill = -1e+30
grad_scale = 65536.0
rim_cells = 6

@jax.custom_vjp
def low(v):
    return lax.optimization_barrier(v.astype(jnp.bfloat16)).astype(jnp.float32)

@jax.custom_vjp
def low_back(v):
    return v

def low_keep(v):
    return (low(v), None)

def low_pass(kept, grad):
    return (grad,)

def back_keep(v):
    return (v, None)

def back_low(kept, grad):
    return (low(grad),)
low.defvjp(low_keep, low_pass)
low_back.defvjp(back_keep, back_low)

def pack_tables(lengths, padding):
    token_start = jnp.cumsum(lengths) - lengths
    return (token_start, token_start + lengths, 2 * lengths - padding)

def byte_layout(places, token_start, token_end, real_bytes, pack_bytes):
    seq_count = token_start.shape[0]
    choose = jnp.arange(seq_count, dtype=jnp.int32)
    seg_index = lax.optimization_barrier(jnp.sum((places[:, None] >= 2 * token_start[None, 1:]).astype(jnp.int32), axis=1))
    matches = (seg_index[:, None] == choose[None, :]).astype(jnp.int32)
    seq_begin = lax.optimization_barrier(jnp.sum(matches * (2 * token_start)[None, :], axis=1))
    seq_finish = lax.optimization_barrier(jnp.sum(matches * (2 * token_end)[None, :], axis=1))
    byte_limit = lax.optimization_barrier(jnp.sum(matches * real_bytes[None, :], axis=1))
    inside = (places >= 0) & (places < pack_bytes)
    seg_code = jnp.where(places < 0, -1, jnp.where(places >= pack_bytes, seq_count, seg_index))
    is_real = inside & (places - seq_begin < byte_limit)
    return (seg_code, seq_begin, seq_finish, is_real)

def token_layout(natural, token_start, real_bytes):
    seq_count = token_start.shape[0]
    seg_index = lax.optimization_barrier(jnp.sum((natural[:, None] >= token_start[None, 1:]).astype(jnp.int32), axis=1))
    matches = (seg_index[:, None] == jnp.arange(seq_count, dtype=jnp.int32)[None, :]).astype(jnp.int32)
    seq_begin = lax.optimization_barrier(jnp.sum(matches * token_start[None, :], axis=1))
    byte_limit = lax.optimization_barrier(jnp.sum(matches * real_bytes[None, :], axis=1))
    within = natural - seq_begin
    return (seg_index, within, 2 * within < byte_limit)

def gbst_core(embedded, seg_code, places, seq_begin, seq_finish, conv_weight, conv_bias, score_weight):
    length = embedded.shape[0]
    inner_len = length - 2 * rim_cells
    conv_len = length - 3
    centre = seg_code[1:1 + conv_len]
    conv_out = jnp.broadcast_to(conv_bias[None, :], (conv_len, embedded.shape[1]))
    for tap_index in range(CONV):
        same_seq = (seg_code[tap_index:tap_index + conv_len] == centre).astype(jnp.float32)
        conv_out = conv_out + conv_weight[tap_index][None, :] * embedded[tap_index:tap_index + conv_len] * same_seq[:, None]
    position = places[rim_cells:rim_cells + inner_len]
    start_in = seq_begin[rim_cells:rim_cells + inner_len]
    end_in = seq_finish[rim_cells:rim_cells + inner_len]
    anchor = rim_cells - 1
    pooled = []
    for block_width in range(1, BLOCKS + 1):
        block_start = start_in + block_width * ((position - start_in) // block_width)
        block_end = jnp.minimum(block_start + block_width, end_in)
        block_sum = jnp.zeros((inner_len, embedded.shape[1]), jnp.float32)
        for offset in range(1 - block_width, block_width):
            member = ((position + offset >= block_start) & (position + offset < block_end)).astype(jnp.float32)
            block_sum = block_sum + member[:, None] * conv_out[anchor + offset:anchor + offset + inner_len]
        pooled.append(block_sum / (block_end - block_start).astype(jnp.float32)[:, None])
    stacked = jnp.stack(pooled, axis=1)
    scores = lax.optimization_barrier(jnp.sum(stacked * score_weight[None, None, :], axis=2))
    weights = jax.nn.softmax(scores, axis=1)
    blended = lax.optimization_barrier(jnp.sum(weights[:, :, None] * stacked, axis=1))
    return blended.reshape(inner_len // 2, 2, -1).mean(axis=1)

def rms_scale(values, gain_vec):
    return values * lax.rsqrt(lax.optimization_barrier(jnp.mean(values * values, axis=-1, keepdims=True)) + eps_norm) * gain_vec

def geglu_value(gate_in, up_in):
    return jax.nn.gelu(gate_in, approximate=True) * up_in

def pack_forward(params, ids_pack, lengths, padding, targets, teacher_pack, rel_buckets):
    byte_table, conv_taps, conv_shift, score_vec, gain_one, query_proj, key_proj, value_proj, bias_table, out_proj, gain_two, gate_proj, up_proj, down_proj = params
    highest = lax.Precision.HIGHEST
    pack_bytes = 2 * TOK_PACK
    token_start, token_end, real_bytes = pack_tables(lengths, padding)
    places = jnp.arange(pack_bytes + 2 * rim_cells, dtype=jnp.int32) - rim_cells
    seg_code, seq_begin, seq_finish, is_real = byte_layout(places, token_start, token_end, real_bytes, pack_bytes)
    symbols = jnp.pad(ids_pack, rim_cells)
    embedded = jnp.take(byte_table, symbols, axis=0) * is_real[:, None].astype(jnp.float32)
    hidden0 = low_back(low(gbst_core(embedded, seg_code, places, seq_begin, seq_finish, conv_taps, conv_shift, score_vec)))
    natural = jnp.arange(TOK_PACK, dtype=jnp.int32)
    seg_tok, place_tok, valid_tok = token_layout(natural, token_start, real_bytes)
    normed1 = low(rms_scale(hidden0, gain_one))
    queries = low_back(low(jnp.dot(normed1, query_proj, precision=highest)))
    keys = low_back(low(jnp.dot(normed1, key_proj, precision=highest)))
    values = low_back(low(jnp.dot(normed1, value_proj, precision=highest)))
    head_bias = jnp.take(bias_table, rel_buckets, axis=0)
    query_heads = queries.reshape(TOK_PACK, H, DH)
    key_heads = keys.reshape(TOK_PACK, H, DH)
    value_heads = values.reshape(TOK_PACK, H, DH)
    rows_per = math.gcd(TOK_PACK, 512)

    def attend(block_index):
        first_row = block_index * rows_per
        query_rows = lax.dynamic_slice_in_dim(query_heads, first_row, rows_per)
        query_seg = lax.dynamic_slice_in_dim(seg_tok, first_row, rows_per)
        query_place = lax.dynamic_slice_in_dim(place_tok, first_row, rows_per)
        raw_dots = jnp.einsum('qhd,khd->hqk', query_rows, key_heads, precision=highest)
        offsets = jnp.clip(place_tok[None, :] - query_place[:, None], -RMAX, RMAX) + RMAX
        bias_block = jnp.transpose(jnp.take(head_bias, offsets, axis=0), (2, 0, 1))
        scores = low_back(raw_dots * (1.0 / math.sqrt(DH)) + bias_block)
        allowed = (query_seg[:, None] == seg_tok[None, :]) & valid_tok[None, :]
        scores = jnp.where(allowed[None], scores, neg_fill)
        probs = low(jax.nn.softmax(scores, axis=-1))
        return jnp.einsum('hqk,khd->qhd', probs, value_heads, precision=highest)
    attended = lax.map(jax.checkpoint(attend), jnp.arange(TOK_PACK // rows_per, dtype=jnp.int32))
    attended = low_back(low(attended.reshape(TOK_PACK, D)))
    residual1 = hidden0 + low_back(jnp.dot(attended, out_proj, precision=highest))
    normed2 = low(rms_scale(residual1, gain_two))
    gate = low_back(jnp.dot(normed2, gate_proj, precision=highest))
    up_value = low_back(jnp.dot(normed2, up_proj, precision=highest))
    gated = low(geglu_value(gate, up_value))
    result = residual1 + low_back(jnp.dot(gated, down_proj, precision=highest))
    source = natural // TOK_DEV
    slot_index = natural % TOK_DEV // UNIT
    dealt_row = jnp.take(targets.reshape(-1), source * N_CTX + slot_index) * TOK_DEV + source * UNIT + natural % UNIT
    teacher_nat = jnp.take(teacher_pack, dealt_row, axis=0)
    difference = (result - teacher_nat) * valid_tok[:, None].astype(jnp.float32)
    return (result, jnp.sum(difference * difference))

def reference(byte_ids, seq_tokens, pad_bytes, deal_targets, rel_buckets, embedding, conv_weight, conv_bias, score_weight, attn_gain, query_weight, key_weight, value_weight, rel_bias, out_weight, mlp_gain, gate_weight, up_weight, down_weight, teacher):
    weights = tuple((array_in.astype(jnp.float32) for array_in in (embedding, conv_weight, conv_bias, score_weight, attn_gain, query_weight, key_weight, value_weight, rel_bias, out_weight, mlp_gain, gate_weight, up_weight, down_weight)))
    ids_packs = byte_ids.reshape(N_FSDP, 2 * TOK_PACK)
    teacher_packs = teacher.astype(jnp.float32).reshape(N_FSDP, TOK_PACK, D)
    real_count = jnp.sum((2 * seq_tokens - pad_bytes + 1) // 2).astype(jnp.float32)

    def objective(*params):

        def one_pack(packed):
            ids_pack, lengths, padding, targets, teacher_pack = packed
            return pack_forward(params, ids_pack, lengths, padding, targets, teacher_pack, rel_buckets)
        results, squares = lax.map(jax.checkpoint(one_pack), (ids_packs, seq_tokens, pad_bytes, deal_targets, teacher_packs))
        loss = jnp.sum(squares) / (2.0 * D * real_count)
        return (grad_scale * loss, (results, loss))
    scaled, back_fn, extras = jax.vjp(objective, *weights, has_aux=True)
    grads = back_fn(jnp.ones_like(scaled))
    results, loss = extras
    output = results.reshape(TOKENS, D).astype(jnp.bfloat16)
    return (output, grads[0], grads[1], grads[2], grads[3], grads[4], grads[5], grads[6], grads[7], grads[8], grads[9], grads[10], grads[11], grads[12], grads[13], loss)
```

```python
import functools
import math

import jax
import jax.numpy as jnp
from jax import lax
from jax.experimental import pallas as pl
from jax.experimental.pallas import tpu as pltpu
from jax.sharding import PartitionSpec as P

D = 768
DH = 64
VOCAB = 259
NB = 32
RMAX = 128
CONV = 4

EPS = 1e-06
NEG = -1e30
GRAD_SCALE = 65536.0
LANES = 128
BLK = 128
HALO = 8
WIN = BLK + 2 * HALO
VP = 384
SROWS = 288
TAP_ROW = VOCAB
SHIFT_ROW = VOCAB + 4
SCORE_ROW = VOCAB + 5
GAIN1_ROW = VOCAB + 6
GAIN2_ROW = VOCAB + 7
BIAS_ROW = 272
f32 = jnp.float32
bf16 = jnp.bfloat16
i32 = jnp.int32
HI = lax.Precision.HIGHEST
ANY = pl.BlockSpec(memory_space=pl.ANY)
VM = pl.BlockSpec(memory_space=pltpu.VMEM)
SM = pl.BlockSpec(memory_space=pltpu.SMEM)


def nn(a, b, **k):
    return lax.dot_general(a, b, (((1,), (0,)), ((), ())), preferred_element_type=f32, **k)


def nt(a, b, **k):
    return lax.dot_general(a, b, (((1,), (1,)), ((), ())), preferred_element_type=f32, **k)


def tn(a, b, **k):
    return lax.dot_general(a, b, (((0,), (0,)), ((), ())), preferred_element_type=f32, **k)


def iota(shape, axis):
    return lax.broadcasted_iota(i32, shape, axis)


def aligned(index, step):
    return pl.multiple_of(index * step, step)


class Layout:
    pass


def token_rows(len_ref, pad_ref, fs, total, first=0):
    t = iota((1, total), 1) + first
    start = jnp.zeros_like(t)
    end = jnp.zeros_like(t)
    limit = jnp.zeros_like(t)
    seg = jnp.zeros_like(t)
    base = jnp.int32(0)
    for k in range(len_ref.shape[1]):
        n = len_ref[fs, k]
        inside = t >= base
        start = jnp.where(inside, base, start)
        end = jnp.where(inside, base + n, end)
        limit = jnp.where(inside, 2 * n - pad_ref[fs, k], limit)
        seg = jnp.where(inside, k, seg)
        base = base + n
    lay = Layout()
    rel = t - start
    lay.seg = seg
    lay.real_e = 2 * rel < limit
    lay.real_o = 2 * rel + 1 < limit
    lay.prev = (rel > 0).astype(f32)
    lay.v = (t + 1 < end).astype(f32)
    third = (rel * 43691) >> 17
    u = rel - 3 * third
    lay.u0 = (u == 0).astype(f32)
    lay.u1 = (u == 1).astype(f32)
    lay.u2 = (u == 2).astype(f32)
    lay.odd = (rel & 1).astype(f32)
    lay.even = 1.0 - lay.odd
    third_f = jnp.float32(1.0 / 3.0)
    last0 = jnp.where(t + 1 < end, third_f, 0.5)
    lay.inv_e3 = jnp.where(u == 0, last0, third_f)
    lay.inv_o3 = jnp.where(u == 0, last0, jnp.where(u == 1, jnp.where(t + 1 < end, third_f, 1.0), third_f))
    lay.inv4 = jnp.where((rel & 1) == 1, 0.25, jnp.where(t + 1 < end, 0.25, 0.5))
    return lay


def forms(x, lay):
    em, om, e0, o0, ep, op = x
    pair = e0 + o0
    after = lay.v * (ep + op)
    first = pair + lay.v * ep
    closing = om + pair
    p2 = 0.5 * pair
    e3 = (lay.u0 * first + lay.u1 * (em + om + e0) + lay.u2 * closing) * lay.inv_e3
    o3 = (lay.u0 * first + lay.u1 * (o0 + after) + lay.u2 * closing) * lay.inv_o3
    p4 = (pair + lay.odd * (em + om) + lay.even * after) * lay.inv4
    return (e0, p2, e3, p4), (o0, p2, o3, p4)


def spread(we, wo, lay):
    e1, e2, e3, e4 = we
    o1, o2, o3, o4 = wo
    e3 = e3 * lay.inv_e3
    o3 = o3 * lay.inv_o3
    both = e3 + o3
    p4 = (e4 + o4) * lay.inv4
    p2 = (e2 + o2) * 0.5
    edge = lay.u0 * both + lay.u2 * both
    em = lay.u1 * e3 + lay.odd * p4
    om = em + lay.u2 * both
    e0 = e1 + p2 + edge + lay.u1 * e3 + p4
    o0 = o1 + p2 + edge + lay.u1 * o3 + p4
    op = lay.v * (lay.u1 * o3 + lay.even * p4)
    ep = op + lay.v * lay.u0 * both
    return em, om, e0, o0, ep, op


def before(row):
    return pltpu.roll(row, 1, 1)


def after(row):
    return pltpu.roll(row, row.shape[1] - 1, 1)


def softmax4(s):
    top = jnp.maximum(jnp.maximum(s[0], s[1]), jnp.maximum(s[2], s[3]))
    e = [jnp.exp(x - top) for x in s]
    inv = 1.0 / (e[0] + e[1] + e[2] + e[3])
    return [x * inv for x in e]


def put_rows(rows, total):
    sub = iota((8, total), 0)
    out = jnp.zeros((8, total), f32)
    for k, r in enumerate(rows):
        out = jnp.where(sub == k, jnp.broadcast_to(r, (8, total)), out)
    return out


def get_row(block, k):
    return jnp.sum(jnp.where(iota(block.shape, 0) == k, block, 0.0), axis=0, keepdims=True)


def eye():
    return (iota((BLK, BLK), 0) == iota((BLK, BLK), 1)).astype(f32)


def byte_scores(sc, lay, shift_score):
    ge = [get_row(sc.ge[...], k) for k in range(4)]
    go = [get_row(sc.go[...], k) for k in range(4)]
    ze = lay.prev * before(go[0]) + ge[1] + go[2] + lay.v * after(ge[3]) + shift_score
    zo = ge[0] + go[1] + lay.v * after(ge[2]) + lay.v * after(go[3]) + shift_score
    return ze, zo


def neighbours(e, o):
    return before(e), before(o), e, o, after(e), after(o)


def param_rows(tab_ref):
    rows = tab_ref[VOCAB - 3 : VOCAB + 13, :].astype(f32)
    return lambda k: rows[k - VOCAB + 3 : k - VOCAB + 4, :]


def front(sc, len_ref, pad_ref, fs, ids_ref, total):
    lay = token_rows(len_ref, pad_ref, fs, total)
    ids_e = jnp.where(lay.real_e, ids_ref[0:1, :], -1).astype(f32)
    ids_o = jnp.where(lay.real_o, ids_ref[1:2, :], -1).astype(f32)
    sc.idr[...] = put_rows([ids_e, ids_o], total)
    row = param_rows(sc.tab)
    score = row(SCORE_ROW)
    sub = iota((16, D), 0)
    cw = jnp.zeros((16, D), f32)
    for k in range(CONV):
        cw = jnp.where(sub == k, jnp.broadcast_to(row(TAP_ROW + k) * score, (16, D)), cw)
    cw = jnp.where(sub == 4, jnp.broadcast_to(score, (16, D)), cw)
    g = nt(cw, sc.tab[...].astype(f32), precision=HI)
    g0 = g.astype(bf16)
    rest = g - g0.astype(f32)
    g1 = rest.astype(bf16)
    g2 = (rest - g1.astype(f32)).astype(bf16)
    shift_score = jnp.sum(row(SHIFT_ROW) * score, axis=1, keepdims=True)
    zero = jnp.zeros((HALO, D), f32)
    for plane in (sc.ee, sc.eo):
        plane[0:HALO, :] = zero
        plane[total + HALO : total + 2 * HALO, :] = zero
    sc.cols[0:HALO, :] = jnp.zeros((HALO, LANES), f32)
    sc.cols[total + HALO : total + 2 * HALO, :] = jnp.zeros((HALO, LANES), f32)
    unit = eye()
    lane = iota((BLK, VP), 1).astype(f32)

    def embed(b, carry):
        cols = pl.ds(aligned(b, BLK), BLK)
        rows = pl.ds(pl.multiple_of(b * BLK + HALO, HALO), BLK)
        ids = nt(unit, sc.idr[:, cols], precision=HI)
        for k, plane, dots in ((0, sc.ee, sc.ge), (1, sc.eo, sc.go)):
            hot = (lane == ids[:, k : k + 1]).astype(bf16)
            plane[rows, :] = nn(hot, sc.tab[...])
            picked = nt(g0, hot) + nt(g1, hot) + nt(g2, hot)
            dots[:, cols] = picked[0:8]
        return carry

    lax.fori_loop(0, total // BLK, embed, 0)
    ze, zo = byte_scores(sc, lay, shift_score)
    se, so = forms(neighbours(ze, zo), lay)
    we, wo = softmax4(se), softmax4(so)
    em, om, e0, o0, ep, op = spread(we, wo, lay)
    half = jnp.float32(0.5)
    sc.idr[...] = put_rows(
        [half * e0, half * o0, half * after(em), half * after(om), half * before(ep), half * before(op), lay.prev, lay.v],
        total,
    )

    def turn(b, carry):
        rows = pl.ds(pl.multiple_of(b * BLK + HALO, HALO), BLK)
        sc.cols[rows, 0:8] = nt(unit, sc.idr[:, pl.ds(aligned(b, BLK), BLK)], precision=HI)
        return carry

    lax.fori_loop(0, total // BLK, turn, 0)
    return lay, we, wo, row


def up1(x):
    return pltpu.roll(x, 1, 0)


def down1(x):
    return pltpu.roll(x, WIN - 1, 0)


def conv_window(sc, win, lanes, row, pv, nx):
    ee = sc.ee[win, lanes]
    eo = sc.eo[win, lanes]
    eo_p = up1(eo) * pv
    ee_n = down1(ee) * nx
    eo_n = down1(eo) * nx
    c = [row(TAP_ROW + k)[:, lanes] for k in range(CONV)]
    b = row(SHIFT_ROW)[:, lanes]
    ce = b + c[0] * eo_p + c[1] * ee + c[2] * eo + c[3] * ee_n
    co = b + c[0] * ee + c[1] * eo + c[2] * ee_n + c[3] * eo_n
    return ee, eo, eo_p, ee_n, eo_n, c, ce, co


def front_scratch(total):
    return [
        pltpu.VMEM((VP, D), bf16),
        pltpu.VMEM((total + 2 * HALO, D), f32),
        pltpu.VMEM((total + 2 * HALO, D), f32),
        pltpu.VMEM((8, total), f32),
        pltpu.VMEM((8, total), f32),
        pltpu.VMEM((8, total), f32),
        pltpu.VMEM((total + 2 * HALO, LANES), f32),
    ]


def front_refs(refs):
    sc = Layout()
    sc.tab, sc.ee, sc.eo, sc.idr, sc.ge, sc.go, sc.cols = refs
    return sc


def run_copies(copies, sems):
    made = [pltpu.make_async_copy(s, d, sems.at[k]) for k, (s, d) in enumerate(copies)]
    for c in made:
        c.start()
    return made


def g_kernel(total, pieces, meta, len_ref, pad_ref, ids_ref, *refs):
    n = 2 if pieces else 1
    parts = refs[:n]
    tab_out, hid_out, n1_out = refs[n : n + 3]
    sc = front_refs(refs[n + 3 : n + 10])
    sems = refs[n + 10]
    fs = meta[0]
    if pieces:
        w = D // 2
        copies = [
            (parts[0], sc.tab.at[pl.ds(0, SROWS), pl.ds(aligned(fs, w), w)]),
            (parts[1], sc.tab.at[pl.ds(0, SROWS), pl.ds(aligned(1 - fs, w), w)]),
        ]
    else:
        copies = [(parts[0], sc.tab.at[pl.ds(0, SROWS), :])]
    made = run_copies(copies, sems)
    sc.tab[SROWS:VP, :] = jnp.zeros((VP - SROWS, D), bf16)
    for c in made:
        c.wait()
    tab_out[...] = sc.tab[...]
    _, _, _, row = front(sc, len_ref, pad_ref, fs, ids_ref, total)
    gain = row(GAIN1_ROW)

    def block(b, carry):
        win = pl.ds(aligned(b, BLK), WIN)
        rows = pl.ds(aligned(b, BLK), BLK)
        cols = sc.cols[win, :]
        col = [cols[:, k : k + 1] for k in range(8)]
        total_sq = jnp.zeros((BLK, LANES), f32)
        for ch in range(D // LANES):
            lanes = slice(ch * LANES, (ch + 1) * LANES)
            *_, ce, co = conv_window(sc, win, lanes, row, col[6], col[7])
            h = (
                col[0] * ce
                + col[1] * co
                + up1(col[2] * ce + col[3] * co)
                + down1(col[4] * ce + col[5] * co)
            )
            low = h[HALO : HALO + BLK].astype(bf16)
            hid_out[rows, lanes] = low
            wide = low.astype(f32)
            total_sq = total_sq + wide * wide
        scale = lax.rsqrt(jnp.sum(total_sq, axis=1, keepdims=True) * (1.0 / D) + EPS)
        for ch in range(D // LANES):
            lanes = slice(ch * LANES, (ch + 1) * LANES)
            n1_out[rows, lanes] = (hid_out[rows, lanes].astype(f32) * scale * gain[:, lanes]).astype(bf16)
        return carry

    lax.fori_loop(0, total // BLK, block, 0)


def attn_weight_copies(pieces, fs, c, parts, wqkv, wo):
    hl = wo.shape[0]
    if not pieces:
        q, k, v, o = parts
        return [(r, wqkv.at[:, pl.ds(j * hl, hl)]) for j, r in enumerate((q, k, v))] + [(o, wo)]
    q, k, v, o, mine, twin = parts
    w = D // 2
    hw = w // 2
    out = []
    for j, r in enumerate((q, k, v)):
        lanes = pl.ds(j * hl, hl)
        out.append((r, wqkv.at[pl.ds(aligned(fs, w), w), lanes]))
        base = (1 - fs) * w
        out.append((mine.at[j], wqkv.at[pl.ds(pl.multiple_of(base + c * hw, hw), hw), lanes]))
        out.append((twin.at[j], wqkv.at[pl.ds(pl.multiple_of(base + (1 - c) * hw, hw), hw), lanes]))
    other = pl.ds(aligned(1 - fs, w), w)
    out.append((o, wo.at[:, pl.ds(aligned(fs, w), w)]))
    out.append((mine.at[3], wo.at[pl.ds(aligned(c, hw), hw), other]))
    out.append((twin.at[3], wo.at[pl.ds(aligned(1 - c, hw), hw), other]))
    return out


def bias_rows(tab_ref, ext_ref, tp, shards_at):
    block = tab_ref[BIAS_ROW : BIAS_ROW + 16, :]
    ext = ext_ref[...]
    width = NB // len(shards_at)
    sub = iota((LANES, ext.shape[1]), 0)
    out = jnp.zeros((16, ext.shape[1]), f32)
    for j, lane in enumerate(shards_at):
        hot = ((sub < width) & (sub + j * width == ext)).astype(bf16)
        out = out + nn(block[:, lane : lane + LANES], hot)
    return out


def bias_plane(band, left, right, cx, plane, total):
    rolled = pltpu.roll(jnp.broadcast_to(band, (BLK, 512)), 0, 1, stride=1, stride_axis=0)
    at = iota((1, total + 2 * BLK), 1)
    plane[...] = jnp.broadcast_to(jnp.where(at < cx * BLK, left, right), plane.shape)
    plane[:, pl.ds(aligned(cx, BLK), 3 * BLK)] = rolled[:, BLK:]
    return plane[:, BLK : BLK + total]


def attn_masks(len_ref, pad_ref, fs, cx, total):
    lay = token_rows(len_ref, pad_ref, fs, total)
    seg = jnp.where(lay.real_e, lay.seg, -1).astype(f32)
    own = token_rows(len_ref, pad_ref, fs, BLK, cx * BLK)
    col = nt(eye(), put_rows([own.seg.astype(f32), own.real_e.astype(f32)], BLK), precision=HI)
    return jnp.where(col[:, 0:1] == seg, 0.0, NEG), col[:, 1:2]


def a_kernel(total, pieces, shards_at, meta, len_ref, pad_ref, ext_ref, tab_ref, n1_ref, *refs):
    n = 6 if pieces else 4
    parts = refs[:n]
    q_out, k_out, v_out, att_out, lse_out, part_out = refs[n : n + 6]
    wqkv, wo, plane, mask, fr, sems = refs[n + 6 :]
    fs, cx, tp, c = meta[0], meta[1], meta[2], meta[3]
    hl = wo.shape[0]
    made = run_copies(attn_weight_copies(pieces, fs, c, parts, wqkv, wo), sems)
    mask[...], _ = attn_masks(len_ref, pad_ref, fs, cx, total)
    fr[...] = bias_rows(tab_ref, ext_ref, tp, shards_at)
    for m in made:
        m.wait()
    own = pl.ds(aligned(cx, BLK), BLK)
    q_out[...] = nn(n1_ref[own, :], wqkv[:, 0:hl]).astype(bf16)
    step = 256

    def project(b, carry):
        rows = pl.ds(aligned(b, step), step)
        kv = nn(n1_ref[rows, :], wqkv[:, hl : 3 * hl])
        k_out[rows, :] = kv[:, 0:hl].astype(bf16)
        v_out[rows, :] = kv[:, hl : 2 * hl].astype(bf16)
        return carry

    lax.fori_loop(0, total // step, project, 0)
    lo = iota((1, LANES), 1) < DH
    lane = iota((BLK, LANES), 1)
    lse = jnp.zeros((BLK, LANES), f32)
    for pair in range(hl // LANES):
        lanes = slice(pair * LANES, (pair + 1) * LANES)
        q2, k2, v2 = q_out[:, lanes], k_out[:, lanes], v_out[:, lanes]
        halves = []
        for half in range(2):
            h = 2 * pair + half
            keep = lo if half == 0 else jnp.logical_not(lo)
            qm = jnp.where(keep, q2, jnp.zeros_like(q2)) * bf16(1.0 / math.sqrt(DH))
            band = fr[h : h + 1, :]
            bias = bias_plane(band, band[:, 0:1], band[:, 511:512], cx, plane, total)
            s = nt(qm, k2) + bias + mask[...]
            top = jnp.max(s, axis=1, keepdims=True)
            e = jnp.exp(s - top)
            tot = jnp.sum(e, axis=1, keepdims=True)
            lse = jnp.where(lane == h, top + jnp.log(tot), lse)
            halves.append(nn((e * (1.0 / tot)).astype(bf16), v2))
        att_out[:, lanes] = jnp.where(lo, halves[0], halves[1]).astype(bf16)
    lse_out[...] = lse
    part_out[...] = nn(att_out[...], wo[...]).astype(bf16)


def mlp_weight_copies(pieces, fs, c, parts, wg, wu, wd):
    if not pieces:
        return list(zip(parts, (wg, wu, wd)))
    g, u, d, gu_mine, gu_twin, d_mine, d_twin = parts
    w = D // 2
    hw = w // 2
    hr = wd.shape[0] // 2
    out = []
    for j, (r, dst) in enumerate(((g, wg), (u, wu))):
        base = (1 - fs) * w
        out.append((r, dst.at[pl.ds(aligned(fs, w), w), :]))
        out.append((gu_mine.at[j], dst.at[pl.ds(pl.multiple_of(base + c * hw, hw), hw), :]))
        out.append((gu_twin.at[j], dst.at[pl.ds(pl.multiple_of(base + (1 - c) * hw, hw), hw), :]))
    other = pl.ds(aligned(1 - fs, w), w)
    out.append((d, wd.at[:, pl.ds(aligned(fs, w), w)]))
    out.append((d_mine, wd.at[pl.ds(aligned(c, hr), hr), other]))
    out.append((d_twin, wd.at[pl.ds(aligned(1 - c, hr), hr), other]))
    return out


def tanh_parts(x):
    k = math.sqrt(2.0 / math.pi)
    th = jnp.tanh(k * (x + 0.044715 * x * x * x))
    return th, k


def b_kernel(pieces, meta, tab_ref, hid_ref, mine_ref, other_ref, *refs):
    n = 7 if pieces else 3
    parts = refs[:n]
    res_out, n2_out, gate_out, up_out, gated_out, part_out = refs[n : n + 6]
    wg, wu, wd, sems = refs[n + 6 :]
    fs, cx, c = meta[0], meta[1], meta[3]
    made = run_copies(mlp_weight_copies(pieces, fs, c, parts, wg, wu, wd), sems)
    gain = param_rows(tab_ref)(GAIN2_ROW)
    own = pl.ds(aligned(cx, BLK), BLK)
    res = hid_ref[own, :].astype(f32) + (mine_ref[...].astype(f32) + other_ref[...].astype(f32))
    res_out[...] = res
    scale = lax.rsqrt(jnp.sum(res * res, axis=1, keepdims=True) * (1.0 / D) + EPS)
    n2_out[...] = (res * scale * gain).astype(bf16)
    for m in made:
        m.wait()
    gate = nn(n2_out[...], wg[...])
    up = nn(n2_out[...], wu[...])
    gate_out[...] = gate
    up_out[...] = up
    th, _ = tanh_parts(gate)
    gated_out[...] = (0.5 * gate * (1.0 + th) * up).astype(bf16)
    part_out[...] = nn(gated_out[...], wd[...]).astype(bf16)


def c_kernel(pieces, meta, len_ref, pad_ref, deal_ref, teach_ref, res_ref, mine_ref, other_ref, gate_ref, up_ref, *refs):
    n = 7 if pieces else 3
    parts = refs[:n]
    out_ref, loss_out, gres_out, low_out, gg_out, gu_out, part_out = refs[n : n + 7]
    wg, wu, wd, teacher, sems = refs[n + 7 :]
    fs, cx, tp, c = meta[0], meta[1], meta[2], meta[3]
    made = run_copies(mlp_weight_copies(pieces, fs, c, parts, wg, wu, wd), sems)
    slots, unit = teach_ref.shape[0], teach_ref.shape[1]
    for s in range(slots):
        teacher[s * unit : (s + 1) * unit, :] = teach_ref[deal_ref[fs, cx, s]].astype(f32)
    count = jnp.int32(0)
    for f in range(len_ref.shape[0]):
        for k in range(len_ref.shape[1]):
            count = count + ((2 * len_ref[f, k] - pad_ref[f, k] + 1) >> 1)
    real_count = jnp.broadcast_to(count, (1, LANES)).astype(f32)[:, 0:1]
    own = token_rows(len_ref, pad_ref, fs, BLK, cx * BLK)
    valid = nt(eye(), put_rows([own.real_e.astype(f32)], BLK), precision=HI)[:, 0:1]
    result = res_ref[...] + (mine_ref[...].astype(f32) + other_ref[...].astype(f32))
    width = out_ref.shape[1]
    out_ref[...] = jnp.where(tp == 0, result[:, 0:width], result[:, D - width : D]).astype(bf16)
    diff = (result - teacher[...]) * valid
    square = jnp.sum(jnp.sum(diff * diff, axis=1, keepdims=True), axis=0, keepdims=True)
    loss_out[...] = jnp.broadcast_to(square / (2.0 * D * real_count), (8, LANES))
    gres = diff * (GRAD_SCALE / (D * real_count))
    gres_out[...] = gres
    low_out[...] = gres.astype(bf16)
    for m in made:
        m.wait()
    ggated = nt(low_out[...], wd[...])
    gate = gate_ref[...]
    up = up_ref[...]
    th, k = tanh_parts(gate)
    value = 0.5 * gate * (1.0 + th)
    slope = 0.5 * (1.0 + th) + 0.5 * gate * (1.0 - th * th) * (k * (1.0 + 3.0 * 0.044715 * gate * gate))
    gg_out[...] = (ggated * up * slope).astype(bf16)
    gu_out[...] = (ggated * value).astype(bf16)
    part_out[...] = (nt(gg_out[...], wg[...]) + nt(gu_out[...], wu[...])).astype(bf16)


def store_pack(wide, outs, fs, c, split):
    if not split:
        outs[0][...] = wide[...]
        return
    quarter = D // 4
    for half, ref in enumerate(outs):
        cc = c if half == 0 else 1 - c
        for rel in range(2):
            f = fs if rel == 0 else 1 - fs
            first = pl.multiple_of(f * (2 * quarter) + cc * quarter, quarter)
            ref[rel] = wide[:, pl.ds(first, quarter), :]


def m_kernel(split, meta, n2_ref, gg_ref, gu_ref, gated_ref, low_ref, *refs):
    n = 2 if split else 1
    outs, wide = refs[:n], refs[n]
    wide[0] = tn(n2_ref[...], gg_ref[...]).astype(bf16)
    wide[1] = tn(n2_ref[...], gu_ref[...]).astype(bf16)
    wide[2] = tn(low_ref[...], gated_ref[...]).astype(bf16)
    store_pack(wide, outs, meta[0], meta[3], split)


def d_kernel(total, pieces, shards_at, tps, meta, len_ref, pad_ref, ext_ref, ext1_ref, tab_ref, n1_ref, q_ref, k_ref, v_ref, att_ref, lse_ref, res_ref, gres_ref, mine_ref, other_ref, *refs):
    n = 6 if pieces else 4
    parts = refs[:n]
    m = 2 if pieces else 1
    packs = refs[n : n + m]
    gn1_out, back_out, extra_out = refs[n + m : n + m + 3]
    wqkv, wo, plane, mask, fr, dsw, stack, ga, dq, dkv, wide, sems = refs[n + m + 3 :]
    fs, cx, tp, c = meta[0], meta[1], meta[2], meta[3]
    hl = wo.shape[0]
    made = run_copies(attn_weight_copies(pieces, fs, c, parts, wqkv, wo), sems)
    mask[...], _ = attn_masks(len_ref, pad_ref, fs, cx, total)
    fr[...] = bias_rows(tab_ref, ext_ref, tp, shards_at)
    gain = param_rows(tab_ref)(GAIN2_ROW)
    gn2 = mine_ref[...].astype(f32) + other_ref[...].astype(f32)
    res = res_ref[...]
    r2 = lax.rsqrt(jnp.sum(res * res, axis=1, keepdims=True) * (1.0 / D) + EPS)
    u = gain * gn2
    gain_grad = jnp.sum(gn2 * res * r2, axis=0, keepdims=True) * (1.0 / tps)
    back = gres_ref[...] + r2 * u - res * (r2 * r2 * r2 * (jnp.sum(u * res, axis=1, keepdims=True) * (1.0 / D)))
    back_out[...] = back * (1.0 / tps)
    branch = back.astype(bf16)
    for x in made:
        x.wait()
    wide[3] = tn(branch, att_ref[...]).astype(bf16)
    ga[...] = nt(branch, wo[...]).astype(bf16)
    lo = iota((1, LANES), 1) < DH
    at = iota((1, total), 1)
    first = cx * BLK - BLK
    rev = (iota((BLK, BLK), 0) + iota((BLK, BLK), 1) == BLK - 1).astype(bf16)
    band_at = iota((1, 512), 1)
    scale = bf16(1.0 / math.sqrt(DH))
    sums = []
    for pair in range(hl // LANES):
        lanes = slice(pair * LANES, (pair + 1) * LANES)
        q2, k2, v2, g2 = q_ref[:, lanes], k_ref[:, lanes], v_ref[:, lanes], ga[:, lanes]
        zero = jnp.zeros_like(q2)
        qs, gs, dqs = [], [], []
        for half in range(2):
            h = 2 * pair + half
            keep = lo if half == 0 else jnp.logical_not(lo)
            qm = jnp.where(keep, q2, zero) * scale
            gm = jnp.where(keep, g2, zero)
            band = fr[h : h + 1, :]
            bias = bias_plane(band, band[:, 0:1], band[:, 511:512], cx, plane, total)
            s = nt(qm, k2) + bias + mask[...]
            p = jnp.exp(s - lse_ref[:, h : h + 1])
            g = nt(gm, v2)
            inner = jnp.sum(p * g, axis=1, keepdims=True)
            ds = p * (g - inner)
            low = ds.astype(bf16)
            stack[0, half * BLK : (half + 1) * BLK, :] = low
            stack[1, half * BLK : (half + 1) * BLK, :] = p.astype(bf16)
            wide_ds = low.astype(f32)
            col = jnp.sum(wide_ds, axis=0, keepdims=True)
            left = jnp.sum(jnp.where(at < first, col, 0.0), axis=1, keepdims=True)
            right = jnp.sum(jnp.where(at >= first + 3 * BLK, col, 0.0), axis=1, keepdims=True)
            dsw[:, BLK : BLK + total] = wide_ds
            if pair == 0 and half == 0:
                dsw[:, 0:BLK] = jnp.zeros((BLK, BLK), f32)
                dsw[:, BLK + total :] = jnp.zeros((BLK, 2 * BLK), f32)
            window = dsw[:, pl.ds(aligned(cx, BLK), 512)]
            window = jnp.where(band_at < 3 * BLK, window, 0.0).astype(bf16)
            turned = pltpu.roll(nn(rev, window), 0, 1, stride=1, stride_axis=0)
            diag = jnp.sum(turned, axis=0, keepdims=True)
            diag = diag + jnp.where(band_at == 0, left, 0.0) + jnp.where(band_at == 510, right, 0.0)
            sums.append(diag)
            dqs.append(nn(low, k2))
            qs.append(qm)
            gs.append(gm)
        dq[:, lanes] = (jnp.where(lo, dqs[0], dqs[1]) * (1.0 / math.sqrt(DH))).astype(bf16)
        dkv[:, lanes] = tn(stack[0], jnp.concatenate(qs, axis=0)).astype(bf16)
        dkv[:, hl + pair * LANES : hl + (pair + 1) * LANES] = tn(stack[1], jnp.concatenate(gs, axis=0)).astype(bf16)
    own = pl.ds(aligned(cx, BLK), BLK)
    wide[0] = tn(n1_ref[own, :], dq[...]).astype(bf16)
    both = tn(n1_ref[...], dkv[...])
    wide[1] = both[:, 0:hl].astype(bf16)
    wide[2] = both[:, hl : 2 * hl].astype(bf16)
    store_pack(wide, packs, fs, c, pieces)
    step = 256

    def back_rows(b, carry):
        rows = pl.ds(aligned(b, step), step)
        gn1_out[rows, :] = nt(dkv[rows, :], wqkv[:, hl : 3 * hl])
        return carry

    lax.fori_loop(0, total // step, back_rows, 0)
    gn1_out[own, :] = gn1_out[own, :] + nt(dq[...], wqkv[:, 0:hl])
    rows = put_rows(sums, 512)
    ext = ext1_ref[...]
    width = NB // len(shards_at)
    sub = iota((LANES, 512), 0)
    extra_out[...] = jnp.zeros(extra_out.shape, f32)
    grads = []
    for j, lane in enumerate(shards_at):
        hot = ((sub < width) & (sub + j * width == ext)).astype(f32)
        extra_out[pl.ds(aligned(tp, 8), 8), lane : lane + LANES] = nt(rows, hot, precision=HI)
    extra_out[16:24, :] = jnp.broadcast_to(gain_grad, (8, D))


def e_kernel(total, split, meta, len_ref, pad_ref, ids_ref, tab_ref, hid_ref, gn1_ref, back_ref, extra_ref, *refs):
    n = 2 if split else 1
    outs = refs[:n]
    sc = front_refs(refs[n : n + 7])
    dh, de, acc, xr, small = refs[n + 7 :]
    fs, cx, c = meta[0], meta[1], meta[3]
    sc.tab[...] = tab_ref[...]
    lay, we, wo, row = front(sc, len_ref, pad_ref, fs, ids_ref, total)
    gain = row(GAIN1_ROW)
    zero = jnp.zeros((HALO, D), f32)
    dh[0:HALO, :] = zero
    dh[total + HALO : total + 2 * HALO, :] = zero

    def norm_back(b, carry):
        rows = pl.ds(aligned(b, BLK), BLK)
        h = hid_ref[rows, :].astype(f32)
        g = gn1_ref[rows, :]
        r = lax.rsqrt(jnp.sum(h * h, axis=1, keepdims=True) * (1.0 / D) + EPS)
        u = gain * g
        d = r * u - h * (r * r * r * (jnp.sum(u * h, axis=1, keepdims=True) * (1.0 / D)))
        mine = jnp.where(b == cx, jnp.float32(1.0), jnp.float32(0.0))
        dh[pl.ds(pl.multiple_of(b * BLK + HALO, HALO), BLK), :] = d + mine * back_ref[...]
        return carry + jnp.sum(g * h * r, axis=0, keepdims=True)

    gain_grad = lax.fori_loop(0, total // BLK, norm_back, jnp.zeros((1, D), f32))
    ones = jnp.ones((8, LANES), f32)

    def inner(b, carry):
        win = pl.ds(aligned(b, BLK), WIN)
        pv, nx = sc.cols[win, 6:7], sc.cols[win, 7:8]
        for ch in range(D // LANES):
            lanes = slice(ch * LANES, (ch + 1) * LANES)
            *_, ce, co = conv_window(sc, win, lanes, row, pv, nx)
            d = dh[win, lanes]
            mid = slice(HALO, HALO + BLK)
            terms = (d * up1(ce), d * up1(co), d * ce, d * co, d * down1(ce), d * down1(co))
            for k, x in enumerate(terms):
                acc[k] = x[mid] if ch == 0 else acc[k] + x[mid]
        cols = pl.ds(aligned(b, BLK), BLK)
        for k in range(6):
            xr[k, :, cols] = nt(ones, acc[k], precision=HI)
        return carry

    lax.fori_loop(0, total // BLK, inner, 0)
    x = [0.5 * xr[k, 0:1, :] for k in range(6)]
    pe, po = forms(x, lay)

    def soft_back(w, p):
        mean = w[0] * p[0] + w[1] * p[1] + w[2] * p[2] + w[3] * p[3]
        return [a * (b - mean) for a, b in zip(w, p)]

    dse, dso = soft_back(we, pe), soft_back(wo, po)
    em, om, e0, o0, ep, op = spread(dse, dso, lay)
    dze = e0 + after(em) + before(ep)
    dzo = o0 + after(om) + before(op)
    sc.ge[...] = put_rows([dze, dzo], total)
    unit = eye()

    def turn(b, carry):
        rows = pl.ds(pl.multiple_of(b * BLK + HALO, HALO), BLK)
        sc.cols[rows, 8:16] = nt(unit, sc.ge[:, pl.ds(aligned(b, BLK), BLK)], precision=HI)
        return carry

    lax.fori_loop(0, total // BLK, turn, 0)
    score = row(SCORE_ROW)
    small[...] = jnp.zeros(small.shape, f32)

    def stencil(b, carry):
        win = pl.ds(aligned(b, BLK), WIN)
        rows = pl.ds(aligned(b, BLK), BLK)
        cols = sc.cols[win, :]
        col = [cols[:, k : k + 1] for k in range(10)]
        mid = slice(HALO, HALO + BLK)
        for ch in range(D // LANES):
            lanes = slice(ch * LANES, (ch + 1) * LANES)
            ee, eo, eo_p, ee_n, eo_n, tap, ce, co = conv_window(sc, win, lanes, row, col[6], col[7])
            d = dh[win, lanes]
            dn, du = down1(d), up1(d)
            sw = score[:, lanes]
            dce = col[0] * d + col[2] * dn + col[4] * du + col[8] * sw
            dco = col[1] * d + col[3] * dn + col[5] * du + col[9] * sw
            dee = tap[0] * dco + tap[1] * dce + up1(col[7] * (tap[3] * dce + tap[2] * dco))
            deo = tap[1] * dco + tap[2] * dce + down1(col[6] * tap[0] * dce) + up1(col[7] * tap[3] * dco)
            de[0, rows, lanes] = dee[mid].astype(bf16)
            de[1, rows, lanes] = deo[mid].astype(bf16)
            dce, dco = dce[mid], dco[mid]
            ee, eo, eo_p, ee_n, eo_n = (a[mid] for a in (ee, eo, eo_p, ee_n, eo_n))
            sums = (
                dce * eo_p + dco * ee,
                dce * ee + dco * eo,
                dce * eo + dco * ee_n,
                dce * ee_n + dco * eo_n,
                dce + dco,
                (col[8] * ce + col[9] * co)[mid],
            )
            for k, s in enumerate(sums):
                small[k : k + 1, lanes] += jnp.sum(s, axis=0, keepdims=True)
        return carry

    lax.fori_loop(0, total // BLK, stencil, 0)
    lay2 = token_rows(len_ref, pad_ref, fs, total)
    sub = iota((VP, total), 0)
    grad = jnp.zeros((VP, D), f32)
    for k, real in ((0, lay2.real_e), (1, lay2.real_o)):
        hot = (sub == jnp.where(real, ids_ref[k : k + 1, :], -1)).astype(bf16)
        grad = grad + nn(hot, de[k])
    wide = sc.ee
    wide[0:VP, :] = grad
    for k in range(6):
        wide[TAP_ROW + k : TAP_ROW + k + 1, :] = small[k : k + 1, :]
    wide[GAIN1_ROW : GAIN1_ROW + 1, :] = gain_grad
    wide[GAIN2_ROW : GAIN2_ROW + 1, :] = extra_ref[16:17, :]
    wide[BIAS_ROW : BIAS_ROW + 16, :] = extra_ref[0:16, :]
    if not split:
        outs[0][...] = wide[0:SROWS, :].astype(bf16)
        return
    w = D // 2
    hr = SROWS // 2
    for half, ref in enumerate(outs):
        cc = c if half == 0 else 1 - c
        for rel in range(2):
            f = fs if rel == 0 else 1 - fs
            ref[rel] = wide[pl.ds(pl.multiple_of(cc * hr, 8), hr), pl.ds(aligned(f, w), w)].astype(bf16)


def sds(shape, dtype):
    return jax.ShapeDtypeStruct(shape, dtype)


def call(kernel, name, ins, in_specs, out_shape, scratch):
    return pl.pallas_call(
        kernel,
        name=name,
        out_shape=out_shape,
        in_specs=in_specs,
        out_specs=jax.tree.map(lambda _: VM, out_shape),
        scratch_shapes=scratch,
        compiler_params=pltpu.CompilerParams(vmem_limit_bytes=60 << 20),
    )(*ins)


def add2(a, b):
    return (a.astype(f32) + b.astype(f32)).astype(bf16)


def shards(
    byte_ids,
    seq_tokens,
    pad_bytes,
    deal_targets,
    rel_buckets,
    embedding,
    conv_weight,
    conv_bias,
    score_weight,
    attn_gain,
    query_weight,
    key_weight,
    value_weight,
    rel_bias,
    out_weight,
    mlp_gain,
    gate_weight,
    up_weight,
    down_weight,
    teacher,
):
    fs = lax.axis_index("fsdp")
    cx = lax.axis_index("ctx")
    tp = lax.axis_index("tp")
    fcount, ccount, tps = lax.axis_size("fsdp"), lax.axis_size("ctx"), lax.axis_size("tp")
    core = cx % 2
    total = teacher.shape[0] * ccount
    unit = teacher.shape[0] // ccount
    hl = query_weight.shape[1]
    heads = hl // DH
    ffl = gate_weight.shape[1]
    split = fcount == 2
    wloc = D // fcount
    bloc = NB // fcount
    meta = jnp.stack([fs, cx, tp, core]).astype(i32)

    def twin(x):
        return lax.ppermute(x, "ctx", [(i, i ^ 1) for i in range(ccount)])

    def across(x):
        return lax.ppermute(x, "fsdp", [(0, 1), (1, 0)])

    def tp_other(x):
        return lax.ppermute(x, "tp", [(i, tps - 1 - i) for i in range(tps)])

    def core_half(x, axis):
        n = x.shape[axis] // 2
        return lax.dynamic_slice_in_dim(x, core * n, n, axis)

    ids = lax.all_gather(byte_ids.reshape(-1, 2).T, "ctx", axis=1, tiled=True)
    teach = lax.all_to_all(teacher.reshape(ccount, unit, D), "ctx", split_axis=0, concat_axis=0, tiled=True)
    ends = lambda k: jnp.broadcast_to(rel_buckets[k : k + 1], (RMAX,))
    ext = jnp.concatenate([ends(0), rel_buckets, ends(2 * RMAX)])
    ext, ext1 = ext[None, :512], ext[None, 1:513]

    bias_t = jnp.pad(rel_bias.T, ((0, 16 - heads), (0, wloc - bloc)))
    small = jnp.concatenate(
        [
            embedding,
            conv_weight,
            conv_bias[None],
            score_weight[None],
            attn_gain[None],
            mlp_gain[None],
            jnp.zeros((BIAS_ROW - GAIN2_ROW - 1, wloc), bf16),
            bias_t,
        ],
        axis=0,
    )
    if split:
        small_parts = (small, across(small))
        attn = jnp.stack([query_weight, key_weight, value_weight, out_weight])
        mine = across(core_half(attn, 1))
        gu_mine = across(core_half(jnp.stack([gate_weight, up_weight]), 1))
        d_mine = across(core_half(down_weight, 0))
        attn_parts = (query_weight, key_weight, value_weight, out_weight, mine, twin(mine))
        mlp_parts = (gate_weight, up_weight, down_weight, gu_mine, twin(gu_mine), d_mine, twin(d_mine))
    else:
        gather = lambda x, axis: lax.all_gather(x, "fsdp", axis=axis, tiled=True)
        full = gather(small, 1)
        bias_all = jnp.pad(gather(rel_bias, 0).T, ((0, 16 - heads), (0, D - NB)))
        small_parts = (jnp.concatenate([full[:BIAS_ROW], bias_all], axis=0),)
        attn_parts = (gather(query_weight, 0), gather(key_weight, 0), gather(value_weight, 0), gather(out_weight, 1))
        mlp_parts = (gather(gate_weight, 0), gather(up_weight, 0), gather(down_weight, 1))
    shards_at = (0, wloc) if split else (0,)

    tab, hid, n1 = call(
        functools.partial(g_kernel, total, split),
        "g",
        (meta, seq_tokens, pad_bytes, ids) + small_parts,
        [SM, SM, SM, VM] + [ANY] * len(small_parts),
        (sds((VP, D), bf16), sds((total, D), bf16), sds((total, D), bf16)),
        front_scratch(total) + [pltpu.SemaphoreType.DMA((2,))],
    )
    na = len(attn_parts)
    attn_scratch = [
        pltpu.VMEM((D, 3 * hl), bf16),
        pltpu.VMEM((hl, D), bf16),
        pltpu.VMEM((BLK, total + 2 * BLK), f32),
        pltpu.VMEM((BLK, total), f32),
        pltpu.VMEM((16, 512), f32),
    ]
    q, k, v, att, lse, part = call(
        functools.partial(a_kernel, total, split, shards_at),
        "a",
        (meta, seq_tokens, pad_bytes, ext, tab, n1) + attn_parts,
        [SM, SM, SM, VM, VM, VM] + [ANY] * na,
        (
            sds((BLK, hl), bf16),
            sds((total, hl), bf16),
            sds((total, hl), bf16),
            sds((BLK, hl), bf16),
            sds((BLK, LANES), f32),
            sds((BLK, D), bf16),
        ),
        attn_scratch + [pltpu.SemaphoreType.DMA((12,))],
    )
    nm = len(mlp_parts)
    mlp_scratch = [pltpu.VMEM((D, ffl), bf16), pltpu.VMEM((D, ffl), bf16), pltpu.VMEM((ffl, D), bf16)]
    res, n2, gate, up, gated, part2 = call(
        functools.partial(b_kernel, split),
        "b",
        (meta, tab, hid, part, tp_other(part)) + mlp_parts,
        [SM, VM, VM, VM, VM] + [ANY] * nm,
        (
            sds((BLK, D), f32),
            sds((BLK, D), bf16),
            sds((BLK, ffl), f32),
            sds((BLK, ffl), f32),
            sds((BLK, ffl), bf16),
            sds((BLK, D), bf16),
        ),
        mlp_scratch + [pltpu.SemaphoreType.DMA((9,))],
    )
    output, loss, gres, low, gg, gu, part3 = call(
        functools.partial(c_kernel, split),
        "c",
        (meta, seq_tokens, pad_bytes, deal_targets, teach, res, part2, tp_other(part2), gate, up) + mlp_parts,
        [SM, SM, SM, SM, VM, VM, VM, VM, VM, VM] + [ANY] * nm,
        (
            sds((BLK, D // tps), bf16),
            sds((8, LANES), f32),
            sds((BLK, D), f32),
            sds((BLK, D), bf16),
            sds((BLK, ffl), bf16),
            sds((BLK, ffl), bf16),
            sds((BLK, D), bf16),
        ),
        mlp_scratch + [pltpu.VMEM((BLK, D), f32), pltpu.SemaphoreType.DMA((9,))],
    )
    part3_other = tp_other(part3)
    quarter = D // 4

    def pack_shape(k, n):
        return (sds((2, k, quarter, n), bf16),) * 2 if split else (sds((k, D, n), bf16),)

    mlp_pack = call(
        functools.partial(m_kernel, split),
        "m",
        (meta, n2, gg, gu, gated, low),
        [SM] + [VM] * 5,
        pack_shape(3, ffl),
        [pltpu.VMEM((3, D, ffl), bf16)],
    )
    *attn_pack, gn1, back, extra = call(
        functools.partial(d_kernel, total, split, shards_at, tps),
        "d",
        (meta, seq_tokens, pad_bytes, ext, ext1, tab, n1, q, k, v, att, lse, res, gres, part3, part3_other) + attn_parts,
        [SM, SM, SM] + [VM] * 13 + [ANY] * na,
        pack_shape(4, hl) + (sds((total, D), f32), sds((BLK, D), f32), sds((24, D), f32)),
        attn_scratch
        + [
            pltpu.VMEM((BLK, total + 3 * BLK), f32),
            pltpu.VMEM((2, 2 * BLK, total), bf16),
            pltpu.VMEM((BLK, hl), bf16),
            pltpu.VMEM((BLK, hl), bf16),
            pltpu.VMEM((total, 2 * hl), bf16),
            pltpu.VMEM((4, D, hl), bf16),
            pltpu.SemaphoreType.DMA((12,)),
        ],
    )
    small_shape = (sds((2, SROWS // 2, wloc), bf16),) * 2 if split else (sds((SROWS, D), bf16),)
    small_pack = call(
        functools.partial(e_kernel, total, split),
        "e",
        (meta, seq_tokens, pad_bytes, ids, tab, hid, gn1, back, extra),
        [SM, SM, SM] + [VM] * 6,
        small_shape,
        front_scratch(total)
        + [
            pltpu.VMEM((total + 2 * HALO, D), f32),
            pltpu.VMEM((2, total, D), bf16),
            pltpu.VMEM((6, BLK, LANES), f32),
            pltpu.VMEM((6, 8, total), f32),
            pltpu.VMEM((8, D), f32),
        ],
    )

    def ctx_perm(x, bit):
        return lax.ppermute(x, "ctx", [(i, i ^ bit) for i in range(ccount)])

    def reduce_pack(pack, over_tp=False):
        if not split:
            (x,) = pack
            x = lax.psum_scatter(x, "fsdp", scatter_dimension=x.ndim - 2 if not over_tp else 1, tiled=True)
            return lax.psum(x, ("ctx", "tp") if over_tp else "ctx").astype(f32)
        keep, send = pack
        s = add2(keep, twin(send))
        t = add2(s[0], across(s[1]))
        if over_tp:
            t = add2(t, tp_other(t))
        bit = 2
        while bit < ccount:
            t = add2(t, ctx_perm(t, bit))
            bit = 2 * bit
        o = twin(t)
        axis = t.ndim - 2
        return jnp.where(
            core == 0, jnp.concatenate([t, o], axis=axis), jnp.concatenate([o, t], axis=axis)
        ).astype(f32)

    mlp_sum = reduce_pack(mlp_pack)
    attn_sum = reduce_pack(attn_pack)
    small_sum = reduce_pack(small_pack, over_tp=True)
    loss_all = loss
    if split:
        loss_all = loss_all + across(loss_all)
        bit = 1
        while bit < ccount:
            loss_all = loss_all + ctx_perm(loss_all, bit)
            bit = 2 * bit
    else:
        loss_all = lax.psum(loss_all, ("fsdp", "ctx"))
    if split:
        bias_rows_out = lax.dynamic_slice_in_dim(small_sum, BIAS_ROW + 8 * tp, 8, 0)[:heads, :bloc]
        bias_grad = bias_rows_out.T
    else:
        (x,) = small_pack
        x = lax.dynamic_slice_in_dim(x, BIAS_ROW + 8 * tp, 8, 0)[:heads, :NB].T
        x = lax.psum(x, ("fsdp", "ctx")).astype(f32)
        bias_grad = lax.dynamic_slice_in_dim(x, fs * bloc, bloc, 0)
    return (
        output,
        small_sum[:VOCAB],
        small_sum[TAP_ROW : TAP_ROW + CONV],
        small_sum[SHIFT_ROW],
        small_sum[SCORE_ROW],
        small_sum[GAIN1_ROW],
        attn_sum[0],
        attn_sum[1],
        attn_sum[2],
        bias_grad,
        attn_sum[3].T,
        small_sum[GAIN2_ROW],
        mlp_sum[0],
        mlp_sum[1],
        mlp_sum[2].T,
        loss_all[0, 0],
    )


def solution(mesh):
    both = ("fsdp", "ctx")
    in_specs = (
        P(both),
        P(),
        P(),
        P(),
        P(),
        P(None, "fsdp"),
        P(None, "fsdp"),
        P("fsdp"),
        P("fsdp"),
        P("fsdp"),
        P("fsdp", "tp"),
        P("fsdp", "tp"),
        P("fsdp", "tp"),
        P("fsdp", "tp"),
        P("tp", "fsdp"),
        P("fsdp"),
        P("fsdp", "tp"),
        P("fsdp", "tp"),
        P("tp", "fsdp"),
        P(both, None),
    )
    out_specs = (
        P(both, "tp"),
        P(None, "fsdp"),
        P(None, "fsdp"),
        P("fsdp"),
        P("fsdp"),
        P("fsdp"),
        P("fsdp", "tp"),
        P("fsdp", "tp"),
        P("fsdp", "tp"),
        P("fsdp", "tp"),
        P("tp", "fsdp"),
        P("fsdp"),
        P("fsdp", "tp"),
        P("fsdp", "tp"),
        P("tp", "fsdp"),
        P(),
    )
    return jax.shard_map(shards, mesh=mesh, in_specs=in_specs, out_specs=out_specs, check_vma=False)
```

```python
import functools
import math

import jax
import jax.numpy as jnp
from jax import lax
from jax.experimental import pallas as pl
from jax.experimental.pallas import tpu as pltpu
from jax.sharding import PartitionSpec as P

D = 768
DH = 64
VOCAB = 259
NB = 32
RMAX = 128
CONV = 4

EPS = 1e-06
NEG = -1e30
GRAD_SCALE = 65536.0
LANES = 128
BLK = 128
HALO = 8
WIN = BLK + 2 * HALO
VP = 384
SROWS = 288
TAP_ROW = VOCAB
SHIFT_ROW = VOCAB + 4
SCORE_ROW = VOCAB + 5
GAIN1_ROW = VOCAB + 6
GAIN2_ROW = VOCAB + 7
BIAS_ROW = 272
LOSS_ROW = 267
f32 = jnp.float32
bf16 = jnp.bfloat16
i32 = jnp.int32
HI = lax.Precision.HIGHEST
ANY = pl.BlockSpec(memory_space=pl.ANY)
VM = pl.BlockSpec(memory_space=pltpu.VMEM)
SM = pl.BlockSpec(memory_space=pltpu.SMEM)


def nn(a, b, **k):
    return lax.dot_general(a, b, (((1,), (0,)), ((), ())), preferred_element_type=f32, **k)


def nt(a, b, **k):
    return lax.dot_general(a, b, (((1,), (1,)), ((), ())), preferred_element_type=f32, **k)


def tn(a, b, **k):
    return lax.dot_general(a, b, (((0,), (0,)), ((), ())), preferred_element_type=f32, **k)


def iota(shape, axis):
    return lax.broadcasted_iota(i32, shape, axis)


def aligned(index, step):
    return pl.multiple_of(index * step, step)


class Layout:
    pass


def token_rows(len_ref, pad_ref, fs, total, first=0, whole=1 << 30):
    t = iota((1, total), 1) + first
    live = (t >= 0) & (t < whole)
    start = jnp.zeros_like(t)
    end = jnp.zeros_like(t)
    limit = jnp.zeros_like(t)
    seg = jnp.zeros_like(t)
    base = jnp.int32(0)
    for k in range(len_ref.shape[1]):
        n = len_ref[fs, k]
        inside = t >= base
        start = jnp.where(inside, base, start)
        end = jnp.where(inside, base + n, end)
        limit = jnp.where(inside, 2 * n - pad_ref[fs, k], limit)
        seg = jnp.where(inside, k, seg)
        base = base + n
    lay = Layout()
    rel = t - start
    lay.seg = seg
    lay.real_e = live & (2 * rel < limit)
    lay.real_o = live & (2 * rel + 1 < limit)
    lay.prev = (live & (rel > 0)).astype(f32)
    lay.v = (live & (t + 1 < end)).astype(f32)
    third = (rel * 43691) >> 17
    u = rel - 3 * third
    lay.u0 = (u == 0).astype(f32)
    lay.u1 = (u == 1).astype(f32)
    lay.u2 = (u == 2).astype(f32)
    lay.odd = (rel & 1).astype(f32)
    lay.even = 1.0 - lay.odd
    third_f = jnp.float32(1.0 / 3.0)
    last0 = jnp.where(t + 1 < end, third_f, 0.5)
    lay.inv_e3 = jnp.where(u == 0, last0, third_f)
    lay.inv_o3 = jnp.where(u == 0, last0, jnp.where(u == 1, jnp.where(t + 1 < end, third_f, 1.0), third_f))
    lay.inv4 = jnp.where((rel & 1) == 1, 0.25, jnp.where(t + 1 < end, 0.25, 0.5))
    return lay


def forms(x, lay):
    em, om, e0, o0, ep, op = x
    pair = e0 + o0
    after = lay.v * (ep + op)
    first = pair + lay.v * ep
    closing = om + pair
    p2 = 0.5 * pair
    e3 = (lay.u0 * first + lay.u1 * (em + om + e0) + lay.u2 * closing) * lay.inv_e3
    o3 = (lay.u0 * first + lay.u1 * (o0 + after) + lay.u2 * closing) * lay.inv_o3
    p4 = (pair + lay.odd * (em + om) + lay.even * after) * lay.inv4
    return (e0, p2, e3, p4), (o0, p2, o3, p4)


def spread(we, wo, lay):
    e1, e2, e3, e4 = we
    o1, o2, o3, o4 = wo
    e3 = e3 * lay.inv_e3
    o3 = o3 * lay.inv_o3
    both = e3 + o3
    p4 = (e4 + o4) * lay.inv4
    p2 = (e2 + o2) * 0.5
    edge = lay.u0 * both + lay.u2 * both
    em = lay.u1 * e3 + lay.odd * p4
    om = em + lay.u2 * both
    e0 = e1 + p2 + edge + lay.u1 * e3 + p4
    o0 = o1 + p2 + edge + lay.u1 * o3 + p4
    op = lay.v * (lay.u1 * o3 + lay.even * p4)
    ep = op + lay.v * lay.u0 * both
    return em, om, e0, o0, ep, op


def before(row):
    return pltpu.roll(row, 1, 1)


def after(row):
    return pltpu.roll(row, row.shape[1] - 1, 1)


def softmax4(s):
    top = jnp.maximum(jnp.maximum(s[0], s[1]), jnp.maximum(s[2], s[3]))
    e = [jnp.exp(x - top) for x in s]
    inv = 1.0 / (e[0] + e[1] + e[2] + e[3])
    return [x * inv for x in e]


def put_rows(rows, total):
    sub = iota((8, total), 0)
    out = jnp.zeros((8, total), f32)
    for k, r in enumerate(rows):
        out = jnp.where(sub == k, jnp.broadcast_to(r, (8, total)), out)
    return out


def get_row(block, k):
    return jnp.sum(jnp.where(iota(block.shape, 0) == k, block, 0.0), axis=0, keepdims=True)


def eye():
    return (iota((BLK, BLK), 0) == iota((BLK, BLK), 1)).astype(f32)


def neighbours(e, o):
    return before(e), before(o), e, o, after(e), after(o)


def param_rows(tab_ref):
    rows = tab_ref[VOCAB - 3 : VOCAB + 13, :].astype(f32)
    return lambda k: rows[k - VOCAB + 3 : k - VOCAB + 4, :]


def id_rows(ids_ref):
    count = ids_ref.shape[0]
    return [jnp.concatenate([ids_ref[d, k : k + 1, :] for d in range(count)], axis=1) for k in range(2)]


def up1(x):
    return pltpu.roll(x, 1, 0)


def down1(x):
    return pltpu.roll(x, WIN - 1, 0)


def conv_window(ee, eo, lanes, row, pv, nx):
    eo_p = up1(eo) * pv
    ee_n = down1(ee) * nx
    eo_n = down1(eo) * nx
    c = [row(TAP_ROW + k)[:, lanes] for k in range(CONV)]
    b = row(SHIFT_ROW)[:, lanes]
    ce = b + c[0] * eo_p + c[1] * ee + c[2] * eo + c[3] * ee_n
    co = b + c[0] * ee + c[1] * eo + c[2] * ee_n + c[3] * eo_n
    return ce, co


def run_copies(copies, sems):
    made = [pltpu.make_async_copy(s, d, sems.at[k]) for k, (s, d) in enumerate(copies)]
    for c in made:
        c.start()
    return made


def split3(x):
    top = x.astype(bf16)
    rest = x - top.astype(f32)
    middle = rest.astype(bf16)
    return top, middle, (rest - middle.astype(f32)).astype(bf16)


def g_kernel(total, pieces, meta, len_ref, pad_ref, ids_ref, *refs):
    n = 2 if pieces else 1
    parts = refs[:n]
    tab_out, hid_out, n1_out, conv_out, rows_out = refs[n : n + 5]
    tab, hot2, ee, eo, idr, ge, go, coef, sems = refs[n + 5 :]
    fs, c = meta[0], meta[3]
    if pieces:
        w = D // 2
        copies = [
            (parts[0], tab.at[pl.ds(0, SROWS), pl.ds(aligned(fs, w), w)]),
            (parts[1], tab.at[pl.ds(0, SROWS), pl.ds(aligned(1 - fs, w), w)]),
        ]
    else:
        copies = [(parts[0], tab.at[pl.ds(0, SROWS), :])]
    made = run_copies(copies, sems)
    tab[SROWS:VP, :] = jnp.zeros((VP - SROWS, D), bf16)
    lay = token_rows(len_ref, pad_ref, fs, total, c * BLK - HALO, total)
    shifted = [jnp.where(c == 0, pltpu.roll(r, HALO, 1), pltpu.roll(r, total - BLK + HALO, 1)) for r in id_rows(ids_ref)]
    id_e = jnp.where(lay.real_e, shifted[0], -1)
    id_o = jnp.where(lay.real_o, shifted[1], -1)
    idr[...] = put_rows([id_e.astype(f32), id_o.astype(f32)], total)
    for m in made:
        m.wait()
    tab_out[...] = tab[...]
    row = param_rows(tab)
    score = row(SCORE_ROW)
    sub = iota((16, D), 0)
    cw = jnp.zeros((16, D), f32)
    for k in range(CONV):
        cw = jnp.where(sub == k, jnp.broadcast_to(row(TAP_ROW + k) * score, (16, D)), cw)
    top, middle, _ = split3(cw)
    g = jnp.concatenate(split3(nt(top, tab[...]) + nt(middle, tab[...])), axis=0)
    shift_score = jnp.sum(row(SHIFT_ROW) * score, axis=1, keepdims=True)
    step = 2 * BLK
    at = iota((VP, step), 0).astype(f32)

    def dots(i, carry):
        lanes = pl.ds(aligned(i, step), step)
        for k, out in ((0, ge), (1, go)):
            x = nn(g, (at == idr[k : k + 1, lanes]).astype(bf16))
            out[:, lanes] = x[0:8] + x[16:24] + x[32:40]
        return carry

    lax.fori_loop(0, total // step, dots, 0)
    qe = [get_row(ge[...], k) for k in range(4)]
    qo = [get_row(go[...], k) for k in range(4)]
    ze = lay.prev * before(qo[0]) + qe[1] + qo[2] + lay.v * after(qe[3]) + shift_score
    zo = qe[0] + qo[1] + lay.v * after(qe[2]) + lay.v * after(qo[3]) + shift_score
    se, so = forms(neighbours(ze, zo), lay)
    we, wo = softmax4(se), softmax4(so)
    em, om, e0, o0, ep, op = [0.5 * x for x in spread(we, wo, lay)]
    coef[...] = put_rows([e0, o0, after(em), after(om), before(ep), before(op), lay.prev, lay.v], total)
    rows_out[0:8, :] = put_rows(list(we) + list(wo), total)
    rows_out[8:16, :] = put_rows([e0, o0, em, om, ep, op], total)
    gain = row(GAIN1_ROW)
    lane = iota((WIN, VP), 1).astype(f32)

    def window(i, carry):
        lanes_at = pl.ds(aligned(i, step), step)
        ids = idr[:, lanes_at].T
        cols = coef[:, lanes_at].T
        hot2[0:WIN, :] = (lane == ids[0:WIN, 0:1]).astype(bf16)
        hot2[WIN : 2 * WIN, :] = (lane == ids[0:WIN, 1:2]).astype(bf16)
        both = nn(hot2[...], tab[...])
        ee[...] = both[0:WIN]
        eo[...] = both[WIN : 2 * WIN]
        col = [jnp.broadcast_to(cols[0:WIN, k : k + 1], (WIN, LANES)) for k in range(8)]
        total_sq = jnp.zeros((WIN, LANES), f32)
        for ch in range(D // LANES):
            lanes = slice(ch * LANES, (ch + 1) * LANES)
            ce, co = conv_window(ee[:, lanes], eo[:, lanes], lanes, row, col[6], col[7])
            conv_out[0, i, :, lanes] = ce.astype(bf16)
            conv_out[1, i, :, lanes] = co.astype(bf16)
            h = col[0] * ce + col[1] * co + up1(col[2] * ce + col[3] * co) + down1(col[4] * ce + col[5] * co)
            low = h.astype(bf16)
            ee[:, lanes] = low.astype(f32)
            total_sq = total_sq + ee[:, lanes] * ee[:, lanes]
        scale = lax.rsqrt(jnp.sum(total_sq, axis=1, keepdims=True) * (1.0 / D) + EPS)
        scale = jnp.broadcast_to(scale, (WIN, LANES))[HALO : HALO + BLK]
        for ch in range(D // LANES):
            lanes = slice(ch * LANES, (ch + 1) * LANES)
            h = ee[HALO : HALO + BLK, lanes]
            hid_out[i, :, lanes] = h.astype(bf16)
            n1_out[i, :, lanes] = (h * scale * gain[:, lanes]).astype(bf16)
        return carry

    lax.fori_loop(0, total // step, window, 0)


def attn_weight_copies(pieces, fs, c, parts, wqkv, wo):
    hl = wo.shape[0]
    if not pieces:
        q, k, v, o = parts
        return [(r, wqkv.at[:, pl.ds(j * hl, hl)]) for j, r in enumerate((q, k, v))] + [(o, wo)]
    q, k, v, o, mine, twin = parts
    w = D // 2
    hw = w // 2
    out = []
    for j, r in enumerate((q, k, v)):
        lanes = pl.ds(j * hl, hl)
        out.append((r, wqkv.at[pl.ds(aligned(fs, w), w), lanes]))
        base = (1 - fs) * w
        out.append((mine.at[j], wqkv.at[pl.ds(pl.multiple_of(base + c * hw, hw), hw), lanes]))
        out.append((twin.at[j], wqkv.at[pl.ds(pl.multiple_of(base + (1 - c) * hw, hw), hw), lanes]))
    other = pl.ds(aligned(1 - fs, w), w)
    out.append((o, wo.at[:, pl.ds(aligned(fs, w), w)]))
    out.append((mine.at[3], wo.at[pl.ds(aligned(c, hw), hw), other]))
    out.append((twin.at[3], wo.at[pl.ds(aligned(1 - c, hw), hw), other]))
    return out


def bias_rows(tab_ref, ext_ref, tp, shards_at):
    block = tab_ref[BIAS_ROW : BIAS_ROW + 16, :]
    ext = ext_ref[...]
    width = NB // len(shards_at)
    sub = iota((LANES, ext.shape[1]), 0)
    out = jnp.zeros((16, ext.shape[1]), f32)
    for j, lane in enumerate(shards_at):
        hot = ((sub < width) & (sub + j * width == ext)).astype(bf16)
        out = out + nn(block[:, lane : lane + LANES], hot)
    return out


def bias_plane(band, left, right, cx, plane, total):
    rolled = pltpu.roll(jnp.broadcast_to(band, (BLK, 512)), 0, 1, stride=1, stride_axis=0)
    at = iota((1, total + 2 * BLK), 1)
    plane[...] = jnp.broadcast_to(jnp.where(at < cx * BLK, left, right), plane.shape)
    plane[:, pl.ds(aligned(cx, BLK), 3 * BLK)] = rolled[:, BLK:]
    return plane[:, BLK : BLK + total]


def attn_masks(len_ref, pad_ref, fs, cx, total):
    lay = token_rows(len_ref, pad_ref, fs, total)
    seg = jnp.where(lay.real_e, lay.seg, -1).astype(f32)
    own = token_rows(len_ref, pad_ref, fs, BLK, cx * BLK)
    col = nt(eye(), put_rows([own.seg.astype(f32), own.real_e.astype(f32)], BLK), precision=HI)
    return jnp.where(col[:, 0:1] == seg, 0.0, NEG), col[:, 1:2]


def a_kernel(total, pieces, shards_at, meta, len_ref, pad_ref, ext_ref, tab_ref, n1_mine, n1_twin, *refs):
    n = 6 if pieces else 4
    parts = refs[:n]
    q_out, k_out, v_out, att_out, lse_out, part_out, n1_out = refs[n : n + 7]
    wqkv, wo, plane, mask, fr, sems = refs[n + 7 :]
    fs, cx, tp, c = meta[0], meta[1], meta[2], meta[3]
    hl = wo.shape[0]
    made = run_copies(attn_weight_copies(pieces, fs, c, parts, wqkv, wo), sems)
    mask[...], _ = attn_masks(len_ref, pad_ref, fs, cx, total)
    fr[...] = bias_rows(tab_ref, ext_ref, tp, shards_at)
    for m in made:
        m.wait()
    q_out[...] = nn(n1_mine[cx >> 1], wqkv[:, 0:hl]).astype(bf16)

    def project(i, carry):
        x = jnp.concatenate([n1_mine[i], n1_twin[i]], axis=0)
        kv = nn(x, wqkv[:, hl : 3 * hl]).astype(bf16)
        for k in range(2):
            rows = pl.ds(aligned(2 * i + (c if k == 0 else 1 - c), BLK), BLK)
            mid = slice(k * BLK, (k + 1) * BLK)
            n1_out[rows, :] = x[mid]
            k_out[rows, :] = kv[mid, 0:hl]
            v_out[rows, :] = kv[mid, hl : 2 * hl]
        return carry

    lax.fori_loop(0, total // (2 * BLK), project, 0)
    lo = iota((1, LANES), 1) < DH
    lane = iota((BLK, LANES), 1)
    lse = jnp.zeros((BLK, LANES), f32)
    for pair in range(hl // LANES):
        lanes = slice(pair * LANES, (pair + 1) * LANES)
        q2, k2, v2 = q_out[:, lanes], k_out[:, lanes], v_out[:, lanes]
        halves = []
        for half in range(2):
            h = 2 * pair + half
            keep = lo if half == 0 else jnp.logical_not(lo)
            qm = jnp.where(keep, q2, jnp.zeros_like(q2)) * bf16(1.0 / math.sqrt(DH))
            band = fr[h : h + 1, :]
            bias = bias_plane(band, band[:, 0:1], band[:, 511:512], cx, plane, total)
            s = nt(qm, k2) + bias + mask[...]
            top = jnp.max(s, axis=1, keepdims=True)
            e = jnp.exp(s - top)
            tot = jnp.sum(e, axis=1, keepdims=True)
            lse = jnp.where(lane == h, top + jnp.log(tot), lse)
            halves.append(nn((e * (1.0 / tot)).astype(bf16), v2))
        att_out[:, lanes] = jnp.where(lo, halves[0], halves[1]).astype(bf16)
    lse_out[...] = lse
    part_out[...] = nn(att_out[...], wo[...]).astype(bf16)


def mlp_weight_copies(pieces, fs, c, parts, wg, wu, wd):
    if not pieces:
        return list(zip(parts, (wg, wu, wd)))
    g, u, d, gu_mine, gu_twin, d_mine, d_twin = parts
    w = D // 2
    hw = w // 2
    hr = wd.shape[0] // 2
    out = []
    for j, (r, dst) in enumerate(((g, wg), (u, wu))):
        base = (1 - fs) * w
        out.append((r, dst.at[pl.ds(aligned(fs, w), w), :]))
        out.append((gu_mine.at[j], dst.at[pl.ds(pl.multiple_of(base + c * hw, hw), hw), :]))
        out.append((gu_twin.at[j], dst.at[pl.ds(pl.multiple_of(base + (1 - c) * hw, hw), hw), :]))
    other = pl.ds(aligned(1 - fs, w), w)
    out.append((d, wd.at[:, pl.ds(aligned(fs, w), w)]))
    out.append((d_mine, wd.at[pl.ds(aligned(c, hr), hr), other]))
    out.append((d_twin, wd.at[pl.ds(aligned(1 - c, hr), hr), other]))
    return out


def tanh_parts(x):
    k = math.sqrt(2.0 / math.pi)
    th = jnp.tanh(k * (x + 0.044715 * x * x * x))
    return th, k


def b_kernel(pieces, meta, tab_ref, hid_ref, mine_ref, other_ref, *refs):
    n = 7 if pieces else 3
    parts = refs[:n]
    res_out, act_out, gate_out, up_out, part_out = refs[n : n + 5]
    wg, wu, wd, sems = refs[n + 5 :]
    ffl = wg.shape[1]
    fs, cx, c = meta[0], meta[1], meta[3]
    made = run_copies(mlp_weight_copies(pieces, fs, c, parts, wg, wu, wd), sems)
    gain = param_rows(tab_ref)(GAIN2_ROW)
    res = hid_ref[cx >> 1].astype(f32) + (mine_ref[...].astype(f32) + other_ref[...].astype(f32))
    res_out[...] = res
    scale = lax.rsqrt(jnp.sum(res * res, axis=1, keepdims=True) * (1.0 / D) + EPS)
    n2 = (res * scale * gain).astype(bf16)
    act_out[:, 0:D] = n2
    for m in made:
        m.wait()
    gate = nn(n2, wg[...])
    up = nn(n2, wu[...])
    gate_out[...] = gate
    up_out[...] = up
    th, _ = tanh_parts(gate)
    gated = (0.5 * gate * (1.0 + th) * up).astype(bf16)
    act_out[:, D : D + ffl] = gated
    part_out[...] = nn(gated, wd[...]).astype(bf16)


def c_kernel(pieces, meta, len_ref, pad_ref, deal_ref, teach_ref, res_ref, mine_ref, other_ref, gate_ref, up_ref, *refs):
    n = 7 if pieces else 3
    parts = refs[:n]
    out_ref, loss_out, gres_out, act_out, part_out = refs[n : n + 5]
    wg, wu, wd, teacher, sems = refs[n + 5 :]
    ffl = wg.shape[1]
    fs, cx, tp, c = meta[0], meta[1], meta[2], meta[3]
    made = run_copies(mlp_weight_copies(pieces, fs, c, parts, wg, wu, wd), sems)
    slots, unit = teach_ref.shape[0], teach_ref.shape[1]
    for s in range(slots):
        teacher[s * unit : (s + 1) * unit, :] = teach_ref[deal_ref[fs, cx, s]].astype(f32)
    count = jnp.int32(0)
    for f in range(len_ref.shape[0]):
        for k in range(len_ref.shape[1]):
            count = count + ((2 * len_ref[f, k] - pad_ref[f, k] + 1) >> 1)
    real_count = jnp.broadcast_to(count, (1, LANES)).astype(f32)[:, 0:1]
    own = token_rows(len_ref, pad_ref, fs, BLK, cx * BLK)
    valid = nt(eye(), put_rows([own.real_e.astype(f32)], BLK), precision=HI)[:, 0:1]
    result = res_ref[...] + (mine_ref[...].astype(f32) + other_ref[...].astype(f32))
    width = out_ref.shape[1]
    out_ref[...] = jnp.where(tp == 0, result[:, 0:width], result[:, D - width : D]).astype(bf16)
    diff = (result - teacher[...]) * valid
    square = jnp.sum(jnp.sum(diff * diff, axis=1, keepdims=True), axis=0, keepdims=True)
    loss_out[...] = jnp.broadcast_to(square / (2.0 * D * real_count), (8, LANES))
    gres = diff * (GRAD_SCALE / (D * real_count))
    gres_out[...] = gres
    low = gres.astype(bf16)
    act_out[:, 0:D] = low
    for m in made:
        m.wait()
    ggated = nt(low, wd[...])
    gate = gate_ref[...]
    up = up_ref[...]
    th, k = tanh_parts(gate)
    value = 0.5 * gate * (1.0 + th)
    slope = 0.5 * (1.0 + th) + 0.5 * gate * (1.0 - th * th) * (k * (1.0 + 3.0 * 0.044715 * gate * gate))
    gg = (ggated * up * slope).astype(bf16)
    gu = (ggated * value).astype(bf16)
    act_out[:, D : D + ffl] = gg
    act_out[:, D + ffl : D + 2 * ffl] = gu
    part_out[...] = (nt(gg, wg[...]) + nt(gu, wu[...])).astype(bf16)


def m_kernel(split, ffl, meta, *refs):
    if not split:
        act1, act2, gu_out, down_out = refs
        n2, gated = act1[:, 0:D], act1[:, D : D + ffl]
        gu_out[0] = tn(n2, act2[:, D : D + ffl]).astype(bf16)
        gu_out[1] = tn(n2, act2[:, D + ffl : D + 2 * ffl]).astype(bf16)
        down_out[...] = tn(gated, act2[:, 0:D]).astype(bf16)
        return
    act1, act1_t, act2, act2_t, g_own, g_oth, u_own, u_oth, d_own, d_oth, wide, tall = refs
    fs, c = meta[0], meta[3]
    w = D // 2
    half = ffl // 2

    def both(mine, twin, first):
        lanes = pl.ds(pl.multiple_of(first + c * half, LANES), half)
        return jnp.concatenate([mine[:, lanes], twin[:, lanes]], axis=0)

    n2 = jnp.concatenate([act1[:, 0:D], act1_t[:, 0:D]], axis=0)
    low = jnp.concatenate([act2[:, 0:D], act2_t[:, 0:D]], axis=0)
    mine, other = pl.ds(aligned(fs, w), w), pl.ds(aligned(1 - fs, w), w)
    tall[...] = tn(both(act1, act1_t, D), low).astype(bf16)
    d_own[...] = tall[:, mine]
    d_oth[...] = tall[:, other]
    for first, own, oth in ((D, g_own, g_oth), (D + ffl, u_own, u_oth)):
        wide[...] = tn(n2, both(act2, act2_t, first)).astype(bf16)
        own[...] = wide[mine, :]
        oth[...] = wide[other, :]


def d_kernel(total, pieces, shards_at, tps, meta, len_ref, pad_ref, ext_ref, ext1_ref, tab_ref, n1_ref, q_ref, k_ref, v_ref, att_ref, lse_ref, res_ref, gres_ref, hid_mine, hid_twin, mine_ref, other_ref, *refs):
    n = 6 if pieces else 4
    parts = refs[:n]
    m = 2
    packs = refs[n : n + m]
    keep_out, send_out, extra_out = refs[n + m : n + m + 3]
    wqkv, wo, plane, mask, fr, dsw, stack, ga, dq, dkv, wide, wo_grad, dh, sems = refs[n + m + 3 :]
    fs, cx, tp, c = meta[0], meta[1], meta[2], meta[3]
    hl = wo.shape[0]
    made = run_copies(attn_weight_copies(pieces, fs, c, parts, wqkv, wo), sems)
    mask[...], _ = attn_masks(len_ref, pad_ref, fs, cx, total)
    fr[...] = bias_rows(tab_ref, ext_ref, tp, shards_at)
    gain = param_rows(tab_ref)(GAIN2_ROW)
    gn2 = mine_ref[...].astype(f32) + other_ref[...].astype(f32)
    res = res_ref[...]
    r2 = lax.rsqrt(jnp.sum(res * res, axis=1, keepdims=True) * (1.0 / D) + EPS)
    u = gain * gn2
    gain_grad = jnp.sum(gn2 * res * r2, axis=0, keepdims=True) * (1.0 / tps)
    back = gres_ref[...] + r2 * u - res * (r2 * r2 * r2 * (jnp.sum(u * res, axis=1, keepdims=True) * (1.0 / D)))
    branch = back.astype(bf16)
    for x in made:
        x.wait()
    wo_grad[...] = tn(att_ref[...], branch).astype(bf16)
    ga[...] = nt(branch, wo[...]).astype(bf16)
    lo = iota((1, LANES), 1) < DH
    at = iota((1, total), 1)
    first = cx * BLK - BLK
    rev = (iota((BLK, BLK), 0) + iota((BLK, BLK), 1) == BLK - 1).astype(bf16)
    band_at = iota((1, 512), 1)
    scale = bf16(1.0 / math.sqrt(DH))
    sums = []
    for pair in range(hl // LANES):
        lanes = slice(pair * LANES, (pair + 1) * LANES)
        q2, k2, v2, g2 = q_ref[:, lanes], k_ref[:, lanes], v_ref[:, lanes], ga[:, lanes]
        zero = jnp.zeros_like(q2)
        qs, gs, dqs = [], [], []
        for half in range(2):
            h = 2 * pair + half
            keep = lo if half == 0 else jnp.logical_not(lo)
            qm = jnp.where(keep, q2, zero) * scale
            gm = jnp.where(keep, g2, zero)
            band = fr[h : h + 1, :]
            bias = bias_plane(band, band[:, 0:1], band[:, 511:512], cx, plane, total)
            s = nt(qm, k2) + bias + mask[...]
            p = jnp.exp(s - lse_ref[:, h : h + 1])
            g = nt(gm, v2)
            inner = jnp.sum(p * g, axis=1, keepdims=True)
            ds = p * (g - inner)
            low = ds.astype(bf16)
            stack[0, half * BLK : (half + 1) * BLK, :] = low
            stack[1, half * BLK : (half + 1) * BLK, :] = p.astype(bf16)
            wide_ds = low.astype(f32)
            col = jnp.sum(wide_ds, axis=0, keepdims=True)
            left = jnp.sum(jnp.where(at < first, col, 0.0), axis=1, keepdims=True)
            right = jnp.sum(jnp.where(at >= first + 3 * BLK, col, 0.0), axis=1, keepdims=True)
            dsw[:, BLK : BLK + total] = wide_ds
            if pair == 0 and half == 0:
                dsw[:, 0:BLK] = jnp.zeros((BLK, BLK), f32)
                dsw[:, BLK + total :] = jnp.zeros((BLK, 2 * BLK), f32)
            window = dsw[:, pl.ds(aligned(cx, BLK), 512)]
            window = jnp.where(band_at < 3 * BLK, window, 0.0).astype(bf16)
            turned = pltpu.roll(nn(rev, window), 0, 1, stride=1, stride_axis=0)
            diag = jnp.sum(turned, axis=0, keepdims=True)
            diag = diag + jnp.where(band_at == 0, left, 0.0) + jnp.where(band_at == 510, right, 0.0)
            sums.append(diag)
            dqs.append(nn(low, k2))
            qs.append(qm)
            gs.append(gm)
        dq[:, lanes] = (jnp.where(lo, dqs[0], dqs[1]) * (1.0 / math.sqrt(DH))).astype(bf16)
        dkv[:, lanes] = tn(stack[0], jnp.concatenate(qs, axis=0)).astype(bf16)
        dkv[:, hl + pair * LANES : hl + (pair + 1) * LANES] = tn(stack[1], jnp.concatenate(gs, axis=0)).astype(bf16)
    own = pl.ds(aligned(cx, BLK), BLK)
    wide[0] = tn(n1_ref[own, :], dq[...]).astype(bf16)
    both = tn(n1_ref[...], dkv[...])
    wide[1] = both[:, 0:hl].astype(bf16)
    wide[2] = both[:, hl : 2 * hl].astype(bf16)
    if pieces:
        w, hw = D // 2, D // 4
        for half, ref in enumerate(packs):
            cc = c if half == 0 else 1 - c
            for rel in range(2):
                f = fs if rel == 0 else 1 - fs
                for j in range(3):
                    ref[rel, j] = wide[j, pl.ds(pl.multiple_of(f * w + cc * hw, hw), hw), :]
                ref[rel, 3] = wo_grad[pl.ds(aligned(cc, hw), hw), pl.ds(aligned(f, w), w)]
    else:
        packs[0][...] = wide[...]
        packs[1][...] = wo_grad[...]
    own_grad = nt(dq[...], wqkv[:, 0:hl])
    gain1 = param_rows(tab_ref)(GAIN1_ROW)
    dh[0:HALO, :] = jnp.zeros((HALO, D), f32)
    dh[total + HALO : total + 2 * HALO, :] = jnp.zeros((HALO, D), f32)

    def norm_back(h, grad):
        r = lax.rsqrt(jnp.sum(h * h, axis=1, keepdims=True) * (1.0 / D) + EPS)
        u = gain1 * grad
        d = r * u - h * (r * r * r * (jnp.sum(u * h, axis=1, keepdims=True) * (1.0 / D)))
        return d, jnp.sum(grad * h * r, axis=0, keepdims=True)

    def back_rows(i, carry):
        for k, hid in enumerate((hid_mine, hid_twin)):
            b = 2 * i + (c if k == 0 else 1 - c)
            grad = nt(dkv[pl.ds(aligned(b, BLK), BLK), :], wqkv[:, hl : 3 * hl])
            d, g = norm_back(hid[i].astype(f32), grad)
            dh[pl.ds(pl.multiple_of(b * BLK + HALO, HALO), BLK), :] = d
            carry = carry + g
        return carry

    gain1_grad = lax.fori_loop(0, total // (2 * BLK), back_rows, jnp.zeros((1, D), f32))
    d, g = norm_back(hid_mine[cx >> 1].astype(f32), own_grad)
    gain1_grad = gain1_grad + g
    here = pl.ds(pl.multiple_of(cx * BLK + HALO, HALO), BLK)
    dh[here, :] = dh[here, :] + (d + back * (1.0 / tps))

    def windows(i, carry):
        for k, out in enumerate((keep_out, send_out)):
            b = 2 * i + (c if k == 0 else 1 - c)
            out[i] = dh[pl.ds(aligned(b, BLK), WIN), :].astype(bf16)
        return carry

    lax.fori_loop(0, total // (2 * BLK), windows, 0)
    rows = put_rows(sums, 512)
    ext = ext1_ref[...]
    width = NB // len(shards_at)
    sub = iota((LANES, 512), 0)
    extra_out[...] = jnp.zeros(extra_out.shape, f32)
    for j, lane in enumerate(shards_at):
        hot = ((sub < width) & (sub + j * width == ext)).astype(f32)
        extra_out[pl.ds(aligned(tp, 8), 8), lane : lane + LANES] = nt(rows, hot, precision=HI)
    extra_out[16:24, :] = put_rows([gain1_grad, gain_grad], D)


def e_kernel(total, split, spots, meta, len_ref, pad_ref, ids_ref, tab_ref, conv_ref, rows_ref, keep_ref, recv_ref, extra_ref, loss_ref, *refs):
    n = 2 if split else 1
    outs = refs[:n]
    xr, dz, idr, dh, dc, hots, wide = refs[n:]
    fs, cx, c = meta[0], meta[1], meta[3]
    windows = total // (2 * BLK)
    step = 2 * BLK
    lay = token_rows(len_ref, pad_ref, fs, total, c * BLK - HALO, total)
    xr[...] = jnp.zeros(xr.shape, f32)
    s_at, t_at = iota((WIN, WIN), 0), iota((WIN, WIN), 1)

    def inner(i, carry):
        d = (keep_ref[i].astype(f32) + recv_ref[i].astype(f32)).astype(bf16)
        dh[i] = d
        for k in range(2):
            gram = nt(conv_ref[k, i], d)
            for j in range(3):
                part = jnp.sum(jnp.where(s_at == t_at + (j - 1), gram, 0.0), axis=0, keepdims=True)
                xr[2 * j + k, 0:1, pl.ds(aligned(i, step), WIN)] = part
        return carry

    lax.fori_loop(0, windows, inner, 0)
    x = [0.5 * xr[k, 0:1, :] for k in range(6)]
    pe, po = forms(x, lay)
    we = [get_row(rows_ref[0:8, :], k) for k in range(4)]
    wo = [get_row(rows_ref[0:8, :], k + 4) for k in range(4)]

    def soft_back(w, p):
        mean = w[0] * p[0] + w[1] * p[1] + w[2] * p[2] + w[3] * p[3]
        return [a * (b - mean) for a, b in zip(w, p)]

    em, om, e0, o0, ep, op = spread(soft_back(we, pe), soft_back(wo, po), lay)
    dze = e0 + after(em) + before(ep)
    dzo = o0 + after(om) + before(op)
    dz[...] = put_rows([dze, dzo], total)
    score = jnp.broadcast_to(tab_ref[SCORE_ROW : SCORE_ROW + 1, :], (WIN, D))
    sub16 = iota((16, WIN), 0)
    at16 = iota((16, WIN), 1)
    own16 = (at16 >= HALO) & (at16 < HALO + BLK)

    def stencil(i, carry):
        lanes = pl.ds(aligned(i, step), WIN)
        d = dh[i]
        for k in range(2):
            z = dz[k : k + 1, lanes]
            mid = rows_ref[8 + k : 9 + k, lanes]
            prv = rows_ref[10 + k : 11 + k, lanes]
            nxt = rows_ref[12 + k : 13 + k, lanes]
            band = jnp.where(t_at == s_at, mid, 0.0)
            band = jnp.where(t_at == s_at + 1, prv, band)
            band = jnp.where(t_at == s_at - 1, nxt, band)
            grad = nn(band.astype(bf16), d) + nn(jnp.where(t_at == s_at, z, 0.0).astype(bf16), score)
            dc[k, pl.ds(aligned(i, BLK), BLK), :] = grad[HALO : HALO + BLK].astype(bf16)
            top = z.astype(bf16).astype(f32)
            pair = jnp.where(sub16 == 0, top, jnp.where(sub16 == 1, z - top, 0.0))
            carry = carry + nn(jnp.where(own16, pair, 0.0).astype(bf16), conv_ref[k, i])
        return carry

    score_rows = lax.fori_loop(0, windows, stencil, jnp.zeros((16, D), f32))
    score_grad = jnp.sum(score_rows, axis=0, keepdims=True)
    whole = token_rows(len_ref, pad_ref, fs, total)
    raw = id_rows(ids_ref)
    id_e = jnp.where(whole.real_e, raw[0], -1).astype(f32)
    id_o = jnp.where(whole.real_o, raw[1], -1).astype(f32)
    later = whole.v > 0.0
    idr[...] = put_rows(
        [
            jnp.where(whole.prev > 0.0, before(id_o), -1.0),
            id_e,
            id_o,
            jnp.where(later, after(id_e), -1.0),
            jnp.where(later, after(id_o), -1.0),
        ],
        total,
    )
    v_at = iota((SROWS, BLK), 0)
    symbol = v_at.astype(f32)

    def spell(i, carry):
        lanes = pl.ds(aligned(2 * i + c, BLK), BLK)
        for k in range(5):
            hot = symbol == idr[k : k + 1, lanes]
            if k == 1:
                hot = hot | (v_at == SROWS - 1)
            hots[k * SROWS : (k + 1) * SROWS, pl.ds(aligned(i, BLK), BLK)] = hot.astype(f32).astype(bf16)
        return carry

    lax.fori_loop(0, windows, spell, 0)
    wide[...] = jnp.zeros(wide.shape, f32)
    table_rows = VOCAB + 5
    taps = tab_ref[TAP_ROW - 3 : TAP_ROW + 13, :].astype(f32)[3 : 3 + CONV]
    table = tab_ref[0:table_rows, :].astype(f32)
    shift_grad = jnp.zeros((1, D), f32)
    for j in range(CONV):
        acc = nn(hots[j * SROWS : (j + 1) * SROWS, :], dc[0]) + nn(hots[(j + 1) * SROWS : (j + 2) * SROWS, :], dc[1])
        wide[0:table_rows, :] += taps[j : j + 1] * acc[0:table_rows]
        tap_grad = jnp.sum(table * acc[0:table_rows], axis=0, keepdims=True)
        shift_grad = shift_grad + acc[SROWS - 1 : SROWS, :]
        wide[SROWS + j : SROWS + j + 1, :] = tap_grad
    for j in range(CONV):
        wide[TAP_ROW + j : TAP_ROW + j + 1, :] = wide[SROWS + j : SROWS + j + 1, :]
    wide[SHIFT_ROW : SHIFT_ROW + 1, :] = shift_grad
    wide[SCORE_ROW : SCORE_ROW + 1, :] = score_grad
    wide[GAIN1_ROW : GAIN1_ROW + 1, :] = extra_ref[16:17, :]
    wide[GAIN2_ROW : GAIN2_ROW + 1, :] = extra_ref[17:18, :]
    wide[BIAS_ROW : BIAS_ROW + 16, :] = extra_ref[0:16, :]
    part = loss_ref[0:1, :]
    top = part.astype(bf16).astype(f32)
    rest = part - top
    middle = rest.astype(bf16).astype(f32)
    at = iota((1, LANES), 1) - 4 * (fs * spots + cx)
    coded = jnp.where(at == 0, top, jnp.where(at == 1, middle, jnp.where(at == 2, rest - middle, 0.0)))
    coded = jnp.where(meta[2] == 0, coded, 0.0)
    for lane in (0, D // 2):
        wide[LOSS_ROW : LOSS_ROW + 1, lane : lane + LANES] = coded
    if not split:
        outs[0][...] = wide[0:SROWS, :].astype(bf16)
        return
    w = D // 2
    hr = SROWS // 2
    for half, ref in enumerate(outs):
        cc = c if half == 0 else 1 - c
        for rel in range(2):
            f = fs if rel == 0 else 1 - fs
            ref[rel] = wide[pl.ds(pl.multiple_of(cc * hr, 8), hr), pl.ds(aligned(f, w), w)].astype(bf16)


def f_mlp_kernel(half, meta, g, g_t, u, u_t, d, d_t, g_out, u_out, d_out):
    c = meta[3]
    mine, other = pl.ds(aligned(c, half), half), pl.ds(aligned(1 - c, half), half)
    for a, b, out in ((g, g_t, g_out), (u, u_t, u_out)):
        out[:, mine] = a[...].astype(f32)
        out[:, other] = b[...].astype(f32)
    d_out[mine, :] = d[...].astype(f32)
    d_out[other, :] = d_t[...].astype(f32)


def f_attn_kernel(meta, x, x_t, *outs):
    c = meta[3]
    hw = x.shape[1]
    for j, out in enumerate(outs):
        out[pl.ds(aligned(c, hw), hw), :] = x[j].astype(f32)
        out[pl.ds(aligned(1 - c, hw), hw), :] = x_t[j].astype(f32)


def f_small_kernel(meta, x, x_t, loss, table, taps, shift, score, gain1, gain2, bias, whole):
    tp, c = meta[2], meta[3]
    hr = x.shape[0]
    whole[pl.ds(aligned(c, hr), hr), :] = x[...].astype(f32)
    whole[pl.ds(aligned(1 - c, hr), hr), :] = x_t[...].astype(f32)
    loss[...] = jnp.broadcast_to(jnp.sum(whole[LOSS_ROW : LOSS_ROW + 1, 0:LANES], axis=1, keepdims=True), (8, LANES))
    table[...] = whole[0:VOCAB, :]
    taps[...] = whole[TAP_ROW : TAP_ROW + CONV, :]
    for k, out in ((SHIFT_ROW, shift), (SCORE_ROW, score), (GAIN1_ROW, gain1), (GAIN2_ROW, gain2)):
        out[...] = whole[k : k + 1, :]
    bias[...] = whole[pl.ds(pl.multiple_of(BIAS_ROW + 8 * tp, 8), 8), 0:LANES]


def sds(shape, dtype):
    return jax.ShapeDtypeStruct(shape, dtype)


def call(kernel, name, us, ins, in_specs, out_shape, scratch):
    return pl.pallas_call(
        kernel,
        name=name,
        cost_estimate=pl.CostEstimate(flops=0, transcendentals=0, bytes_accessed=int(us * 3.69e6)),
        out_shape=out_shape,
        in_specs=in_specs,
        out_specs=jax.tree.map(lambda _: VM, out_shape),
        scratch_shapes=scratch,
        compiler_params=pltpu.CompilerParams(vmem_limit_bytes=60 << 20),
    )(*ins)


def add2(a, b):
    return (a.astype(f32) + b.astype(f32)).astype(bf16)


def shards(
    byte_ids,
    seq_tokens,
    pad_bytes,
    deal_targets,
    rel_buckets,
    embedding,
    conv_weight,
    conv_bias,
    score_weight,
    attn_gain,
    query_weight,
    key_weight,
    value_weight,
    rel_bias,
    out_weight,
    mlp_gain,
    gate_weight,
    up_weight,
    down_weight,
    teacher,
):
    fs = lax.axis_index("fsdp")
    cx = lax.axis_index("ctx")
    tp = lax.axis_index("tp")
    fcount, ccount, tps = lax.axis_size("fsdp"), lax.axis_size("ctx"), lax.axis_size("tp")
    core = cx % 2
    total = teacher.shape[0] * ccount
    unit = teacher.shape[0] // ccount
    hl = query_weight.shape[1]
    heads = hl // DH
    ffl = gate_weight.shape[1]
    split = fcount == 2
    wloc = D // fcount
    bloc = NB // fcount
    meta = jnp.stack([fs, cx, tp, core]).astype(i32)

    def twin(x):
        return lax.ppermute(x, "ctx", [(i, i ^ 1) for i in range(ccount)])

    def across(x):
        return lax.ppermute(x, "fsdp", [(0, 1), (1, 0)])

    def tp_other(x):
        return lax.ppermute(x, "tp", [(i, tps - 1 - i) for i in range(tps)])

    def core_half(x, axis):
        n = x.shape[axis] // 2
        return lax.dynamic_slice_in_dim(x, core * n, n, axis)

    ends = lambda k: jnp.broadcast_to(rel_buckets[k : k + 1], (RMAX,))
    ext = jnp.concatenate([ends(0), rel_buckets, ends(2 * RMAX)])
    ext, ext1 = ext[None, :512], ext[None, 1:513]

    def exchange(x):
        return lax.all_to_all(x, "ctx", split_axis=0, concat_axis=0, tiled=True)

    bias_t = jnp.pad(rel_bias.T, ((0, 16 - heads), (0, wloc - bloc)))
    small = jnp.concatenate(
        [
            embedding,
            conv_weight,
            conv_bias[None],
            score_weight[None],
            attn_gain[None],
            mlp_gain[None],
            jnp.zeros((BIAS_ROW - GAIN2_ROW - 1, wloc), bf16),
            bias_t,
        ],
        axis=0,
    )
    ids = exchange(jnp.broadcast_to(byte_ids.reshape(-1, 2).T[None], (ccount, 2, byte_ids.shape[0] // 2)))
    if split:
        small_other = across(small)
        small_parts = (small, small_other)
        attn = jnp.stack([query_weight, key_weight, value_weight, out_weight])
        mine = across(core_half(attn, 1))
    else:
        gather = lambda x, axis: lax.all_gather(x, "fsdp", axis=axis, tiled=True)
        full = gather(small, 1)
        bias_all = jnp.pad(gather(rel_bias, 0).T, ((0, 16 - heads), (0, D - NB)))
        small_parts = (jnp.concatenate([full[:BIAS_ROW], bias_all], axis=0),)
        attn_parts = (gather(query_weight, 0), gather(key_weight, 0), gather(value_weight, 0), gather(out_weight, 1))
        mlp_parts = (gather(gate_weight, 0), gather(up_weight, 0), gather(down_weight, 1))
    shards_at = (0, wloc) if split else (0,)
    teach_in, ids = lax.optimization_barrier((teacher.reshape(ccount, unit, D), ids))
    teach = exchange(teach_in)

    nw = total // (2 * BLK)
    tab, hid, n1, conv, rows = call(
        functools.partial(g_kernel, total, split),
        "g",
        8,
        (meta, seq_tokens, pad_bytes, ids) + small_parts,
        [SM, SM, SM, VM] + [ANY] * len(small_parts),
        (
            sds((VP, D), bf16),
            sds((nw, BLK, D), bf16),
            sds((nw, BLK, D), bf16),
            sds((2, nw, WIN, D), bf16),
            sds((16, total), f32),
        ),
        [
            pltpu.VMEM((VP, D), bf16),
            pltpu.VMEM((2 * WIN, VP), bf16),
            pltpu.VMEM((WIN, D), f32),
            pltpu.VMEM((WIN, D), f32),
            pltpu.VMEM((8, total), f32),
            pltpu.VMEM((8, total), f32),
            pltpu.VMEM((8, total), f32),
            pltpu.VMEM((8, total), f32),
            pltpu.SemaphoreType.DMA((2,)),
        ],
    )
    n1_twin = twin(n1)
    hid_twin = twin(hid)
    if split:
        mine, n1_twin, teach = lax.optimization_barrier((mine, n1_twin, teach))
        attn_parts = (query_weight, key_weight, value_weight, out_weight, mine, twin(mine))
        gu_half = core_half(jnp.stack([gate_weight, up_weight]), 1)
        d_half = core_half(down_weight, 0)
        gu_half, d_half, _ = lax.optimization_barrier((gu_half, d_half, mine))
        gu_mine = across(gu_half)
        d_mine = across(d_half)
    na = len(attn_parts)
    attn_scratch = [
        pltpu.VMEM((D, 3 * hl), bf16),
        pltpu.VMEM((hl, D), bf16),
        pltpu.VMEM((BLK, total + 2 * BLK), f32),
        pltpu.VMEM((BLK, total), f32),
        pltpu.VMEM((16, 512), f32),
    ]
    q, k, v, att, lse, part, n1_full = call(
        functools.partial(a_kernel, total, split, shards_at),
        "a",
        10,
        (meta, seq_tokens, pad_bytes, ext, tab, n1, n1_twin) + attn_parts,
        [SM, SM, SM, VM, VM, VM, VM] + [ANY] * na,
        (
            sds((BLK, hl), bf16),
            sds((total, hl), bf16),
            sds((total, hl), bf16),
            sds((BLK, hl), bf16),
            sds((BLK, LANES), f32),
            sds((BLK, D), bf16),
            sds((total, D), bf16),
        ),
        attn_scratch + [pltpu.SemaphoreType.DMA((12,))],
    )
    part_other = tp_other(part)
    if split:
        gu_mine, d_mine, part = lax.optimization_barrier((gu_mine, d_mine, part))
        mlp_parts = (gate_weight, up_weight, down_weight, gu_mine, twin(gu_mine), d_mine, twin(d_mine))
    nm = len(mlp_parts)
    mlp_scratch = [pltpu.VMEM((D, ffl), bf16), pltpu.VMEM((D, ffl), bf16), pltpu.VMEM((ffl, D), bf16)]
    res, act1, gate, up, part2 = call(
        functools.partial(b_kernel, split),
        "b",
        6,
        (meta, tab, hid, part, part_other) + mlp_parts,
        [SM, VM, VM, VM, VM] + [ANY] * nm,
        (
            sds((BLK, D), f32),
            sds((BLK, D + ffl), bf16),
            sds((BLK, ffl), f32),
            sds((BLK, ffl), f32),
            sds((BLK, D), bf16),
        ),
        mlp_scratch + [pltpu.SemaphoreType.DMA((9,))],
    )
    part2_other = tp_other(part2)
    if split:
        act1_t = twin(act1)
        act1_t, part2_other = lax.optimization_barrier((act1_t, part2_other))
    output, loss, gres, act2, part3 = call(
        functools.partial(c_kernel, split),
        "c",
        7,
        (meta, seq_tokens, pad_bytes, deal_targets, teach, res, part2, part2_other, gate, up) + mlp_parts,
        [SM, SM, SM, SM, VM, VM, VM, VM, VM, VM] + [ANY] * nm,
        (
            sds((BLK, D // tps), bf16),
            sds((8, LANES), f32),
            sds((BLK, D), f32),
            sds((BLK, D + 2 * ffl), bf16),
            sds((BLK, D), bf16),
        ),
        mlp_scratch + [pltpu.VMEM((BLK, D), f32), pltpu.SemaphoreType.DMA((9,))],
    )
    part3_other = tp_other(part3)
    quarter = D // 4
    half = ffl // 2
    if split:
        mlp_ins = (act1, act1_t, act2, twin(act2))
        mlp_shape = (sds((wloc, half), bf16),) * 4 + (sds((half, wloc), bf16),) * 2
        mlp_tmp = [pltpu.VMEM((D, half), bf16), pltpu.VMEM((half, D), bf16)]
    else:
        mlp_ins = (act1, act2)
        mlp_shape = (sds((2, D, ffl), bf16), sds((ffl, D), bf16))
        mlp_tmp = []
    mlp_pack = call(
        functools.partial(m_kernel, split, ffl), "m", 4, (meta,) + mlp_ins, [SM] + [VM] * len(mlp_ins), mlp_shape, mlp_tmp
    )
    if split:
        part3_other, *mlp_pack = lax.optimization_barrier((part3_other, *mlp_pack))
        g_own, g_oth, u_own, u_oth, d_own, d_oth = mlp_pack
        g_near = across(g_oth)
    attn_shape = (sds((2, 4, quarter, hl), bf16),) * 2 if split else (sds((3, D, hl), bf16), sds((hl, D), bf16))
    *attn_pack, dh_keep, dh_send, extra = call(
        functools.partial(d_kernel, total, split, shards_at, tps),
        "d",
        15,
        (meta, seq_tokens, pad_bytes, ext, ext1, tab, n1_full, q, k, v, att, lse, res, gres, hid, hid_twin, part3, part3_other) + attn_parts,
        [SM, SM, SM] + [VM] * 15 + [ANY] * na,
        attn_shape + (sds((nw, WIN, D), bf16),) * 2 + (sds((24, D), f32),),
        attn_scratch
        + [
            pltpu.VMEM((BLK, total + 3 * BLK), f32),
            pltpu.VMEM((2, 2 * BLK, total), bf16),
            pltpu.VMEM((BLK, hl), bf16),
            pltpu.VMEM((BLK, hl), bf16),
            pltpu.VMEM((total, 2 * hl), bf16),
            pltpu.VMEM((3, D, hl), bf16),
            pltpu.VMEM((hl, D), bf16),
            pltpu.VMEM((total + 2 * HALO, D), f32),
            pltpu.SemaphoreType.DMA((12,)),
        ],
    )
    if split:
        dh_keep, g_near = lax.optimization_barrier((dh_keep, g_near))
    dh_recv = twin(dh_send)
    small_shape = (sds((2, SROWS // 2, wloc), bf16),) * 2 if split else (sds((SROWS, D), bf16),)
    small_pack = call(
        functools.partial(e_kernel, total, split, ccount),
        "e",
        9,
        (meta, seq_tokens, pad_bytes, ids, tab, conv, rows, dh_keep, dh_recv, extra, loss),
        [SM, SM, SM] + [VM] * 8,
        small_shape,
        [
            pltpu.VMEM((6, 8, total), f32),
            pltpu.VMEM((8, total), f32),
            pltpu.VMEM((8, total), f32),
            pltpu.VMEM((nw, WIN, D), bf16),
            pltpu.VMEM((2, total // 2, D), bf16),
            pltpu.VMEM((5 * SROWS, total // 2), bf16),
            pltpu.VMEM((SROWS + 8, D), f32),
        ],
    )

    def ctx_perm(x, bit):
        return lax.ppermute(x, "ctx", [(i, i ^ bit) for i in range(ccount)])

    chip = cx // 2
    inner = (chip == 1) | (chip == 2)

    def chips(x, pairs):
        return lax.ppermute(x, "ctx", [(2 * a + k, 2 * b + k) for a, b in pairs for k in range(2)])

    def line_sum(t):
        t = add2(t, chips(t, [(0, 1), (3, 2)]))
        t = add2(t, chips(t, [(1, 2), (2, 1)]))
        return jnp.where(inner, t, chips(t, [(1, 0), (2, 3)]))

    if split:
        parts = []
        for own, near in ((g_own, g_near), (u_own, across(u_oth)), (d_own, across(d_oth))):
            x = line_sum(add2(own, near))
            parts += [x, twin(x)]
        gate_grad, up_grad, down_grad = call(
            functools.partial(f_mlp_kernel, half),
            "f",
            5,
            (meta,) + tuple(parts),
            [SM] + [VM] * 6,
            (sds((wloc, ffl), f32), sds((wloc, ffl), f32), sds((ffl, wloc), f32)),
            [],
        )
        keep, send = attn_pack
        s = add2(keep, twin(send))
        x = line_sum(add2(s[0], across(s[1])))
        attn_grads = call(
            f_attn_kernel,
            "h",
            3,
            (meta, x, twin(x)),
            [SM] + [VM] * 2,
            (sds((wloc, hl), f32),) * 3 + (sds((hl, wloc), f32),),
            [],
        )
        keep, send = small_pack
        s = add2(keep, twin(send))
        t = add2(s[0], across(s[1]))
        t = add2(t, tp_other(t))
        t = add2(t, ctx_perm(t, 2))
        t = add2(t, ctx_perm(t, 4))
        loss, table_grad, taps_grad, shift_grad, score_grad, gain1_grad, gain2_grad, bias_grad = call(
            f_small_kernel,
            "s",
            1,
            (meta, t, twin(t)),
            [SM] + [VM] * 2,
            (
                sds((8, LANES), f32),
                sds((VOCAB, wloc), f32),
                sds((CONV, wloc), f32),
                sds((1, wloc), f32),
                sds((1, wloc), f32),
                sds((1, wloc), f32),
                sds((1, wloc), f32),
                sds((8, LANES), f32),
            ),
            [pltpu.VMEM((SROWS, wloc), f32)],
        )
        shift_grad, score_grad, gain1_grad, gain2_grad = shift_grad[0], score_grad[0], gain1_grad[0], gain2_grad[0]
        bias_grad = bias_grad[:heads, :bloc].T
    else:

        def owner_sum(x, axis, axes="ctx"):
            return lax.psum(lax.psum_scatter(x, "fsdp", scatter_dimension=axis, tiled=True), axes).astype(f32)

        gu, down = mlp_pack
        gate_grad, up_grad = owner_sum(gu, 1)
        down_grad = owner_sum(down, 1)
        qkv, wo = attn_pack
        attn_grads = tuple(owner_sum(qkv, 1)) + (owner_sum(wo, 1),)
        (x,) = small_pack
        t = owner_sum(x, 1, ("ctx", "tp"))
        table_grad, taps_grad, shift_grad, score_grad = t[:VOCAB], t[TAP_ROW : TAP_ROW + CONV], t[SHIFT_ROW], t[SCORE_ROW]
        gain1_grad, gain2_grad = t[GAIN1_ROW], t[GAIN2_ROW]
        x = lax.dynamic_slice_in_dim(x, BIAS_ROW + 8 * tp, 8, 0)[:heads, :NB].T
        bias_grad = lax.dynamic_slice_in_dim(lax.psum(x, ("fsdp", "ctx")).astype(f32), fs * bloc, bloc, 0)
        loss = lax.psum(loss, ("fsdp", "ctx"))
    query_grad, key_grad, value_grad, out_grad = attn_grads
    return (
        output,
        table_grad,
        taps_grad,
        shift_grad,
        score_grad,
        gain1_grad,
        query_grad,
        key_grad,
        value_grad,
        bias_grad,
        out_grad,
        gain2_grad,
        gate_grad,
        up_grad,
        down_grad,
        loss[0, 0],
    )


def solution(mesh):
    both = ("fsdp", "ctx")
    in_specs = (
        P(both),
        P(),
        P(),
        P(),
        P(),
        P(None, "fsdp"),
        P(None, "fsdp"),
        P("fsdp"),
        P("fsdp"),
        P("fsdp"),
        P("fsdp", "tp"),
        P("fsdp", "tp"),
        P("fsdp", "tp"),
        P("fsdp", "tp"),
        P("tp", "fsdp"),
        P("fsdp"),
        P("fsdp", "tp"),
        P("fsdp", "tp"),
        P("tp", "fsdp"),
        P(both, None),
    )
    out_specs = (
        P(both, "tp"),
        P(None, "fsdp"),
        P(None, "fsdp"),
        P("fsdp"),
        P("fsdp"),
        P("fsdp"),
        P("fsdp", "tp"),
        P("fsdp", "tp"),
        P("fsdp", "tp"),
        P("fsdp", "tp"),
        P("tp", "fsdp"),
        P("fsdp"),
        P("fsdp", "tp"),
        P("fsdp", "tp"),
        P("tp", "fsdp"),
        P(),
    )
    return jax.shard_map(shards, mesh=mesh, in_specs=in_specs, out_specs=out_specs, check_vma=False)
```

```python
import functools
import math

import jax
import jax.numpy as jnp
from jax import lax
from jax.experimental import pallas as pl
from jax.experimental.pallas import tpu as pltpu
from jax.sharding import PartitionSpec as P

D = 768
DH = 64
VOCAB = 259
NB = 32
RMAX = 128
CONV = 4

EPS = 1e-06
NEG = -1e30
GRAD_SCALE = 65536.0
LANES = 128
BLK = 128
HALO = 8
WIN = BLK + 2 * HALO
VP = 384
SROWS = 288
TAP_ROW = VOCAB
SHIFT_ROW = VOCAB + 4
SCORE_ROW = VOCAB + 5
GAIN1_ROW = VOCAB + 6
GAIN2_ROW = VOCAB + 7
BIAS_ROW = 272
LOSS_ROW = 267
f32 = jnp.float32
bf16 = jnp.bfloat16
i32 = jnp.int32
HI = lax.Precision.HIGHEST
ANY = pl.BlockSpec(memory_space=pl.ANY)
VM = pl.BlockSpec(memory_space=pltpu.VMEM)
SM = pl.BlockSpec(memory_space=pltpu.SMEM)


def nn(a, b, **k):
    return lax.dot_general(a, b, (((1,), (0,)), ((), ())), preferred_element_type=f32, **k)


def nt(a, b, **k):
    return lax.dot_general(a, b, (((1,), (1,)), ((), ())), preferred_element_type=f32, **k)


def tn(a, b, **k):
    return lax.dot_general(a, b, (((0,), (0,)), ((), ())), preferred_element_type=f32, **k)


def iota(shape, axis):
    return lax.broadcasted_iota(i32, shape, axis)


def aligned(index, step):
    return pl.multiple_of(index * step, step)


class Layout:
    pass


def token_rows(len_ref, pad_ref, fs, total, first=0, whole=1 << 30):
    t = iota((1, total), 1) + first
    live = (t >= 0) & (t < whole)
    start = jnp.zeros_like(t)
    end = jnp.zeros_like(t)
    limit = jnp.zeros_like(t)
    seg = jnp.zeros_like(t)
    base = jnp.int32(0)
    for k in range(len_ref.shape[1]):
        n = len_ref[fs, k]
        inside = t >= base
        start = jnp.where(inside, base, start)
        end = jnp.where(inside, base + n, end)
        limit = jnp.where(inside, 2 * n - pad_ref[fs, k], limit)
        seg = jnp.where(inside, k, seg)
        base = base + n
    lay = Layout()
    rel = t - start
    lay.seg = seg
    lay.real_e = live & (2 * rel < limit)
    lay.real_o = live & (2 * rel + 1 < limit)
    lay.prev = (live & (rel > 0)).astype(f32)
    lay.v = (live & (t + 1 < end)).astype(f32)
    third = (rel * 43691) >> 17
    u = rel - 3 * third
    lay.u0 = (u == 0).astype(f32)
    lay.u1 = (u == 1).astype(f32)
    lay.u2 = (u == 2).astype(f32)
    lay.odd = (rel & 1).astype(f32)
    lay.even = 1.0 - lay.odd
    third_f = jnp.float32(1.0 / 3.0)
    last0 = jnp.where(t + 1 < end, third_f, 0.5)
    lay.inv_e3 = jnp.where(u == 0, last0, third_f)
    lay.inv_o3 = jnp.where(u == 0, last0, jnp.where(u == 1, jnp.where(t + 1 < end, third_f, 1.0), third_f))
    lay.inv4 = jnp.where((rel & 1) == 1, 0.25, jnp.where(t + 1 < end, 0.25, 0.5))
    return lay


def forms(x, lay):
    em, om, e0, o0, ep, op = x
    pair = e0 + o0
    after = lay.v * (ep + op)
    first = pair + lay.v * ep
    closing = om + pair
    p2 = 0.5 * pair
    e3 = (lay.u0 * first + lay.u1 * (em + om + e0) + lay.u2 * closing) * lay.inv_e3
    o3 = (lay.u0 * first + lay.u1 * (o0 + after) + lay.u2 * closing) * lay.inv_o3
    p4 = (pair + lay.odd * (em + om) + lay.even * after) * lay.inv4
    return (e0, p2, e3, p4), (o0, p2, o3, p4)


def spread(we, wo, lay):
    e1, e2, e3, e4 = we
    o1, o2, o3, o4 = wo
    e3 = e3 * lay.inv_e3
    o3 = o3 * lay.inv_o3
    both = e3 + o3
    p4 = (e4 + o4) * lay.inv4
    p2 = (e2 + o2) * 0.5
    edge = lay.u0 * both + lay.u2 * both
    em = lay.u1 * e3 + lay.odd * p4
    om = em + lay.u2 * both
    e0 = e1 + p2 + edge + lay.u1 * e3 + p4
    o0 = o1 + p2 + edge + lay.u1 * o3 + p4
    op = lay.v * (lay.u1 * o3 + lay.even * p4)
    ep = op + lay.v * lay.u0 * both
    return em, om, e0, o0, ep, op


def before(row):
    return pltpu.roll(row, 1, 1)


def after(row):
    return pltpu.roll(row, row.shape[1] - 1, 1)


def softmax4(s):
    top = jnp.maximum(jnp.maximum(s[0], s[1]), jnp.maximum(s[2], s[3]))
    e = [jnp.exp(x - top) for x in s]
    inv = 1.0 / (e[0] + e[1] + e[2] + e[3])
    return [x * inv for x in e]


def put_rows(rows, total):
    sub = iota((8, total), 0)
    out = jnp.zeros((8, total), f32)
    for k, r in enumerate(rows):
        out = jnp.where(sub == k, jnp.broadcast_to(r, (8, total)), out)
    return out


def get_row(block, k):
    return jnp.sum(jnp.where(iota(block.shape, 0) == k, block, 0.0), axis=0, keepdims=True)


def eye():
    return (iota((BLK, BLK), 0) == iota((BLK, BLK), 1)).astype(f32)


def neighbours(e, o):
    return before(e), before(o), e, o, after(e), after(o)


def param_rows(tab_ref):
    rows = tab_ref[VOCAB - 3 : VOCAB + 13, :].astype(f32)
    return lambda k: rows[k - VOCAB + 3 : k - VOCAB + 4, :]


def id_rows(ids_ref):
    count = ids_ref.shape[0]
    return [jnp.concatenate([ids_ref[d, k : k + 1, :] for d in range(count)], axis=1) for k in range(2)]


def up1(x):
    return pltpu.roll(x, 1, 0)


def down1(x):
    return pltpu.roll(x, WIN - 1, 0)


def conv_window(ee, eo, lanes, row, pv, nx):
    eo_p = up1(eo) * pv
    ee_n = down1(ee) * nx
    eo_n = down1(eo) * nx
    c = [row(TAP_ROW + k)[:, lanes] for k in range(CONV)]
    b = row(SHIFT_ROW)[:, lanes]
    ce = b + c[0] * eo_p + c[1] * ee + c[2] * eo + c[3] * ee_n
    co = b + c[0] * ee + c[1] * eo + c[2] * ee_n + c[3] * eo_n
    return ce, co


def run_copies(copies, sems):
    made = [pltpu.make_async_copy(s, d, sems.at[k]) for k, (s, d) in enumerate(copies)]
    for c in made:
        c.start()
    return made


def split3(x):
    top = x.astype(bf16)
    rest = x - top.astype(f32)
    middle = rest.astype(bf16)
    return top, middle, (rest - middle.astype(f32)).astype(bf16)


def g_kernel(total, pieces, meta, len_ref, pad_ref, ids_ref, *refs):
    n = 2 if pieces else 1
    parts = refs[:n]
    tab_out, hid_out, n1_out, conv_out, rows_out = refs[n : n + 5]
    tab, hot2, ee, eo, idr, ge, go, coef, sems = refs[n + 5 :]
    fs, c = meta[0], meta[3]
    if pieces:
        w = D // 2
        copies = [
            (parts[0], tab.at[pl.ds(0, SROWS), pl.ds(aligned(fs, w), w)]),
            (parts[1], tab.at[pl.ds(0, SROWS), pl.ds(aligned(1 - fs, w), w)]),
        ]
    else:
        copies = [(parts[0], tab.at[pl.ds(0, SROWS), :])]
    made = run_copies(copies, sems)
    tab[SROWS:VP, :] = jnp.zeros((VP - SROWS, D), bf16)
    lay = token_rows(len_ref, pad_ref, fs, total, c * BLK - HALO, total)
    shifted = [jnp.where(c == 0, pltpu.roll(r, HALO, 1), pltpu.roll(r, total - BLK + HALO, 1)) for r in id_rows(ids_ref)]
    id_e = jnp.where(lay.real_e, shifted[0], -1)
    id_o = jnp.where(lay.real_o, shifted[1], -1)
    idr[...] = put_rows([id_e.astype(f32), id_o.astype(f32)], total)
    for m in made:
        m.wait()
    tab_out[...] = tab[...]
    row = param_rows(tab)
    score = row(SCORE_ROW)
    sub = iota((16, D), 0)
    cw = jnp.zeros((16, D), f32)
    for k in range(CONV):
        cw = jnp.where(sub == k, jnp.broadcast_to(row(TAP_ROW + k) * score, (16, D)), cw)
    top, middle, _ = split3(cw)
    g = jnp.concatenate(split3(nt(top, tab[...]) + nt(middle, tab[...])), axis=0)
    shift_score = jnp.sum(row(SHIFT_ROW) * score, axis=1, keepdims=True)
    step = 2 * BLK
    at = iota((VP, step), 0).astype(f32)

    def dots(i, carry):
        lanes = pl.ds(aligned(i, step), step)
        for k, out in ((0, ge), (1, go)):
            x = nn(g, (at == idr[k : k + 1, lanes]).astype(bf16))
            out[:, lanes] = x[0:8] + x[16:24] + x[32:40]
        return carry

    lax.fori_loop(0, total // step, dots, 0)
    qe = [get_row(ge[...], k) for k in range(4)]
    qo = [get_row(go[...], k) for k in range(4)]
    ze = lay.prev * before(qo[0]) + qe[1] + qo[2] + lay.v * after(qe[3]) + shift_score
    zo = qe[0] + qo[1] + lay.v * after(qe[2]) + lay.v * after(qo[3]) + shift_score
    se, so = forms(neighbours(ze, zo), lay)
    we, wo = softmax4(se), softmax4(so)
    em, om, e0, o0, ep, op = [0.5 * x for x in spread(we, wo, lay)]
    coef[...] = put_rows([e0, o0, after(em), after(om), before(ep), before(op), lay.prev, lay.v], total)
    rows_out[0:8, :] = put_rows(list(we) + list(wo), total)
    rows_out[8:16, :] = put_rows([e0, o0, em, om, ep, op], total)
    gain = row(GAIN1_ROW)
    lane = iota((WIN, VP), 1).astype(f32)

    def window(i, carry):
        lanes_at = pl.ds(aligned(i, step), step)
        ids = idr[:, lanes_at].T
        cols = coef[:, lanes_at].T
        hot2[0:WIN, :] = (lane == ids[0:WIN, 0:1]).astype(bf16)
        hot2[WIN : 2 * WIN, :] = (lane == ids[0:WIN, 1:2]).astype(bf16)
        both = nn(hot2[...], tab[...])
        ee[...] = both[0:WIN]
        eo[...] = both[WIN : 2 * WIN]
        col = [jnp.broadcast_to(cols[0:WIN, k : k + 1], (WIN, LANES)) for k in range(8)]
        total_sq = jnp.zeros((WIN, LANES), f32)
        for ch in range(D // LANES):
            lanes = slice(ch * LANES, (ch + 1) * LANES)
            ce, co = conv_window(ee[:, lanes], eo[:, lanes], lanes, row, col[6], col[7])
            conv_out[0, i, :, lanes] = ce.astype(bf16)
            conv_out[1, i, :, lanes] = co.astype(bf16)
            h = col[0] * ce + col[1] * co + up1(col[2] * ce + col[3] * co) + down1(col[4] * ce + col[5] * co)
            low = h.astype(bf16)
            ee[:, lanes] = low.astype(f32)
            total_sq = total_sq + ee[:, lanes] * ee[:, lanes]
        scale = lax.rsqrt(jnp.sum(total_sq, axis=1, keepdims=True) * (1.0 / D) + EPS)
        scale = jnp.broadcast_to(scale, (WIN, LANES))[HALO : HALO + BLK]
        for ch in range(D // LANES):
            lanes = slice(ch * LANES, (ch + 1) * LANES)
            h = ee[HALO : HALO + BLK, lanes]
            hid_out[i, :, lanes] = h.astype(bf16)
            n1_out[i, :, lanes] = (h * scale * gain[:, lanes]).astype(bf16)
        return carry

    lax.fori_loop(0, total // step, window, 0)


def attn_weight_copies(pieces, fs, c, parts, wqkv, wo):
    hl = wo.shape[0]
    if not pieces:
        q, k, v, o = parts
        return [(r, wqkv.at[:, pl.ds(j * hl, hl)]) for j, r in enumerate((q, k, v))] + [(o, wo)]
    q, k, v, o, mine, twin = parts
    w = D // 2
    hw = w // 2
    out = []
    for j, r in enumerate((q, k, v)):
        lanes = pl.ds(j * hl, hl)
        out.append((r, wqkv.at[pl.ds(aligned(fs, w), w), lanes]))
        base = (1 - fs) * w
        out.append((mine.at[j], wqkv.at[pl.ds(pl.multiple_of(base + c * hw, hw), hw), lanes]))
        out.append((twin.at[j], wqkv.at[pl.ds(pl.multiple_of(base + (1 - c) * hw, hw), hw), lanes]))
    other = pl.ds(aligned(1 - fs, w), w)
    out.append((o, wo.at[:, pl.ds(aligned(fs, w), w)]))
    out.append((mine.at[3], wo.at[pl.ds(aligned(c, hw), hw), other]))
    out.append((twin.at[3], wo.at[pl.ds(aligned(1 - c, hw), hw), other]))
    return out


def bias_rows(tab_ref, ext_ref, tp, shards_at):
    block = tab_ref[BIAS_ROW : BIAS_ROW + 16, :]
    ext = ext_ref[...]
    width = NB // len(shards_at)
    sub = iota((LANES, ext.shape[1]), 0)
    out = jnp.zeros((16, ext.shape[1]), f32)
    for j, lane in enumerate(shards_at):
        hot = ((sub < width) & (sub + j * width == ext)).astype(bf16)
        out = out + nn(block[:, lane : lane + LANES], hot)
    return out


def bias_plane(band, left, right, cx, plane, total):
    rolled = pltpu.roll(jnp.broadcast_to(band, (BLK, 512)), 0, 1, stride=1, stride_axis=0)
    at = iota((1, total + 2 * BLK), 1)
    plane[...] = jnp.broadcast_to(jnp.where(at < cx * BLK, left, right), plane.shape)
    plane[:, pl.ds(aligned(cx, BLK), 3 * BLK)] = rolled[:, BLK:]
    return plane[:, BLK : BLK + total]


def attn_masks(len_ref, pad_ref, fs, cx, total):
    lay = token_rows(len_ref, pad_ref, fs, total)
    seg = jnp.where(lay.real_e, lay.seg, -1).astype(f32)
    own = token_rows(len_ref, pad_ref, fs, BLK, cx * BLK)
    col = nt(eye(), put_rows([own.seg.astype(f32), own.real_e.astype(f32)], BLK), precision=HI)
    return jnp.where(col[:, 0:1] == seg, 0.0, NEG), col[:, 1:2]


def a_kernel(total, pieces, shards_at, meta, len_ref, pad_ref, ext_ref, tab_ref, n1_mine, n1_twin, *refs):
    n = 6 if pieces else 4
    parts = refs[:n]
    q_out, k_out, v_out, att_out, lse_out, part_out, n1_out = refs[n : n + 7]
    wqkv, wo, plane, mask, fr, sems = refs[n + 7 :]
    fs, cx, tp, c = meta[0], meta[1], meta[2], meta[3]
    hl = wo.shape[0]
    made = run_copies(attn_weight_copies(pieces, fs, c, parts, wqkv, wo), sems)
    mask[...], _ = attn_masks(len_ref, pad_ref, fs, cx, total)
    fr[...] = bias_rows(tab_ref, ext_ref, tp, shards_at)
    for m in made:
        m.wait()
    q_out[...] = nn(n1_mine[cx >> 1], wqkv[:, 0:hl]).astype(bf16)

    def project(i, carry):
        x = jnp.concatenate([n1_mine[i], n1_twin[i]], axis=0)
        kv = nn(x, wqkv[:, hl : 3 * hl]).astype(bf16)
        for k in range(2):
            rows = pl.ds(aligned(2 * i + (c if k == 0 else 1 - c), BLK), BLK)
            mid = slice(k * BLK, (k + 1) * BLK)
            n1_out[rows, :] = x[mid]
            k_out[rows, :] = kv[mid, 0:hl]
            v_out[rows, :] = kv[mid, hl : 2 * hl]
        return carry

    lax.fori_loop(0, total // (2 * BLK), project, 0)
    lo = iota((1, LANES), 1) < DH
    lane = iota((BLK, LANES), 1)
    lse = jnp.zeros((BLK, LANES), f32)
    for pair in range(hl // LANES):
        lanes = slice(pair * LANES, (pair + 1) * LANES)
        q2, k2, v2 = q_out[:, lanes], k_out[:, lanes], v_out[:, lanes]
        halves = []
        for half in range(2):
            h = 2 * pair + half
            keep = lo if half == 0 else jnp.logical_not(lo)
            qm = jnp.where(keep, q2, jnp.zeros_like(q2)) * bf16(1.0 / math.sqrt(DH))
            band = fr[h : h + 1, :]
            bias = bias_plane(band, band[:, 0:1], band[:, 511:512], cx, plane, total)
            s = nt(qm, k2) + bias + mask[...]
            top = jnp.max(s, axis=1, keepdims=True)
            e = jnp.exp(s - top)
            tot = jnp.sum(e, axis=1, keepdims=True)
            lse = jnp.where(lane == h, top + jnp.log(tot), lse)
            halves.append(nn((e * (1.0 / tot)).astype(bf16), v2))
        att_out[:, lanes] = jnp.where(lo, halves[0], halves[1]).astype(bf16)
    lse_out[...] = lse
    part_out[...] = nn(att_out[...], wo[...]).astype(bf16)


def mlp_weight_copies(pieces, fs, c, parts, wg, wu, wd):
    if not pieces:
        return list(zip(parts, (wg, wu, wd)))
    g, u, d, gu_mine, gu_twin, d_mine, d_twin = parts
    w = D // 2
    hw = w // 2
    hr = wd.shape[0] // 2
    out = []
    for j, (r, dst) in enumerate(((g, wg), (u, wu))):
        base = (1 - fs) * w
        out.append((r, dst.at[pl.ds(aligned(fs, w), w), :]))
        out.append((gu_mine.at[j], dst.at[pl.ds(pl.multiple_of(base + c * hw, hw), hw), :]))
        out.append((gu_twin.at[j], dst.at[pl.ds(pl.multiple_of(base + (1 - c) * hw, hw), hw), :]))
    other = pl.ds(aligned(1 - fs, w), w)
    out.append((d, wd.at[:, pl.ds(aligned(fs, w), w)]))
    out.append((d_mine, wd.at[pl.ds(aligned(c, hr), hr), other]))
    out.append((d_twin, wd.at[pl.ds(aligned(1 - c, hr), hr), other]))
    return out


def tanh_parts(x):
    k = math.sqrt(2.0 / math.pi)
    th = jnp.tanh(k * (x + 0.044715 * x * x * x))
    return th, k


def b_kernel(pieces, meta, tab_ref, hid_ref, mine_ref, other_ref, *refs):
    n = 7 if pieces else 3
    parts = refs[:n]
    res_out, act_out, gate_out, up_out, part_out = refs[n : n + 5]
    wg, wu, wd, sems = refs[n + 5 :]
    ffl = wg.shape[1]
    fs, cx, c = meta[0], meta[1], meta[3]
    made = run_copies(mlp_weight_copies(pieces, fs, c, parts, wg, wu, wd), sems)
    gain = param_rows(tab_ref)(GAIN2_ROW)
    res = hid_ref[cx >> 1].astype(f32) + (mine_ref[...].astype(f32) + other_ref[...].astype(f32))
    res_out[...] = res
    scale = lax.rsqrt(jnp.sum(res * res, axis=1, keepdims=True) * (1.0 / D) + EPS)
    n2 = (res * scale * gain).astype(bf16)
    act_out[:, 0:D] = n2
    for m in made:
        m.wait()
    gate = nn(n2, wg[...])
    up = nn(n2, wu[...])
    gate_out[...] = gate
    up_out[...] = up
    th, _ = tanh_parts(gate)
    gated = (0.5 * gate * (1.0 + th) * up).astype(bf16)
    act_out[:, D : D + ffl] = gated
    part_out[...] = nn(gated, wd[...]).astype(bf16)


def c_kernel(pieces, meta, len_ref, pad_ref, deal_ref, teach_ref, res_ref, mine_ref, other_ref, gate_ref, up_ref, *refs):
    n = 7 if pieces else 3
    parts = refs[:n]
    out_ref, loss_out, gres_out, act_out, part_out = refs[n : n + 5]
    wg, wu, wd, teacher, sems = refs[n + 5 :]
    ffl = wg.shape[1]
    fs, cx, tp, c = meta[0], meta[1], meta[2], meta[3]
    made = run_copies(mlp_weight_copies(pieces, fs, c, parts, wg, wu, wd), sems)
    slots, unit = teach_ref.shape[0], teach_ref.shape[1]
    for s in range(slots):
        teacher[s * unit : (s + 1) * unit, :] = teach_ref[deal_ref[fs, cx, s]].astype(f32)
    count = jnp.int32(0)
    for f in range(len_ref.shape[0]):
        for k in range(len_ref.shape[1]):
            count = count + ((2 * len_ref[f, k] - pad_ref[f, k] + 1) >> 1)
    real_count = jnp.broadcast_to(count, (1, LANES)).astype(f32)[:, 0:1]
    own = token_rows(len_ref, pad_ref, fs, BLK, cx * BLK)
    valid = nt(eye(), put_rows([own.real_e.astype(f32)], BLK), precision=HI)[:, 0:1]
    result = res_ref[...] + (mine_ref[...].astype(f32) + other_ref[...].astype(f32))
    width = out_ref.shape[1]
    out_ref[...] = jnp.where(tp == 0, result[:, 0:width], result[:, D - width : D]).astype(bf16)
    diff = (result - teacher[...]) * valid
    square = jnp.sum(jnp.sum(diff * diff, axis=1, keepdims=True), axis=0, keepdims=True)
    loss_out[...] = jnp.broadcast_to(square / (2.0 * D * real_count), (8, LANES))
    gres = diff * (GRAD_SCALE / (D * real_count))
    gres_out[...] = gres
    low = gres.astype(bf16)
    act_out[:, 0:D] = low
    for m in made:
        m.wait()
    ggated = nt(low, wd[...])
    gate = gate_ref[...]
    up = up_ref[...]
    th, k = tanh_parts(gate)
    value = 0.5 * gate * (1.0 + th)
    slope = 0.5 * (1.0 + th) + 0.5 * gate * (1.0 - th * th) * (k * (1.0 + 3.0 * 0.044715 * gate * gate))
    gg = (ggated * up * slope).astype(bf16)
    gu = (ggated * value).astype(bf16)
    act_out[:, D : D + ffl] = gg
    act_out[:, D + ffl : D + 2 * ffl] = gu
    part_out[...] = (nt(gg, wg[...]) + nt(gu, wu[...])).astype(bf16)


def m_kernel(split, ffl, meta, *refs):
    if not split:
        act1, act2, gu_out, down_out = refs
        n2, gated = act1[:, 0:D], act1[:, D : D + ffl]
        gu_out[0] = tn(n2, act2[:, D : D + ffl]).astype(bf16)
        gu_out[1] = tn(n2, act2[:, D + ffl : D + 2 * ffl]).astype(bf16)
        down_out[...] = tn(gated, act2[:, 0:D]).astype(bf16)
        return
    act1, act1_t, act2, act2_t, gu_own, gu_oth, d_own, d_oth, wide, tall = refs
    fs, c = meta[0], meta[3]
    w = D // 2
    half = ffl // 2

    def both(mine, twin, first):
        lanes = pl.ds(pl.multiple_of(first + c * half, LANES), half)
        return jnp.concatenate([mine[:, lanes], twin[:, lanes]], axis=0)

    n2 = jnp.concatenate([act1[:, 0:D], act1_t[:, 0:D]], axis=0)
    low = jnp.concatenate([act2[:, 0:D], act2_t[:, 0:D]], axis=0)
    mine, other = pl.ds(aligned(fs, w), w), pl.ds(aligned(1 - fs, w), w)
    for j in range(2):
        wide[...] = tn(n2, both(act2, act2_t, D + j * ffl)).astype(bf16)
        gu_own[j] = wide[mine, :]
        gu_oth[j] = wide[other, :]
    tall[...] = tn(both(act1, act1_t, D), low).astype(bf16)
    d_own[...] = tall[:, mine]
    d_oth[...] = tall[:, other]


def d_kernel(total, pieces, shards_at, tps, meta, len_ref, pad_ref, ext_ref, ext1_ref, tab_ref, n1_ref, q_ref, k_ref, v_ref, att_ref, lse_ref, res_ref, gres_ref, hid_mine, hid_twin, mine_ref, other_ref, *refs):
    n = 6 if pieces else 4
    parts = refs[:n]
    m = 2
    packs = refs[n : n + m]
    keep_out, send_out, extra_out = refs[n + m : n + m + 3]
    wqkv, wo, plane, mask, fr, dsw, stack, ga, dq, dkv, wide, wo_grad, dh, sems = refs[n + m + 3 :]
    fs, cx, tp, c = meta[0], meta[1], meta[2], meta[3]
    hl = wo.shape[0]
    made = run_copies(attn_weight_copies(pieces, fs, c, parts, wqkv, wo), sems)
    mask[...], _ = attn_masks(len_ref, pad_ref, fs, cx, total)
    fr[...] = bias_rows(tab_ref, ext_ref, tp, shards_at)
    gain = param_rows(tab_ref)(GAIN2_ROW)
    gn2 = mine_ref[...].astype(f32) + other_ref[...].astype(f32)
    res = res_ref[...]
    r2 = lax.rsqrt(jnp.sum(res * res, axis=1, keepdims=True) * (1.0 / D) + EPS)
    u = gain * gn2
    gain_grad = jnp.sum(gn2 * res * r2, axis=0, keepdims=True) * (1.0 / tps)
    back = gres_ref[...] + r2 * u - res * (r2 * r2 * r2 * (jnp.sum(u * res, axis=1, keepdims=True) * (1.0 / D)))
    branch = back.astype(bf16)
    for x in made:
        x.wait()
    wo_grad[...] = tn(att_ref[...], branch).astype(bf16)
    ga[...] = nt(branch, wo[...]).astype(bf16)
    lo = iota((1, LANES), 1) < DH
    at = iota((1, total), 1)
    first = cx * BLK - BLK
    rev = (iota((BLK, BLK), 0) + iota((BLK, BLK), 1) == BLK - 1).astype(bf16)
    band_at = iota((1, 512), 1)
    scale = bf16(1.0 / math.sqrt(DH))
    sums = []
    for pair in range(hl // LANES):
        lanes = slice(pair * LANES, (pair + 1) * LANES)
        q2, k2, v2, g2 = q_ref[:, lanes], k_ref[:, lanes], v_ref[:, lanes], ga[:, lanes]
        zero = jnp.zeros_like(q2)
        qs, gs, dqs = [], [], []
        for half in range(2):
            h = 2 * pair + half
            keep = lo if half == 0 else jnp.logical_not(lo)
            qm = jnp.where(keep, q2, zero) * scale
            gm = jnp.where(keep, g2, zero)
            band = fr[h : h + 1, :]
            bias = bias_plane(band, band[:, 0:1], band[:, 511:512], cx, plane, total)
            s = nt(qm, k2) + bias + mask[...]
            p = jnp.exp(s - lse_ref[:, h : h + 1])
            g = nt(gm, v2)
            inner = jnp.sum(p * g, axis=1, keepdims=True)
            ds = p * (g - inner)
            low = ds.astype(bf16)
            stack[0, half * BLK : (half + 1) * BLK, :] = low
            stack[1, half * BLK : (half + 1) * BLK, :] = p.astype(bf16)
            wide_ds = low.astype(f32)
            col = jnp.sum(wide_ds, axis=0, keepdims=True)
            left = jnp.sum(jnp.where(at < first, col, 0.0), axis=1, keepdims=True)
            right = jnp.sum(jnp.where(at >= first + 3 * BLK, col, 0.0), axis=1, keepdims=True)
            dsw[:, BLK : BLK + total] = wide_ds
            if pair == 0 and half == 0:
                dsw[:, 0:BLK] = jnp.zeros((BLK, BLK), f32)
                dsw[:, BLK + total :] = jnp.zeros((BLK, 2 * BLK), f32)
            window = dsw[:, pl.ds(aligned(cx, BLK), 512)]
            window = jnp.where(band_at < 3 * BLK, window, 0.0).astype(bf16)
            turned = pltpu.roll(nn(rev, window), 0, 1, stride=1, stride_axis=0)
            diag = jnp.sum(turned, axis=0, keepdims=True)
            diag = diag + jnp.where(band_at == 0, left, 0.0) + jnp.where(band_at == 510, right, 0.0)
            sums.append(diag)
            dqs.append(nn(low, k2))
            qs.append(qm)
            gs.append(gm)
        dq[:, lanes] = (jnp.where(lo, dqs[0], dqs[1]) * (1.0 / math.sqrt(DH))).astype(bf16)
        dkv[:, lanes] = tn(stack[0], jnp.concatenate(qs, axis=0)).astype(bf16)
        dkv[:, hl + pair * LANES : hl + (pair + 1) * LANES] = tn(stack[1], jnp.concatenate(gs, axis=0)).astype(bf16)
    own = pl.ds(aligned(cx, BLK), BLK)
    wide[0] = tn(n1_ref[own, :], dq[...]).astype(bf16)
    both = tn(n1_ref[...], dkv[...])
    wide[1] = both[:, 0:hl].astype(bf16)
    wide[2] = both[:, hl : 2 * hl].astype(bf16)
    if pieces:
        w, hw = D // 2, D // 4
        for half, ref in enumerate(packs):
            cc = c if half == 0 else 1 - c
            for rel in range(2):
                f = fs if rel == 0 else 1 - fs
                for j in range(3):
                    ref[rel, j] = wide[j, pl.ds(pl.multiple_of(f * w + cc * hw, hw), hw), :]
                ref[rel, 3] = wo_grad[pl.ds(aligned(cc, hw), hw), pl.ds(aligned(f, w), w)]
    else:
        packs[0][...] = wide[...]
        packs[1][...] = wo_grad[...]
    own_grad = nt(dq[...], wqkv[:, 0:hl])
    gain1 = param_rows(tab_ref)(GAIN1_ROW)
    dh[0:HALO, :] = jnp.zeros((HALO, D), f32)
    dh[total + HALO : total + 2 * HALO, :] = jnp.zeros((HALO, D), f32)

    def norm_back(h, grad):
        r = lax.rsqrt(jnp.sum(h * h, axis=1, keepdims=True) * (1.0 / D) + EPS)
        u = gain1 * grad
        d = r * u - h * (r * r * r * (jnp.sum(u * h, axis=1, keepdims=True) * (1.0 / D)))
        return d, jnp.sum(grad * h * r, axis=0, keepdims=True)

    def back_rows(i, carry):
        for k, hid in enumerate((hid_mine, hid_twin)):
            b = 2 * i + (c if k == 0 else 1 - c)
            grad = nt(dkv[pl.ds(aligned(b, BLK), BLK), :], wqkv[:, hl : 3 * hl])
            d, g = norm_back(hid[i].astype(f32), grad)
            dh[pl.ds(pl.multiple_of(b * BLK + HALO, HALO), BLK), :] = d
            carry = carry + g
        return carry

    gain1_grad = lax.fori_loop(0, total // (2 * BLK), back_rows, jnp.zeros((1, D), f32))
    d, g = norm_back(hid_mine[cx >> 1].astype(f32), own_grad)
    gain1_grad = gain1_grad + g
    here = pl.ds(pl.multiple_of(cx * BLK + HALO, HALO), BLK)
    dh[here, :] = dh[here, :] + (d + back * (1.0 / tps))

    def windows(i, carry):
        for k, out in enumerate((keep_out, send_out)):
            b = 2 * i + (c if k == 0 else 1 - c)
            out[i] = dh[pl.ds(aligned(b, BLK), WIN), :].astype(bf16)
        return carry

    lax.fori_loop(0, total // (2 * BLK), windows, 0)
    rows = put_rows(sums, 512)
    ext = ext1_ref[...]
    width = NB // len(shards_at)
    sub = iota((LANES, 512), 0)
    extra_out[...] = jnp.zeros(extra_out.shape, f32)
    for j, lane in enumerate(shards_at):
        hot = ((sub < width) & (sub + j * width == ext)).astype(f32)
        extra_out[pl.ds(aligned(tp, 8), 8), lane : lane + LANES] = nt(rows, hot, precision=HI)
    extra_out[16:24, :] = put_rows([gain1_grad, gain_grad], D)


def e_kernel(total, split, spots, meta, len_ref, pad_ref, ids_ref, tab_ref, conv_ref, rows_ref, keep_ref, recv_ref, extra_ref, loss_ref, *refs):
    n = 2 if split else 1
    outs = refs[:n]
    xr, dz, idr, dh, dc, hots, wide = refs[n:]
    fs, cx, c = meta[0], meta[1], meta[3]
    windows = total // (2 * BLK)
    step = 2 * BLK
    lay = token_rows(len_ref, pad_ref, fs, total, c * BLK - HALO, total)
    xr[...] = jnp.zeros(xr.shape, f32)
    s_at, t_at = iota((WIN, WIN), 0), iota((WIN, WIN), 1)

    def inner(i, carry):
        d = (keep_ref[i].astype(f32) + recv_ref[i].astype(f32)).astype(bf16)
        dh[i] = d
        for k in range(2):
            gram = nt(conv_ref[k, i], d)
            for j in range(3):
                part = jnp.sum(jnp.where(s_at == t_at + (j - 1), gram, 0.0), axis=0, keepdims=True)
                xr[2 * j + k, 0:1, pl.ds(aligned(i, step), WIN)] = part
        return carry

    lax.fori_loop(0, windows, inner, 0)
    x = [0.5 * xr[k, 0:1, :] for k in range(6)]
    pe, po = forms(x, lay)
    we = [get_row(rows_ref[0:8, :], k) for k in range(4)]
    wo = [get_row(rows_ref[0:8, :], k + 4) for k in range(4)]

    def soft_back(w, p):
        mean = w[0] * p[0] + w[1] * p[1] + w[2] * p[2] + w[3] * p[3]
        return [a * (b - mean) for a, b in zip(w, p)]

    em, om, e0, o0, ep, op = spread(soft_back(we, pe), soft_back(wo, po), lay)
    dze = e0 + after(em) + before(ep)
    dzo = o0 + after(om) + before(op)
    dz[...] = put_rows([dze, dzo], total)
    score = jnp.broadcast_to(tab_ref[SCORE_ROW : SCORE_ROW + 1, :], (WIN, D))
    sub16 = iota((16, WIN), 0)
    at16 = iota((16, WIN), 1)
    own16 = (at16 >= HALO) & (at16 < HALO + BLK)

    def stencil(i, carry):
        lanes = pl.ds(aligned(i, step), WIN)
        d = dh[i]
        for k in range(2):
            z = dz[k : k + 1, lanes]
            mid = rows_ref[8 + k : 9 + k, lanes]
            prv = rows_ref[10 + k : 11 + k, lanes]
            nxt = rows_ref[12 + k : 13 + k, lanes]
            band = jnp.where(t_at == s_at, mid, 0.0)
            band = jnp.where(t_at == s_at + 1, prv, band)
            band = jnp.where(t_at == s_at - 1, nxt, band)
            grad = nn(band.astype(bf16), d) + nn(jnp.where(t_at == s_at, z, 0.0).astype(bf16), score)
            dc[k, pl.ds(aligned(i, BLK), BLK), :] = grad[HALO : HALO + BLK].astype(bf16)
            top = z.astype(bf16).astype(f32)
            pair = jnp.where(sub16 == 0, top, jnp.where(sub16 == 1, z - top, 0.0))
            carry = carry + nn(jnp.where(own16, pair, 0.0).astype(bf16), conv_ref[k, i])
        return carry

    score_rows = lax.fori_loop(0, windows, stencil, jnp.zeros((16, D), f32))
    score_grad = jnp.sum(score_rows, axis=0, keepdims=True)
    whole = token_rows(len_ref, pad_ref, fs, total)
    raw = id_rows(ids_ref)
    id_e = jnp.where(whole.real_e, raw[0], -1).astype(f32)
    id_o = jnp.where(whole.real_o, raw[1], -1).astype(f32)
    later = whole.v > 0.0
    idr[...] = put_rows(
        [
            jnp.where(whole.prev > 0.0, before(id_o), -1.0),
            id_e,
            id_o,
            jnp.where(later, after(id_e), -1.0),
            jnp.where(later, after(id_o), -1.0),
        ],
        total,
    )
    v_at = iota((SROWS, BLK), 0)
    symbol = v_at.astype(f32)

    def spell(i, carry):
        lanes = pl.ds(aligned(2 * i + c, BLK), BLK)
        for k in range(5):
            hot = symbol == idr[k : k + 1, lanes]
            if k == 1:
                hot = hot | (v_at == SROWS - 1)
            hots[k * SROWS : (k + 1) * SROWS, pl.ds(aligned(i, BLK), BLK)] = hot.astype(f32).astype(bf16)
        return carry

    lax.fori_loop(0, windows, spell, 0)
    wide[...] = jnp.zeros(wide.shape, f32)
    table_rows = VOCAB + 5
    taps = tab_ref[TAP_ROW - 3 : TAP_ROW + 13, :].astype(f32)[3 : 3 + CONV]
    table = tab_ref[0:table_rows, :].astype(f32)
    shift_grad = jnp.zeros((1, D), f32)
    for j in range(CONV):
        acc = nn(hots[j * SROWS : (j + 1) * SROWS, :], dc[0]) + nn(hots[(j + 1) * SROWS : (j + 2) * SROWS, :], dc[1])
        wide[0:table_rows, :] += taps[j : j + 1] * acc[0:table_rows]
        tap_grad = jnp.sum(table * acc[0:table_rows], axis=0, keepdims=True)
        shift_grad = shift_grad + acc[SROWS - 1 : SROWS, :]
        wide[SROWS + j : SROWS + j + 1, :] = tap_grad
    for j in range(CONV):
        wide[TAP_ROW + j : TAP_ROW + j + 1, :] = wide[SROWS + j : SROWS + j + 1, :]
    wide[SHIFT_ROW : SHIFT_ROW + 1, :] = shift_grad
    wide[SCORE_ROW : SCORE_ROW + 1, :] = score_grad
    wide[GAIN1_ROW : GAIN1_ROW + 1, :] = extra_ref[16:17, :]
    wide[GAIN2_ROW : GAIN2_ROW + 1, :] = extra_ref[17:18, :]
    wide[BIAS_ROW : BIAS_ROW + 16, :] = extra_ref[0:16, :]
    part = loss_ref[0:1, :]
    top = part.astype(bf16).astype(f32)
    rest = part - top
    middle = rest.astype(bf16).astype(f32)
    at = iota((1, LANES), 1) - 4 * (fs * spots + cx)
    coded = jnp.where(at == 0, top, jnp.where(at == 1, middle, jnp.where(at == 2, rest - middle, 0.0)))
    coded = jnp.where(meta[2] == 0, coded, 0.0)
    for lane in (0, D // 2):
        wide[LOSS_ROW : LOSS_ROW + 1, lane : lane + LANES] = coded
    if not split:
        outs[0][...] = wide[0:SROWS, :].astype(bf16)
        return
    w = D // 2
    hr = SROWS // 2
    for half, ref in enumerate(outs):
        cc = c if half == 0 else 1 - c
        for rel in range(2):
            f = fs if rel == 0 else 1 - fs
            ref[rel] = wide[pl.ds(pl.multiple_of(cc * hr, 8), hr), pl.ds(aligned(f, w), w)].astype(bf16)


def f_mlp_kernel(meta, gu, gu_o, gu_t, gu_ot, d, d_o, d_t, d_ot, g_out, u_out, d_out):
    c, odd = meta[3], (meta[1] >> 1) & 1
    half = d.shape[0] * 2
    mine, other = pl.ds(aligned(c, half), half), pl.ds(aligned(1 - c, half), half)
    first = odd == 0
    for lanes, a, b in ((mine, gu, gu_o), (other, gu_t, gu_ot)):
        a, b = a[...].astype(f32), b[...].astype(f32)
        g_out[:, lanes] = jnp.where(first, a, b)
        u_out[:, lanes] = jnp.where(first, b, a)
    q = d.shape[0]
    for at, a, b in ((c, d, d_o), (1 - c, d_t, d_ot)):
        d_out[pl.ds(aligned(2 * at + odd, q), q), :] = a[...].astype(f32)
        d_out[pl.ds(aligned(2 * at + 1 - odd, q), q), :] = b[...].astype(f32)


def f_attn_kernel(meta, x, x_o, x_t, x_ot, *outs):
    c, odd = meta[3], (meta[1] >> 1) & 1
    hw = x.shape[1]
    first = odd == 0
    for rows, a, b in ((pl.ds(aligned(c, hw), hw), x, x_o), (pl.ds(aligned(1 - c, hw), hw), x_t, x_ot)):
        for j in range(2):
            p, q = a[j].astype(f32), b[j].astype(f32)
            outs[j][rows, :] = jnp.where(first, p, q)
            outs[2 + j][rows, :] = jnp.where(first, q, p)


def f_small_kernel(meta, x, x_t, loss, table, taps, shift, score, gain1, gain2, bias, whole):
    tp, c = meta[2], meta[3]
    hr = x.shape[0]
    whole[pl.ds(aligned(c, hr), hr), :] = x[...].astype(f32)
    whole[pl.ds(aligned(1 - c, hr), hr), :] = x_t[...].astype(f32)
    loss[0, 0] = jnp.sum(whole[LOSS_ROW : LOSS_ROW + 1, 0:LANES])
    table[...] = whole[0:VOCAB, :]
    taps[...] = whole[TAP_ROW : TAP_ROW + CONV, :]
    for k, out in ((SHIFT_ROW, shift), (SCORE_ROW, score), (GAIN1_ROW, gain1), (GAIN2_ROW, gain2)):
        out[...] = whole[k : k + 1, :].reshape(out.shape)
    rows = whole[pl.ds(pl.multiple_of(BIAS_ROW + 8 * tp, 8), 8), 0:LANES]
    bias[...] = rows[0 : bias.shape[0], 0 : bias.shape[1]]


def p_kernel(emb, taps, shift, score, gain1, gain2, bias, out, wide):
    wide[...] = jnp.zeros(wide.shape, f32)
    wide[0:VOCAB, :] = emb[...].astype(f32)
    wide[TAP_ROW : TAP_ROW + CONV, :] = taps[...].astype(f32)
    for k, ref in ((SHIFT_ROW, shift), (SCORE_ROW, score), (GAIN1_ROW, gain1), (GAIN2_ROW, gain2)):
        wide[k : k + 1, :] = ref[...].astype(f32).reshape(1, ref.shape[0])
    m, n = bias.shape
    wide[BIAS_ROW : BIAS_ROW + m, 0:n] = bias[...].astype(f32)
    out[...] = wide[...].astype(bf16)


def sds(shape, dtype):
    return jax.ShapeDtypeStruct(shape, dtype)


def call(kernel, name, us, ins, in_specs, out_shape, scratch, out_specs=None):
    return pl.pallas_call(
        kernel,
        name=name,
        cost_estimate=pl.CostEstimate(flops=0, transcendentals=0, bytes_accessed=int(us * 3.69e6)),
        out_shape=out_shape,
        in_specs=in_specs,
        out_specs=out_specs or jax.tree.map(lambda _: VM, out_shape),
        scratch_shapes=scratch,
        compiler_params=pltpu.CompilerParams(vmem_limit_bytes=60 << 20),
    )(*ins)


def once(x, *others):
    return lax.optimization_barrier((x, *others))[0]


def add2(a, b):
    return (a.astype(f32) + b.astype(f32)).astype(bf16)


def shards(
    byte_ids,
    seq_tokens,
    pad_bytes,
    deal_targets,
    rel_buckets,
    embedding,
    conv_weight,
    conv_bias,
    score_weight,
    attn_gain,
    query_weight,
    key_weight,
    value_weight,
    rel_bias,
    out_weight,
    mlp_gain,
    gate_weight,
    up_weight,
    down_weight,
    teacher,
):
    fs = lax.axis_index("fsdp")
    cx = lax.axis_index("ctx")
    tp = lax.axis_index("tp")
    fcount, ccount, tps = lax.axis_size("fsdp"), lax.axis_size("ctx"), lax.axis_size("tp")
    core = cx % 2
    total = teacher.shape[0] * ccount
    unit = teacher.shape[0] // ccount
    hl = query_weight.shape[1]
    heads = hl // DH
    ffl = gate_weight.shape[1]
    split = fcount == 2
    wloc = D // fcount
    bloc = NB // fcount
    meta = jnp.stack([fs, cx, tp, core]).astype(i32)

    def twin(x):
        return lax.ppermute(x, "ctx", [(i, i ^ 1) for i in range(ccount)])

    def across(x):
        return lax.ppermute(x, "fsdp", [(0, 1), (1, 0)])

    def tp_other(x):
        return lax.ppermute(x, "tp", [(i, tps - 1 - i) for i in range(tps)])

    def core_half(x, axis):
        n = x.shape[axis] // 2
        return lax.dynamic_slice_in_dim(x, core * n, n, axis)

    ends = lambda k: jnp.broadcast_to(rel_buckets[k : k + 1], (RMAX,))
    ext = jnp.concatenate([ends(0), rel_buckets, ends(2 * RMAX)])
    ext, ext1 = ext[None, :512], ext[None, 1:513]

    def exchange(x):
        return lax.all_to_all(x, "ctx", split_axis=0, concat_axis=0, tiled=True)

    small_ins = (embedding, conv_weight, conv_bias, score_weight, attn_gain, mlp_gain, rel_bias.T)
    small = call(p_kernel, "p", 1, small_ins, [VM] * 7, sds((SROWS, wloc), bf16), [pltpu.VMEM((SROWS, wloc), f32)])
    ids = exchange(jnp.broadcast_to(byte_ids.reshape(-1, 2).T[None], (ccount, 2, byte_ids.shape[0] // 2)))
    if split:
        small_other = across(small)
        small_parts = (small, small_other)
        attn = core_half(jnp.stack([query_weight, key_weight, value_weight, out_weight]), 1)
        mine = across(once(attn, small_other, ids))
        d_mine = across(once(core_half(down_weight, 0), small_other, ids))
    else:
        gather = lambda x, axis: lax.all_gather(x, "fsdp", axis=axis, tiled=True)
        full = gather(small, 1)
        bias_all = jnp.pad(gather(rel_bias, 0).T, ((0, 16 - heads), (0, D - NB)))
        small_parts = (jnp.concatenate([full[:BIAS_ROW], bias_all], axis=0),)
        attn_parts = (gather(query_weight, 0), gather(key_weight, 0), gather(value_weight, 0), gather(out_weight, 1))
        mlp_parts = (gather(gate_weight, 0), gather(up_weight, 0), gather(down_weight, 1))
    shards_at = (0, wloc) if split else (0,)
    teach = exchange(once(teacher.reshape(ccount, unit, D), ids))

    nw = total // (2 * BLK)
    tab, hid, n1, conv, rows = call(
        functools.partial(g_kernel, total, split),
        "g",
        8,
        (meta, seq_tokens, pad_bytes, ids) + small_parts,
        [SM, SM, SM, VM] + [ANY] * len(small_parts),
        (
            sds((VP, D), bf16),
            sds((nw, BLK, D), bf16),
            sds((nw, BLK, D), bf16),
            sds((2, nw, WIN, D), bf16),
            sds((16, total), f32),
        ),
        [
            pltpu.VMEM((VP, D), bf16),
            pltpu.VMEM((2 * WIN, VP), bf16),
            pltpu.VMEM((WIN, D), f32),
            pltpu.VMEM((WIN, D), f32),
            pltpu.VMEM((8, total), f32),
            pltpu.VMEM((8, total), f32),
            pltpu.VMEM((8, total), f32),
            pltpu.VMEM((8, total), f32),
            pltpu.SemaphoreType.DMA((2,)),
        ],
    )
    if split:
        n1_twin, hid_twin = twin(once(n1, mine, d_mine, teach)), twin(once(hid, mine))
        attn_parts = (query_weight, key_weight, value_weight, out_weight, mine, twin(mine))
        gu_mine = across(once(core_half(jnp.stack([gate_weight, up_weight]), 1), mine))
    else:
        n1_twin, hid_twin = twin(n1), twin(hid)
    na = len(attn_parts)
    attn_scratch = [
        pltpu.VMEM((D, 3 * hl), bf16),
        pltpu.VMEM((hl, D), bf16),
        pltpu.VMEM((BLK, total + 2 * BLK), f32),
        pltpu.VMEM((BLK, total), f32),
        pltpu.VMEM((16, 512), f32),
    ]
    q, k, v, att, lse, part, n1_full = call(
        functools.partial(a_kernel, total, split, shards_at),
        "a",
        10,
        (meta, seq_tokens, pad_bytes, ext, tab, n1, n1_twin) + attn_parts,
        [SM, SM, SM, VM, VM, VM, VM] + [ANY] * na,
        (
            sds((BLK, hl), bf16),
            sds((total, hl), bf16),
            sds((total, hl), bf16),
            sds((BLK, hl), bf16),
            sds((BLK, LANES), f32),
            sds((BLK, D), bf16),
            sds((total, D), bf16),
        ),
        attn_scratch + [pltpu.SemaphoreType.DMA((12,))],
    )
    part_other = tp_other(part)
    if split:
        gu_mine = once(gu_mine, part_other)
        d_mine = once(d_mine, part)
        mlp_parts = (gate_weight, up_weight, down_weight, gu_mine, twin(gu_mine), d_mine, twin(d_mine))
    nm = len(mlp_parts)
    mlp_scratch = [pltpu.VMEM((D, ffl), bf16), pltpu.VMEM((D, ffl), bf16), pltpu.VMEM((ffl, D), bf16)]
    res, act1, gate, up, part2 = call(
        functools.partial(b_kernel, split),
        "b",
        6,
        (meta, tab, hid, part, part_other) + mlp_parts,
        [SM, VM, VM, VM, VM] + [ANY] * nm,
        (
            sds((BLK, D), f32),
            sds((BLK, D + ffl), bf16),
            sds((BLK, ffl), f32),
            sds((BLK, ffl), f32),
            sds((BLK, D), bf16),
        ),
        mlp_scratch + [pltpu.SemaphoreType.DMA((9,))],
    )
    part2_other = tp_other(part2)
    if split:
        act1_t = twin(act1)
        part2_other = once(part2_other, act1_t)
    output, loss, gres, act2, part3 = call(
        functools.partial(c_kernel, split),
        "c",
        7,
        (meta, seq_tokens, pad_bytes, deal_targets, teach, res, part2, part2_other, gate, up) + mlp_parts,
        [SM, SM, SM, SM, VM, VM, VM, VM, VM, VM] + [ANY] * nm,
        (
            sds((BLK, D // tps), bf16),
            sds((8, LANES), f32),
            sds((BLK, D), f32),
            sds((BLK, D + 2 * ffl), bf16),
            sds((BLK, D), bf16),
        ),
        mlp_scratch + [pltpu.VMEM((BLK, D), f32), pltpu.SemaphoreType.DMA((9,))],
    )
    part3_other = tp_other(part3)
    quarter = D // 4
    half = ffl // 2
    if split:
        mlp_ins = (act1, act1_t, act2, twin(act2))
        mlp_shape = (sds((2, wloc, half), bf16),) * 2 + (sds((half, wloc), bf16),) * 2
        mlp_tmp = [pltpu.VMEM((D, half), bf16), pltpu.VMEM((half, D), bf16)]
    else:
        mlp_ins = (act1, act2)
        mlp_shape = (sds((2, D, ffl), bf16), sds((ffl, D), bf16))
        mlp_tmp = []
    mlp_pack = call(
        functools.partial(m_kernel, split, ffl), "m", 4, (meta,) + mlp_ins, [SM] + [VM] * len(mlp_ins), mlp_shape, mlp_tmp
    )
    if split:
        part3_other, *mlp_pack = lax.optimization_barrier((part3_other, *mlp_pack))
        gu_own, gu_oth, d_own, d_oth = mlp_pack
        gu_near, d_near = across(gu_oth), across(d_oth)
    attn_shape = (sds((2, 4, quarter, hl), bf16),) * 2 if split else (sds((3, D, hl), bf16), sds((hl, D), bf16))
    *attn_pack, dh_keep, dh_send, extra = call(
        functools.partial(d_kernel, total, split, shards_at, tps),
        "d",
        15,
        (meta, seq_tokens, pad_bytes, ext, ext1, tab, n1_full, q, k, v, att, lse, res, gres, hid, hid_twin, part3, part3_other) + attn_parts,
        [SM, SM, SM] + [VM] * 15 + [ANY] * na,
        attn_shape + (sds((nw, WIN, D), bf16),) * 2 + (sds((24, D), f32),),
        attn_scratch
        + [
            pltpu.VMEM((BLK, total + 3 * BLK), f32),
            pltpu.VMEM((2, 2 * BLK, total), bf16),
            pltpu.VMEM((BLK, hl), bf16),
            pltpu.VMEM((BLK, hl), bf16),
            pltpu.VMEM((total, 2 * hl), bf16),
            pltpu.VMEM((3, D, hl), bf16),
            pltpu.VMEM((hl, D), bf16),
            pltpu.VMEM((total + 2 * HALO, D), f32),
            pltpu.SemaphoreType.DMA((12,)),
        ],
    )
    if split:
        dh_send, attn_send = once(dh_send, gu_near, d_near), once(attn_pack[1], gu_near, d_near)
    def ctx_perm(x, bit):
        return lax.ppermute(x, "ctx", [(i, i ^ bit) for i in range(ccount)])

    odd = (cx // 2) % 2

    def add_halves(own, near):
        n = own.shape[0] // 2
        part = lambda x, k: lax.dynamic_slice_in_dim(x, k * n, n, 0)
        return tuple(add2(part(own, k), part(near, k)) for k in (odd, 1 - odd))

    dh_recv = twin(dh_send)
    if split:
        gu_keep, gu_send = add_halves(gu_own, gu_near)
        gu_got = ctx_perm(gu_send, 2)
        attn_own = add2(attn_pack[0], twin(attn_send))
        d_keep, d_send = add_halves(d_own, once(d_near, gu_send))
        d_got = ctx_perm(d_send, 2)
        attn_near = across(attn_own[1])
        dh_recv = once(dh_recv, attn_own, d_send)
    small_shape = (sds((2, SROWS // 2, wloc), bf16),) * 2 if split else (sds((SROWS, D), bf16),)
    small_pack = call(
        functools.partial(e_kernel, total, split, ccount),
        "e",
        9,
        (meta, seq_tokens, pad_bytes, ids, tab, conv, rows, dh_keep, dh_recv, extra, loss),
        [SM, SM, SM] + [VM] * 8,
        small_shape,
        [
            pltpu.VMEM((6, 8, total), f32),
            pltpu.VMEM((8, total), f32),
            pltpu.VMEM((8, total), f32),
            pltpu.VMEM((nw, WIN, D), bf16),
            pltpu.VMEM((2, total // 2, D), bf16),
            pltpu.VMEM((5 * SROWS, total // 2), bf16),
            pltpu.VMEM((SROWS + 8, D), f32),
        ],
    )

    if split:
        small_keep, small_send = small_pack
        gu = add2(gu_keep, once(gu_got, small_send))
        d = add2(d_keep, once(d_got, small_send))
        small_send = once(small_send, gu, d, attn_near)
        x_keep, x_send = add_halves(attn_own[0], attn_near)
        x_got = ctx_perm(x_send, 2)
        d = add2(d, once(ctx_perm(d, 4), x_got))
        gu = add2(gu, once(ctx_perm(gu, 4), x_got))
        d_o, gu_o = ctx_perm(d, 2), ctx_perm(gu, 2)
        x = add2(x_keep, once(x_got, gu))
        x = add2(x, once(ctx_perm(x, 4), gu_o, d_o))
        x_o = ctx_perm(x, 2)
        gu_parts = [a.reshape(wloc, half) for a in (gu, gu_o, twin(gu), twin(gu_o))]
        d_parts = (d, d_o, twin(d), twin(d_o))
        gate_grad, up_grad, down_grad = call(
            f_mlp_kernel,
            "f",
            5,
            (meta, *gu_parts, *d_parts),
            [SM] + [VM] * 8,
            (sds((wloc, ffl), f32), sds((wloc, ffl), f32), sds((ffl, wloc), f32)),
            [],
        )
        s = add2(small_keep, twin(small_send))
        t = add2(s[0], across(s[1]))
        t = add2(t, tp_other(t))
        t = add2(t, once(ctx_perm(t, 2), gu))
        t = add2(t, once(ctx_perm(t, 4), x))
        loss, table_grad, taps_grad, shift_grad, score_grad, gain1_grad, gain2_grad, bias_grad = call(
            f_small_kernel,
            "s",
            1,
            (meta, t, twin(t)),
            [SM] + [VM] * 2,
            (
                sds((1, 1), f32),
                sds((VOCAB, wloc), f32),
                sds((CONV, wloc), f32),
                sds((wloc,), f32),
                sds((wloc,), f32),
                sds((wloc,), f32),
                sds((wloc,), f32),
                sds((heads, bloc), f32),
            ),
            [pltpu.VMEM((SROWS, wloc), f32)],
            (SM,) + (VM,) * 7,
        )
        bias_grad = bias_grad.T
        attn_out = (x, x_o, twin(x), twin(once(x_o, gate_grad, table_grad)))
        attn_grads = call(
            f_attn_kernel,
            "h",
            3,
            (meta, *attn_out),
            [SM] + [VM] * 4,
            (sds((wloc, hl), f32),) * 3 + (sds((hl, wloc), f32),),
            [],
        )
    else:

        def owner_sum(x, axis, axes="ctx"):
            return lax.psum(lax.psum_scatter(x, "fsdp", scatter_dimension=axis, tiled=True), axes).astype(f32)

        gu, down = mlp_pack
        gate_grad, up_grad = owner_sum(gu, 1)
        down_grad = owner_sum(down, 1)
        qkv, wo = attn_pack
        attn_grads = tuple(owner_sum(qkv, 1)) + (owner_sum(wo, 1),)
        (x,) = small_pack
        t = owner_sum(x, 1, ("ctx", "tp"))
        table_grad, taps_grad, shift_grad, score_grad = t[:VOCAB], t[TAP_ROW : TAP_ROW + CONV], t[SHIFT_ROW], t[SCORE_ROW]
        gain1_grad, gain2_grad = t[GAIN1_ROW], t[GAIN2_ROW]
        x = lax.dynamic_slice_in_dim(x, BIAS_ROW + 8 * tp, 8, 0)[:heads, :NB].T
        bias_grad = lax.dynamic_slice_in_dim(lax.psum(x, ("fsdp", "ctx")).astype(f32), fs * bloc, bloc, 0)
        loss = lax.psum(loss, ("fsdp", "ctx"))
    query_grad, key_grad, value_grad, out_grad = attn_grads
    return (
        output,
        table_grad,
        taps_grad,
        shift_grad,
        score_grad,
        gain1_grad,
        query_grad,
        key_grad,
        value_grad,
        bias_grad,
        out_grad,
        gain2_grad,
        gate_grad,
        up_grad,
        down_grad,
        loss[0, 0],
    )


def solution(mesh):
    both = ("fsdp", "ctx")
    in_specs = (
        P(both),
        P(),
        P(),
        P(),
        P(),
        P(None, "fsdp"),
        P(None, "fsdp"),
        P("fsdp"),
        P("fsdp"),
        P("fsdp"),
        P("fsdp", "tp"),
        P("fsdp", "tp"),
        P("fsdp", "tp"),
        P("fsdp", "tp"),
        P("tp", "fsdp"),
        P("fsdp"),
        P("fsdp", "tp"),
        P("fsdp", "tp"),
        P("tp", "fsdp"),
        P(both, None),
    )
    out_specs = (
        P(both, "tp"),
        P(None, "fsdp"),
        P(None, "fsdp"),
        P("fsdp"),
        P("fsdp"),
        P("fsdp"),
        P("fsdp", "tp"),
        P("fsdp", "tp"),
        P("fsdp", "tp"),
        P("fsdp", "tp"),
        P("tp", "fsdp"),
        P("fsdp"),
        P("fsdp", "tp"),
        P("fsdp", "tp"),
        P("tp", "fsdp"),
        P(),
    )
    return jax.shard_map(shards, mesh=mesh, in_specs=in_specs, out_specs=out_specs, check_vma=False)
```

```python
import functools
import math

import jax
import jax.numpy as jnp
from jax import lax
from jax.experimental import pallas as pl
from jax.experimental.pallas import tpu as pltpu
from jax.sharding import PartitionSpec as P

D = 768
DH = 64
VOCAB = 259
NB = 32
RMAX = 128
CONV = 4

EPS = 1e-06
NEG = -1e30
GRAD_SCALE = 65536.0
LANES = 128
BLK = 128
HALO = 8
WIN = BLK + 2 * HALO
VP = 384
SROWS = 288
TAP_ROW = VOCAB
SHIFT_ROW = VOCAB + 4
SCORE_ROW = VOCAB + 5
GAIN1_ROW = VOCAB + 6
GAIN2_ROW = VOCAB + 7
BIAS_ROW = 272
LOSS_ROW = 267
f32 = jnp.float32
bf16 = jnp.bfloat16
i32 = jnp.int32
HI = lax.Precision.HIGHEST
ANY = pl.BlockSpec(memory_space=pl.ANY)
VM = pl.BlockSpec(memory_space=pltpu.VMEM)
SM = pl.BlockSpec(memory_space=pltpu.SMEM)


def nn(a, b, **k):
    return lax.dot_general(a, b, (((1,), (0,)), ((), ())), preferred_element_type=f32, **k)


def nt(a, b, **k):
    return lax.dot_general(a, b, (((1,), (1,)), ((), ())), preferred_element_type=f32, **k)


def tn(a, b, **k):
    return lax.dot_general(a, b, (((0,), (0,)), ((), ())), preferred_element_type=f32, **k)


def iota(shape, axis):
    return lax.broadcasted_iota(i32, shape, axis)


def aligned(index, step):
    return pl.multiple_of(index * step, step)


class Layout:
    pass


def token_rows(len_ref, pad_ref, fs, total, first=0, whole=1 << 30):
    t = iota((1, total), 1) + first
    live = (t >= 0) & (t < whole)
    start = jnp.zeros_like(t)
    end = jnp.zeros_like(t)
    limit = jnp.zeros_like(t)
    seg = jnp.zeros_like(t)
    base = jnp.int32(0)
    for k in range(len_ref.shape[1]):
        n = len_ref[fs, k]
        inside = t >= base
        start = jnp.where(inside, base, start)
        end = jnp.where(inside, base + n, end)
        limit = jnp.where(inside, 2 * n - pad_ref[fs, k], limit)
        seg = jnp.where(inside, k, seg)
        base = base + n
    lay = Layout()
    rel = t - start
    lay.seg = seg
    lay.real_e = live & (2 * rel < limit)
    lay.real_o = live & (2 * rel + 1 < limit)
    lay.prev = (live & (rel > 0)).astype(f32)
    lay.v = (live & (t + 1 < end)).astype(f32)
    third = (rel * 43691) >> 17
    u = rel - 3 * third
    lay.u0 = (u == 0).astype(f32)
    lay.u1 = (u == 1).astype(f32)
    lay.u2 = (u == 2).astype(f32)
    lay.odd = (rel & 1).astype(f32)
    lay.even = 1.0 - lay.odd
    third_f = jnp.float32(1.0 / 3.0)
    last0 = jnp.where(t + 1 < end, third_f, 0.5)
    lay.inv_e3 = jnp.where(u == 0, last0, third_f)
    lay.inv_o3 = jnp.where(u == 0, last0, jnp.where(u == 1, jnp.where(t + 1 < end, third_f, 1.0), third_f))
    lay.inv4 = jnp.where((rel & 1) == 1, 0.25, jnp.where(t + 1 < end, 0.25, 0.5))
    return lay


def forms(x, lay):
    em, om, e0, o0, ep, op = x
    pair = e0 + o0
    after = lay.v * (ep + op)
    first = pair + lay.v * ep
    closing = om + pair
    p2 = 0.5 * pair
    e3 = (lay.u0 * first + lay.u1 * (em + om + e0) + lay.u2 * closing) * lay.inv_e3
    o3 = (lay.u0 * first + lay.u1 * (o0 + after) + lay.u2 * closing) * lay.inv_o3
    p4 = (pair + lay.odd * (em + om) + lay.even * after) * lay.inv4
    return (e0, p2, e3, p4), (o0, p2, o3, p4)


def spread(we, wo, lay):
    e1, e2, e3, e4 = we
    o1, o2, o3, o4 = wo
    e3 = e3 * lay.inv_e3
    o3 = o3 * lay.inv_o3
    both = e3 + o3
    p4 = (e4 + o4) * lay.inv4
    p2 = (e2 + o2) * 0.5
    edge = lay.u0 * both + lay.u2 * both
    em = lay.u1 * e3 + lay.odd * p4
    om = em + lay.u2 * both
    e0 = e1 + p2 + edge + lay.u1 * e3 + p4
    o0 = o1 + p2 + edge + lay.u1 * o3 + p4
    op = lay.v * (lay.u1 * o3 + lay.even * p4)
    ep = op + lay.v * lay.u0 * both
    return em, om, e0, o0, ep, op


def before(row):
    return pltpu.roll(row, 1, 1)


def after(row):
    return pltpu.roll(row, row.shape[1] - 1, 1)


def softmax4(s):
    top = jnp.maximum(jnp.maximum(s[0], s[1]), jnp.maximum(s[2], s[3]))
    e = [jnp.exp(x - top) for x in s]
    inv = 1.0 / (e[0] + e[1] + e[2] + e[3])
    return [x * inv for x in e]


def put_rows(rows, total):
    sub = iota((8, total), 0)
    out = jnp.zeros((8, total), f32)
    for k, r in enumerate(rows):
        out = jnp.where(sub == k, jnp.broadcast_to(r, (8, total)), out)
    return out


def get_row(block, k):
    return jnp.sum(jnp.where(iota(block.shape, 0) == k, block, 0.0), axis=0, keepdims=True)


def eye():
    return (iota((BLK, BLK), 0) == iota((BLK, BLK), 1)).astype(f32)


def neighbours(e, o):
    return before(e), before(o), e, o, after(e), after(o)


def param_rows(tab_ref):
    rows = tab_ref[VOCAB - 3 : VOCAB + 13, :].astype(f32)
    return lambda k: rows[k - VOCAB + 3 : k - VOCAB + 4, :]


def id_rows(ids_ref):
    count = ids_ref.shape[0]
    return [jnp.concatenate([ids_ref[d, k : k + 1, :] for d in range(count)], axis=1) for k in range(2)]


def up1(x):
    return pltpu.roll(x, 1, 0)


def down1(x):
    return pltpu.roll(x, WIN - 1, 0)


def conv_window(ee, eo, lanes, row, pv, nx):
    eo_p = up1(eo) * pv
    ee_n = down1(ee) * nx
    eo_n = down1(eo) * nx
    c = [row(TAP_ROW + k)[:, lanes] for k in range(CONV)]
    b = row(SHIFT_ROW)[:, lanes]
    ce = b + c[0] * eo_p + c[1] * ee + c[2] * eo + c[3] * ee_n
    co = b + c[0] * ee + c[1] * eo + c[2] * ee_n + c[3] * eo_n
    return ce, co


def run_copies(copies, sems):
    made = [pltpu.make_async_copy(s, d, sems.at[k]) for k, (s, d) in enumerate(copies)]
    for c in made:
        c.start()
    return made


def split3(x):
    top = x.astype(bf16)
    rest = x - top.astype(f32)
    middle = rest.astype(bf16)
    return top, middle, (rest - middle.astype(f32)).astype(bf16)


def g_kernel(total, pieces, meta, len_ref, pad_ref, ids_ref, *refs):
    n = 2 if pieces else 1
    parts = refs[:n]
    tab_out, hid_out, n1_out, conv_out, rows_out = refs[n : n + 5]
    tab, hot2, ee, eo, idr, ge, go, coef, sems = refs[n + 5 :]
    fs, c = meta[0], meta[3]
    if pieces:
        w = D // 2
        copies = [
            (parts[0], tab.at[pl.ds(0, SROWS), pl.ds(aligned(fs, w), w)]),
            (parts[1], tab.at[pl.ds(0, SROWS), pl.ds(aligned(1 - fs, w), w)]),
        ]
    else:
        copies = [(parts[0], tab.at[pl.ds(0, SROWS), :])]
    made = run_copies(copies, sems)
    tab[SROWS:VP, :] = jnp.zeros((VP - SROWS, D), bf16)
    lay = token_rows(len_ref, pad_ref, fs, total, c * BLK - HALO, total)
    shifted = [jnp.where(c == 0, pltpu.roll(r, HALO, 1), pltpu.roll(r, total - BLK + HALO, 1)) for r in id_rows(ids_ref)]
    id_e = jnp.where(lay.real_e, shifted[0], -1)
    id_o = jnp.where(lay.real_o, shifted[1], -1)
    idr[...] = put_rows([id_e.astype(f32), id_o.astype(f32)], total)
    for m in made:
        m.wait()
    tab_out[...] = tab[...]
    row = param_rows(tab)
    score = row(SCORE_ROW)
    sub = iota((16, D), 0)
    cw = jnp.zeros((16, D), f32)
    for k in range(CONV):
        cw = jnp.where(sub == k, jnp.broadcast_to(row(TAP_ROW + k) * score, (16, D)), cw)
    top, middle, _ = split3(cw)
    g = jnp.concatenate(split3(nt(top, tab[...]) + nt(middle, tab[...])), axis=0)
    shift_score = jnp.sum(row(SHIFT_ROW) * score, axis=1, keepdims=True)
    step = 2 * BLK
    at = iota((VP, step), 0).astype(f32)

    def dots(i, carry):
        lanes = pl.ds(aligned(i, step), step)
        for k, out in ((0, ge), (1, go)):
            x = nn(g, (at == idr[k : k + 1, lanes]).astype(bf16))
            out[:, lanes] = x[0:8] + x[16:24] + x[32:40]
        return carry

    lax.fori_loop(0, total // step, dots, 0)
    qe = [get_row(ge[...], k) for k in range(4)]
    qo = [get_row(go[...], k) for k in range(4)]
    ze = lay.prev * before(qo[0]) + qe[1] + qo[2] + lay.v * after(qe[3]) + shift_score
    zo = qe[0] + qo[1] + lay.v * after(qe[2]) + lay.v * after(qo[3]) + shift_score
    se, so = forms(neighbours(ze, zo), lay)
    we, wo = softmax4(se), softmax4(so)
    em, om, e0, o0, ep, op = [0.5 * x for x in spread(we, wo, lay)]
    coef[...] = put_rows([e0, o0, after(em), after(om), before(ep), before(op), lay.prev, lay.v], total)
    rows_out[0:8, :] = put_rows(list(we) + list(wo), total)
    rows_out[8:16, :] = put_rows([e0, o0, em, om, ep, op], total)
    gain = row(GAIN1_ROW)
    lane = iota((WIN, VP), 1).astype(f32)

    def window(i, carry):
        lanes_at = pl.ds(aligned(i, step), step)
        ids = idr[:, lanes_at].T
        cols = coef[:, lanes_at].T
        hot2[0:WIN, :] = (lane == ids[0:WIN, 0:1]).astype(bf16)
        hot2[WIN : 2 * WIN, :] = (lane == ids[0:WIN, 1:2]).astype(bf16)
        both = nn(hot2[...], tab[...])
        ee[...] = both[0:WIN]
        eo[...] = both[WIN : 2 * WIN]
        col = [jnp.broadcast_to(cols[0:WIN, k : k + 1], (WIN, LANES)) for k in range(8)]
        total_sq = jnp.zeros((WIN, LANES), f32)
        for ch in range(D // LANES):
            lanes = slice(ch * LANES, (ch + 1) * LANES)
            ce, co = conv_window(ee[:, lanes], eo[:, lanes], lanes, row, col[6], col[7])
            conv_out[0, i, :, lanes] = ce.astype(bf16)
            conv_out[1, i, :, lanes] = co.astype(bf16)
            h = col[0] * ce + col[1] * co + up1(col[2] * ce + col[3] * co) + down1(col[4] * ce + col[5] * co)
            low = h.astype(bf16)
            ee[:, lanes] = low.astype(f32)
            total_sq = total_sq + ee[:, lanes] * ee[:, lanes]
        scale = lax.rsqrt(jnp.sum(total_sq, axis=1, keepdims=True) * (1.0 / D) + EPS)
        scale = jnp.broadcast_to(scale, (WIN, LANES))[HALO : HALO + BLK]
        for ch in range(D // LANES):
            lanes = slice(ch * LANES, (ch + 1) * LANES)
            h = ee[HALO : HALO + BLK, lanes]
            hid_out[i, :, lanes] = h.astype(bf16)
            n1_out[i, :, lanes] = (h * scale * gain[:, lanes]).astype(bf16)
        return carry

    lax.fori_loop(0, total // step, window, 0)


def attn_weight_copies(pieces, fs, c, parts, wqkv, wo):
    hl = wo.shape[0]
    if not pieces:
        q, k, v, o = parts
        return [(r, wqkv.at[:, pl.ds(j * hl, hl)]) for j, r in enumerate((q, k, v))] + [(o, wo)]
    q, k, v, o, mine, twin = parts
    w = D // 2
    hw = w // 2
    out = []
    for j, r in enumerate((q, k, v)):
        lanes = pl.ds(j * hl, hl)
        out.append((r, wqkv.at[pl.ds(aligned(fs, w), w), lanes]))
        base = (1 - fs) * w
        out.append((mine.at[j], wqkv.at[pl.ds(pl.multiple_of(base + c * hw, hw), hw), lanes]))
        out.append((twin.at[j], wqkv.at[pl.ds(pl.multiple_of(base + (1 - c) * hw, hw), hw), lanes]))
    other = pl.ds(aligned(1 - fs, w), w)
    out.append((o, wo.at[:, pl.ds(aligned(fs, w), w)]))
    out.append((mine.at[3], wo.at[pl.ds(aligned(c, hw), hw), other]))
    out.append((twin.at[3], wo.at[pl.ds(aligned(1 - c, hw), hw), other]))
    return out


def bias_rows(tab_ref, ext_ref, tp, shards_at):
    block = tab_ref[BIAS_ROW : BIAS_ROW + 16, :]
    ext = ext_ref[...]
    width = NB // len(shards_at)
    sub = iota((LANES, ext.shape[1]), 0)
    out = jnp.zeros((16, ext.shape[1]), f32)
    for j, lane in enumerate(shards_at):
        hot = ((sub < width) & (sub + j * width == ext)).astype(bf16)
        out = out + nn(block[:, lane : lane + LANES], hot)
    return out


def bias_plane(band, left, right, cx, plane, total):
    rolled = pltpu.roll(jnp.broadcast_to(band, (BLK, 512)), 0, 1, stride=1, stride_axis=0)
    at = iota((1, total + 2 * BLK), 1)
    plane[...] = jnp.broadcast_to(jnp.where(at < cx * BLK, left, right), plane.shape)
    plane[:, pl.ds(aligned(cx, BLK), 3 * BLK)] = rolled[:, BLK:]
    return plane[:, BLK : BLK + total]


def attn_masks(len_ref, pad_ref, fs, cx, total):
    lay = token_rows(len_ref, pad_ref, fs, total)
    seg = jnp.where(lay.real_e, lay.seg, -1).astype(f32)
    own = token_rows(len_ref, pad_ref, fs, BLK, cx * BLK)
    col = nt(eye(), put_rows([own.seg.astype(f32), own.real_e.astype(f32)], BLK), precision=HI)
    return jnp.where(col[:, 0:1] == seg, 0.0, NEG), col[:, 1:2]


def a_kernel(total, pieces, shards_at, meta, len_ref, pad_ref, ext_ref, tab_ref, n1_mine, n1_twin, *refs):
    n = 6 if pieces else 4
    parts = refs[:n]
    q_out, k_out, v_out, att_out, lse_out, part_out, n1_out = refs[n : n + 7]
    wqkv, wo, plane, mask, fr, sems = refs[n + 7 :]
    fs, cx, tp, c = meta[0], meta[1], meta[2], meta[3]
    hl = wo.shape[0]
    made = run_copies(attn_weight_copies(pieces, fs, c, parts, wqkv, wo), sems)
    mask[...], _ = attn_masks(len_ref, pad_ref, fs, cx, total)
    fr[...] = bias_rows(tab_ref, ext_ref, tp, shards_at)
    for m in made:
        m.wait()
    q_out[...] = nn(n1_mine[cx >> 1], wqkv[:, 0:hl]).astype(bf16)

    def project(i, carry):
        x = jnp.concatenate([n1_mine[i], n1_twin[i]], axis=0)
        kv = nn(x, wqkv[:, hl : 3 * hl]).astype(bf16)
        for k in range(2):
            rows = pl.ds(aligned(2 * i + (c if k == 0 else 1 - c), BLK), BLK)
            mid = slice(k * BLK, (k + 1) * BLK)
            n1_out[rows, :] = x[mid]
            k_out[rows, :] = kv[mid, 0:hl]
            v_out[rows, :] = kv[mid, hl : 2 * hl]
        return carry

    lax.fori_loop(0, total // (2 * BLK), project, 0)
    lo = iota((1, LANES), 1) < DH
    lane = iota((BLK, LANES), 1)
    lse = jnp.zeros((BLK, LANES), f32)
    for pair in range(hl // LANES):
        lanes = slice(pair * LANES, (pair + 1) * LANES)
        q2, k2, v2 = q_out[:, lanes], k_out[:, lanes], v_out[:, lanes]
        halves = []
        for half in range(2):
            h = 2 * pair + half
            keep = lo if half == 0 else jnp.logical_not(lo)
            qm = jnp.where(keep, q2, jnp.zeros_like(q2)) * bf16(1.0 / math.sqrt(DH))
            band = fr[h : h + 1, :]
            bias = bias_plane(band, band[:, 0:1], band[:, 511:512], cx, plane, total)
            s = nt(qm, k2) + bias + mask[...]
            top = jnp.max(s, axis=1, keepdims=True)
            e = jnp.exp(s - top)
            tot = jnp.sum(e, axis=1, keepdims=True)
            lse = jnp.where(lane == h, top + jnp.log(tot), lse)
            halves.append(nn((e * (1.0 / tot)).astype(bf16), v2))
        att_out[:, lanes] = jnp.where(lo, halves[0], halves[1]).astype(bf16)
    lse_out[...] = lse
    part_out[...] = nn(att_out[...], wo[...]).astype(bf16)


def mlp_weight_copies(pieces, fs, c, parts, wg, wu, wd):
    if not pieces:
        return list(zip(parts, (wg, wu, wd)))
    g, u, d, gu_mine, gu_twin, d_mine, d_twin = parts
    w = D // 2
    hw = w // 2
    hr = wd.shape[0] // 2
    out = []
    for j, (r, dst) in enumerate(((g, wg), (u, wu))):
        base = (1 - fs) * w
        out.append((r, dst.at[pl.ds(aligned(fs, w), w), :]))
        out.append((gu_mine.at[j], dst.at[pl.ds(pl.multiple_of(base + c * hw, hw), hw), :]))
        out.append((gu_twin.at[j], dst.at[pl.ds(pl.multiple_of(base + (1 - c) * hw, hw), hw), :]))
    other = pl.ds(aligned(1 - fs, w), w)
    out.append((d, wd.at[:, pl.ds(aligned(fs, w), w)]))
    out.append((d_mine, wd.at[pl.ds(aligned(c, hr), hr), other]))
    out.append((d_twin, wd.at[pl.ds(aligned(1 - c, hr), hr), other]))
    return out


def tanh_parts(x):
    k = math.sqrt(2.0 / math.pi)
    th = jnp.tanh(k * (x + 0.044715 * x * x * x))
    return th, k


def b_kernel(pieces, meta, tab_ref, hid_ref, mine_ref, other_ref, *refs):
    n = 7 if pieces else 3
    parts = refs[:n]
    res_out, act_out, gate_out, up_out, part_out = refs[n : n + 5]
    wg, wu, wd, sems = refs[n + 5 :]
    ffl = wg.shape[1]
    fs, cx, c = meta[0], meta[1], meta[3]
    made = run_copies(mlp_weight_copies(pieces, fs, c, parts, wg, wu, wd), sems)
    gain = param_rows(tab_ref)(GAIN2_ROW)
    res = hid_ref[cx >> 1].astype(f32) + (mine_ref[...].astype(f32) + other_ref[...].astype(f32))
    res_out[...] = res
    scale = lax.rsqrt(jnp.sum(res * res, axis=1, keepdims=True) * (1.0 / D) + EPS)
    n2 = (res * scale * gain).astype(bf16)
    act_out[:, 0:D] = n2
    for m in made:
        m.wait()
    gate = nn(n2, wg[...])
    up = nn(n2, wu[...])
    gate_out[...] = gate
    up_out[...] = up
    th, _ = tanh_parts(gate)
    gated = (0.5 * gate * (1.0 + th) * up).astype(bf16)
    act_out[:, D : D + ffl] = gated
    part_out[...] = nn(gated, wd[...]).astype(bf16)


def c_kernel(pieces, meta, len_ref, pad_ref, deal_ref, teach_ref, res_ref, mine_ref, other_ref, gate_ref, up_ref, *refs):
    n = 7 if pieces else 3
    parts = refs[:n]
    out_ref, loss_out, gres_out, act_out, part_out = refs[n : n + 5]
    wg, wu, wd, teacher, sems = refs[n + 5 :]
    ffl = wg.shape[1]
    fs, cx, tp, c = meta[0], meta[1], meta[2], meta[3]
    made = run_copies(mlp_weight_copies(pieces, fs, c, parts, wg, wu, wd), sems)
    slots, unit = teach_ref.shape[0], teach_ref.shape[1]
    for s in range(slots):
        teacher[s * unit : (s + 1) * unit, :] = teach_ref[deal_ref[fs, cx, s]].astype(f32)
    count = jnp.int32(0)
    for f in range(len_ref.shape[0]):
        for k in range(len_ref.shape[1]):
            count = count + ((2 * len_ref[f, k] - pad_ref[f, k] + 1) >> 1)
    real_count = jnp.broadcast_to(count, (1, LANES)).astype(f32)[:, 0:1]
    own = token_rows(len_ref, pad_ref, fs, BLK, cx * BLK)
    valid = nt(eye(), put_rows([own.real_e.astype(f32)], BLK), precision=HI)[:, 0:1]
    result = res_ref[...] + (mine_ref[...].astype(f32) + other_ref[...].astype(f32))
    width = out_ref.shape[1]
    out_ref[...] = jnp.where(tp == 0, result[:, 0:width], result[:, D - width : D]).astype(bf16)
    diff = (result - teacher[...]) * valid
    square = jnp.sum(jnp.sum(diff * diff, axis=1, keepdims=True), axis=0, keepdims=True)
    loss_out[...] = jnp.broadcast_to(square / (2.0 * D * real_count), (8, LANES))
    gres = diff * (GRAD_SCALE / (D * real_count))
    gres_out[...] = gres
    low = gres.astype(bf16)
    act_out[:, 0:D] = low
    for m in made:
        m.wait()
    ggated = nt(low, wd[...])
    gate = gate_ref[...]
    up = up_ref[...]
    th, k = tanh_parts(gate)
    value = 0.5 * gate * (1.0 + th)
    slope = 0.5 * (1.0 + th) + 0.5 * gate * (1.0 - th * th) * (k * (1.0 + 3.0 * 0.044715 * gate * gate))
    gg = (ggated * up * slope).astype(bf16)
    gu = (ggated * value).astype(bf16)
    act_out[:, D : D + ffl] = gg
    act_out[:, D + ffl : D + 2 * ffl] = gu
    part_out[...] = (nt(gg, wg[...]) + nt(gu, wu[...])).astype(bf16)


def m_kernel(split, ffl, meta, *refs):
    if not split:
        act1, act2, gu_out, down_out = refs
        n2, gated = act1[:, 0:D], act1[:, D : D + ffl]
        gu_out[0] = tn(n2, act2[:, D : D + ffl]).astype(bf16)
        gu_out[1] = tn(n2, act2[:, D + ffl : D + 2 * ffl]).astype(bf16)
        down_out[...] = tn(gated, act2[:, 0:D]).astype(bf16)
        return
    act1, act1_t, act2, act2_t, gu_own, gu_oth, d_own, d_oth, wide, tall = refs
    fs, c = meta[0], meta[3]
    w = D // 2
    half = ffl // 2

    def both(mine, twin, first):
        lanes = pl.ds(pl.multiple_of(first + c * half, LANES), half)
        return jnp.concatenate([mine[:, lanes], twin[:, lanes]], axis=0)

    n2 = jnp.concatenate([act1[:, 0:D], act1_t[:, 0:D]], axis=0)
    low = jnp.concatenate([act2[:, 0:D], act2_t[:, 0:D]], axis=0)
    mine, other = pl.ds(aligned(fs, w), w), pl.ds(aligned(1 - fs, w), w)
    for j in range(2):
        wide[...] = tn(n2, both(act2, act2_t, D + j * ffl)).astype(bf16)
        gu_own[j] = wide[mine, :]
        gu_oth[j] = wide[other, :]
    tall[...] = tn(both(act1, act1_t, D), low).astype(bf16)
    d_own[...] = tall[:, mine]
    d_oth[...] = tall[:, other]


def d_kernel(total, pieces, shards_at, tps, meta, len_ref, pad_ref, ext_ref, ext1_ref, tab_ref, n1_ref, q_ref, k_ref, v_ref, att_ref, lse_ref, res_ref, gres_ref, hid_mine, hid_twin, mine_ref, other_ref, *refs):
    n = 6 if pieces else 4
    parts = refs[:n]
    m = 2
    packs = refs[n : n + m]
    keep_out, send_out, extra_out = refs[n + m : n + m + 3]
    wqkv, wo, plane, mask, fr, dsw, stack, ga, dq, dkv, wide, wo_grad, dh, sems = refs[n + m + 3 :]
    fs, cx, tp, c = meta[0], meta[1], meta[2], meta[3]
    hl = wo.shape[0]
    made = run_copies(attn_weight_copies(pieces, fs, c, parts, wqkv, wo), sems)
    mask[...], _ = attn_masks(len_ref, pad_ref, fs, cx, total)
    fr[...] = bias_rows(tab_ref, ext_ref, tp, shards_at)
    gain = param_rows(tab_ref)(GAIN2_ROW)
    gn2 = mine_ref[...].astype(f32) + other_ref[...].astype(f32)
    res = res_ref[...]
    r2 = lax.rsqrt(jnp.sum(res * res, axis=1, keepdims=True) * (1.0 / D) + EPS)
    u = gain * gn2
    gain_grad = jnp.sum(gn2 * res * r2, axis=0, keepdims=True) * (1.0 / tps)
    back = gres_ref[...] + r2 * u - res * (r2 * r2 * r2 * (jnp.sum(u * res, axis=1, keepdims=True) * (1.0 / D)))
    branch = back.astype(bf16)
    for x in made:
        x.wait()
    wo_grad[...] = tn(att_ref[...], branch).astype(bf16)
    ga[...] = nt(branch, wo[...]).astype(bf16)
    lo = iota((1, LANES), 1) < DH
    at = iota((1, total), 1)
    first = cx * BLK - BLK
    rev = (iota((BLK, BLK), 0) + iota((BLK, BLK), 1) == BLK - 1).astype(bf16)
    band_at = iota((1, 512), 1)
    scale = bf16(1.0 / math.sqrt(DH))
    sums = []
    for pair in range(hl // LANES):
        lanes = slice(pair * LANES, (pair + 1) * LANES)
        q2, k2, v2, g2 = q_ref[:, lanes], k_ref[:, lanes], v_ref[:, lanes], ga[:, lanes]
        zero = jnp.zeros_like(q2)
        qs, gs, dqs = [], [], []
        for half in range(2):
            h = 2 * pair + half
            keep = lo if half == 0 else jnp.logical_not(lo)
            qm = jnp.where(keep, q2, zero) * scale
            gm = jnp.where(keep, g2, zero)
            band = fr[h : h + 1, :]
            bias = bias_plane(band, band[:, 0:1], band[:, 511:512], cx, plane, total)
            s = nt(qm, k2) + bias + mask[...]
            p = jnp.exp(s - lse_ref[:, h : h + 1])
            g = nt(gm, v2)
            inner = jnp.sum(p * g, axis=1, keepdims=True)
            ds = p * (g - inner)
            low = ds.astype(bf16)
            stack[0, half * BLK : (half + 1) * BLK, :] = low
            stack[1, half * BLK : (half + 1) * BLK, :] = p.astype(bf16)
            wide_ds = low.astype(f32)
            col = jnp.sum(wide_ds, axis=0, keepdims=True)
            left = jnp.sum(jnp.where(at < first, col, 0.0), axis=1, keepdims=True)
            right = jnp.sum(jnp.where(at >= first + 3 * BLK, col, 0.0), axis=1, keepdims=True)
            dsw[:, BLK : BLK + total] = wide_ds
            if pair == 0 and half == 0:
                dsw[:, 0:BLK] = jnp.zeros((BLK, BLK), f32)
                dsw[:, BLK + total :] = jnp.zeros((BLK, 2 * BLK), f32)
            window = dsw[:, pl.ds(aligned(cx, BLK), 512)]
            window = jnp.where(band_at < 3 * BLK, window, 0.0).astype(bf16)
            turned = pltpu.roll(nn(rev, window), 0, 1, stride=1, stride_axis=0)
            diag = jnp.sum(turned, axis=0, keepdims=True)
            diag = diag + jnp.where(band_at == 0, left, 0.0) + jnp.where(band_at == 510, right, 0.0)
            sums.append(diag)
            dqs.append(nn(low, k2))
            qs.append(qm)
            gs.append(gm)
        dq[:, lanes] = (jnp.where(lo, dqs[0], dqs[1]) * (1.0 / math.sqrt(DH))).astype(bf16)
        dkv[:, lanes] = tn(stack[0], jnp.concatenate(qs, axis=0)).astype(bf16)
        dkv[:, hl + pair * LANES : hl + (pair + 1) * LANES] = tn(stack[1], jnp.concatenate(gs, axis=0)).astype(bf16)
    own = pl.ds(aligned(cx, BLK), BLK)
    wide[0] = tn(n1_ref[own, :], dq[...]).astype(bf16)
    both = tn(n1_ref[...], dkv[...])
    wide[1] = both[:, 0:hl].astype(bf16)
    wide[2] = both[:, hl : 2 * hl].astype(bf16)
    if pieces:
        w, hw = D // 2, D // 4
        for half, ref in enumerate(packs):
            cc = c if half == 0 else 1 - c
            for rel in range(2):
                f = fs if rel == 0 else 1 - fs
                for j in range(3):
                    ref[rel, j] = wide[j, pl.ds(pl.multiple_of(f * w + cc * hw, hw), hw), :]
                ref[rel, 3] = wo_grad[pl.ds(aligned(cc, hw), hw), pl.ds(aligned(f, w), w)]
    else:
        packs[0][...] = wide[...]
        packs[1][...] = wo_grad[...]
    own_grad = nt(dq[...], wqkv[:, 0:hl])
    gain1 = param_rows(tab_ref)(GAIN1_ROW)
    dh[0:HALO, :] = jnp.zeros((HALO, D), f32)
    dh[total + HALO : total + 2 * HALO, :] = jnp.zeros((HALO, D), f32)

    def norm_back(h, grad):
        r = lax.rsqrt(jnp.sum(h * h, axis=1, keepdims=True) * (1.0 / D) + EPS)
        u = gain1 * grad
        d = r * u - h * (r * r * r * (jnp.sum(u * h, axis=1, keepdims=True) * (1.0 / D)))
        return d, jnp.sum(grad * h * r, axis=0, keepdims=True)

    def back_rows(i, carry):
        for k, hid in enumerate((hid_mine, hid_twin)):
            b = 2 * i + (c if k == 0 else 1 - c)
            grad = nt(dkv[pl.ds(aligned(b, BLK), BLK), :], wqkv[:, hl : 3 * hl])
            d, g = norm_back(hid[i].astype(f32), grad)
            dh[pl.ds(pl.multiple_of(b * BLK + HALO, HALO), BLK), :] = d
            carry = carry + g
        return carry

    gain1_grad = lax.fori_loop(0, total // (2 * BLK), back_rows, jnp.zeros((1, D), f32))
    d, g = norm_back(hid_mine[cx >> 1].astype(f32), own_grad)
    gain1_grad = gain1_grad + g
    here = pl.ds(pl.multiple_of(cx * BLK + HALO, HALO), BLK)
    dh[here, :] = dh[here, :] + (d + back * (1.0 / tps))

    def windows(i, carry):
        for k, out in enumerate((keep_out, send_out)):
            b = 2 * i + (c if k == 0 else 1 - c)
            out[i] = dh[pl.ds(aligned(b, BLK), WIN), :].astype(bf16)
        return carry

    lax.fori_loop(0, total // (2 * BLK), windows, 0)
    rows = put_rows(sums, 512)
    ext = ext1_ref[...]
    width = NB // len(shards_at)
    sub = iota((LANES, 512), 0)
    extra_out[...] = jnp.zeros(extra_out.shape, f32)
    for j, lane in enumerate(shards_at):
        hot = ((sub < width) & (sub + j * width == ext)).astype(f32)
        extra_out[pl.ds(aligned(tp, 8), 8), lane : lane + LANES] = nt(rows, hot, precision=HI)
    extra_out[16:24, :] = put_rows([gain1_grad, gain_grad], D)


def e_kernel(total, split, spots, meta, len_ref, pad_ref, ids_ref, tab_ref, conv_ref, rows_ref, keep_ref, recv_ref, extra_ref, loss_ref, *refs):
    n = 2 if split else 1
    outs = refs[:n]
    xr, dz, idr, dh, dc, hots, wide = refs[n:]
    fs, cx, c = meta[0], meta[1], meta[3]
    windows = total // (2 * BLK)
    step = 2 * BLK
    lay = token_rows(len_ref, pad_ref, fs, total, c * BLK - HALO, total)
    xr[...] = jnp.zeros(xr.shape, f32)
    s_at, t_at = iota((WIN, WIN), 0), iota((WIN, WIN), 1)

    def inner(i, carry):
        d = (keep_ref[i].astype(f32) + recv_ref[i].astype(f32)).astype(bf16)
        dh[i] = d
        for k in range(2):
            gram = nt(conv_ref[k, i], d)
            for j in range(3):
                part = jnp.sum(jnp.where(s_at == t_at + (j - 1), gram, 0.0), axis=0, keepdims=True)
                xr[2 * j + k, 0:1, pl.ds(aligned(i, step), WIN)] = part
        return carry

    lax.fori_loop(0, windows, inner, 0)
    x = [0.5 * xr[k, 0:1, :] for k in range(6)]
    pe, po = forms(x, lay)
    we = [get_row(rows_ref[0:8, :], k) for k in range(4)]
    wo = [get_row(rows_ref[0:8, :], k + 4) for k in range(4)]

    def soft_back(w, p):
        mean = w[0] * p[0] + w[1] * p[1] + w[2] * p[2] + w[3] * p[3]
        return [a * (b - mean) for a, b in zip(w, p)]

    em, om, e0, o0, ep, op = spread(soft_back(we, pe), soft_back(wo, po), lay)
    dze = e0 + after(em) + before(ep)
    dzo = o0 + after(om) + before(op)
    dz[...] = put_rows([dze, dzo], total)
    score = jnp.broadcast_to(tab_ref[SCORE_ROW : SCORE_ROW + 1, :], (WIN, D))
    sub16 = iota((16, WIN), 0)
    at16 = iota((16, WIN), 1)
    own16 = (at16 >= HALO) & (at16 < HALO + BLK)

    def stencil(i, carry):
        lanes = pl.ds(aligned(i, step), WIN)
        d = dh[i]
        for k in range(2):
            z = dz[k : k + 1, lanes]
            mid = rows_ref[8 + k : 9 + k, lanes]
            prv = rows_ref[10 + k : 11 + k, lanes]
            nxt = rows_ref[12 + k : 13 + k, lanes]
            band = jnp.where(t_at == s_at, mid, 0.0)
            band = jnp.where(t_at == s_at + 1, prv, band)
            band = jnp.where(t_at == s_at - 1, nxt, band)
            grad = nn(band.astype(bf16), d) + nn(jnp.where(t_at == s_at, z, 0.0).astype(bf16), score)
            dc[k, pl.ds(aligned(i, BLK), BLK), :] = grad[HALO : HALO + BLK].astype(bf16)
            top = z.astype(bf16).astype(f32)
            pair = jnp.where(sub16 == 0, top, jnp.where(sub16 == 1, z - top, 0.0))
            carry = carry + nn(jnp.where(own16, pair, 0.0).astype(bf16), conv_ref[k, i])
        return carry

    score_rows = lax.fori_loop(0, windows, stencil, jnp.zeros((16, D), f32))
    score_grad = jnp.sum(score_rows, axis=0, keepdims=True)
    whole = token_rows(len_ref, pad_ref, fs, total)
    raw = id_rows(ids_ref)
    id_e = jnp.where(whole.real_e, raw[0], -1).astype(f32)
    id_o = jnp.where(whole.real_o, raw[1], -1).astype(f32)
    later = whole.v > 0.0
    idr[...] = put_rows(
        [
            jnp.where(whole.prev > 0.0, before(id_o), -1.0),
            id_e,
            id_o,
            jnp.where(later, after(id_e), -1.0),
            jnp.where(later, after(id_o), -1.0),
        ],
        total,
    )
    v_at = iota((SROWS, BLK), 0)
    symbol = v_at.astype(f32)

    def spell(i, carry):
        lanes = pl.ds(aligned(2 * i + c, BLK), BLK)
        for k in range(5):
            hot = symbol == idr[k : k + 1, lanes]
            if k == 1:
                hot = hot | (v_at == SROWS - 1)
            hots[k * SROWS : (k + 1) * SROWS, pl.ds(aligned(i, BLK), BLK)] = hot.astype(f32).astype(bf16)
        return carry

    lax.fori_loop(0, windows, spell, 0)
    wide[...] = jnp.zeros(wide.shape, f32)
    table_rows = VOCAB + 5
    taps = tab_ref[TAP_ROW - 3 : TAP_ROW + 13, :].astype(f32)[3 : 3 + CONV]
    table = tab_ref[0:table_rows, :].astype(f32)
    shift_grad = jnp.zeros((1, D), f32)
    for j in range(CONV):
        acc = nn(hots[j * SROWS : (j + 1) * SROWS, :], dc[0]) + nn(hots[(j + 1) * SROWS : (j + 2) * SROWS, :], dc[1])
        wide[0:table_rows, :] += taps[j : j + 1] * acc[0:table_rows]
        tap_grad = jnp.sum(table * acc[0:table_rows], axis=0, keepdims=True)
        shift_grad = shift_grad + acc[SROWS - 1 : SROWS, :]
        wide[SROWS + j : SROWS + j + 1, :] = tap_grad
    for j in range(CONV):
        wide[TAP_ROW + j : TAP_ROW + j + 1, :] = wide[SROWS + j : SROWS + j + 1, :]
    wide[SHIFT_ROW : SHIFT_ROW + 1, :] = shift_grad
    wide[SCORE_ROW : SCORE_ROW + 1, :] = score_grad
    wide[GAIN1_ROW : GAIN1_ROW + 1, :] = extra_ref[16:17, :]
    wide[GAIN2_ROW : GAIN2_ROW + 1, :] = extra_ref[17:18, :]
    wide[BIAS_ROW : BIAS_ROW + 16, :] = extra_ref[0:16, :]
    part = loss_ref[0:1, :]
    top = part.astype(bf16).astype(f32)
    rest = part - top
    middle = rest.astype(bf16).astype(f32)
    at = iota((1, LANES), 1) - 4 * (fs * spots + cx)
    coded = jnp.where(at == 0, top, jnp.where(at == 1, middle, jnp.where(at == 2, rest - middle, 0.0)))
    coded = jnp.where(meta[2] == 0, coded, 0.0)
    for lane in (0, D // 2):
        wide[LOSS_ROW : LOSS_ROW + 1, lane : lane + LANES] = coded
    if not split:
        outs[0][...] = wide[0:SROWS, :].astype(bf16)
        return
    w = D // 2
    hr = SROWS // 2
    for half, ref in enumerate(outs):
        cc = c if half == 0 else 1 - c
        for rel in range(2):
            f = fs if rel == 0 else 1 - fs
            ref[rel] = wide[pl.ds(pl.multiple_of(cc * hr, 8), hr), pl.ds(aligned(f, w), w)].astype(bf16)


def f_mlp_kernel(meta, gu, gu_o, gu_t, gu_ot, d, d_o, d_t, d_ot, g_out, u_out, d_out):
    c, odd = meta[3], (meta[1] >> 1) & 1
    half = d.shape[0] * 2
    mine, other = pl.ds(aligned(c, half), half), pl.ds(aligned(1 - c, half), half)
    first = odd == 0
    for lanes, a, b in ((mine, gu, gu_o), (other, gu_t, gu_ot)):
        a, b = a[...].astype(f32), b[...].astype(f32)
        g_out[:, lanes] = jnp.where(first, a, b)
        u_out[:, lanes] = jnp.where(first, b, a)
    q = d.shape[0]
    for at, a, b in ((c, d, d_o), (1 - c, d_t, d_ot)):
        d_out[pl.ds(aligned(2 * at + odd, q), q), :] = a[...].astype(f32)
        d_out[pl.ds(aligned(2 * at + 1 - odd, q), q), :] = b[...].astype(f32)


def f_attn_kernel(meta, x, x_o, x_t, x_ot, *refs):
    outs = refs[0:4]
    loss, table, taps, shift, score, gain1, gain2, bias, whole = refs[4:]
    tp, c, odd = meta[2], meta[3], (meta[1] >> 1) & 1
    hw = D // 4
    hr = SROWS // 4
    first = odd == 0
    for at, a, b in ((c, x, x_o), (1 - c, x_t, x_ot)):
        rows = pl.ds(aligned(at, hw), hw)
        for j in range(2):
            p, q = a[j * hw : (j + 1) * hw, :].astype(f32), b[j * hw : (j + 1) * hw, :].astype(f32)
            outs[j][rows, :] = jnp.where(first, p, q)
            outs[2 + j][rows, :] = jnp.where(first, q, p)
        whole[pl.ds(aligned(2 * at + odd, hr), hr), :] = a[2 * hw : 2 * hw + hr, :].astype(f32)
        whole[pl.ds(aligned(2 * at + 1 - odd, hr), hr), :] = b[2 * hw : 2 * hw + hr, :].astype(f32)
    loss[0, 0] = jnp.sum(whole[LOSS_ROW : LOSS_ROW + 1, 0:LANES])
    table[...] = whole[0:VOCAB, :]
    taps[...] = whole[TAP_ROW : TAP_ROW + CONV, :]
    for k, out in ((SHIFT_ROW, shift), (SCORE_ROW, score), (GAIN1_ROW, gain1), (GAIN2_ROW, gain2)):
        out[...] = whole[k : k + 1, :].reshape(out.shape)
    rows = whole[pl.ds(pl.multiple_of(BIAS_ROW + 8 * tp, 8), 8), 0:LANES]
    bias[...] = rows[0 : bias.shape[0], 0 : bias.shape[1]]


def p_kernel(emb, taps, shift, score, gain1, gain2, bias, out, wide):
    wide[...] = jnp.zeros(wide.shape, f32)
    wide[0:VOCAB, :] = emb[...].astype(f32)
    wide[TAP_ROW : TAP_ROW + CONV, :] = taps[...].astype(f32)
    for k, ref in ((SHIFT_ROW, shift), (SCORE_ROW, score), (GAIN1_ROW, gain1), (GAIN2_ROW, gain2)):
        wide[k : k + 1, :] = ref[...].astype(f32).reshape(1, ref.shape[0])
    m, n = bias.shape
    wide[BIAS_ROW : BIAS_ROW + m, 0:n] = bias[...].astype(f32)
    out[...] = wide[...].astype(bf16)


def sds(shape, dtype):
    return jax.ShapeDtypeStruct(shape, dtype)


def call(kernel, name, us, ins, in_specs, out_shape, scratch, out_specs=None):
    return pl.pallas_call(
        kernel,
        name=name,
        cost_estimate=pl.CostEstimate(flops=0, transcendentals=0, bytes_accessed=int(us * 3.69e6)),
        out_shape=out_shape,
        in_specs=in_specs,
        out_specs=out_specs or jax.tree.map(lambda _: VM, out_shape),
        scratch_shapes=scratch,
        compiler_params=pltpu.CompilerParams(vmem_limit_bytes=60 << 20),
    )(*ins)


def once(x, *others):
    return lax.optimization_barrier((x, *others))[0]


def add2(a, b):
    return (a.astype(f32) + b.astype(f32)).astype(bf16)


def shards(
    byte_ids,
    seq_tokens,
    pad_bytes,
    deal_targets,
    rel_buckets,
    embedding,
    conv_weight,
    conv_bias,
    score_weight,
    attn_gain,
    query_weight,
    key_weight,
    value_weight,
    rel_bias,
    out_weight,
    mlp_gain,
    gate_weight,
    up_weight,
    down_weight,
    teacher,
):
    fs = lax.axis_index("fsdp")
    cx = lax.axis_index("ctx")
    tp = lax.axis_index("tp")
    fcount, ccount, tps = lax.axis_size("fsdp"), lax.axis_size("ctx"), lax.axis_size("tp")
    core = cx % 2
    total = teacher.shape[0] * ccount
    unit = teacher.shape[0] // ccount
    hl = query_weight.shape[1]
    heads = hl // DH
    ffl = gate_weight.shape[1]
    split = fcount == 2
    wloc = D // fcount
    bloc = NB // fcount
    meta = jnp.stack([fs, cx, tp, core]).astype(i32)

    def twin(x):
        return lax.ppermute(x, "ctx", [(i, i ^ 1) for i in range(ccount)])

    def across(x):
        return lax.ppermute(x, "fsdp", [(0, 1), (1, 0)])

    def tp_other(x):
        return lax.ppermute(x, "tp", [(i, tps - 1 - i) for i in range(tps)])

    def core_half(x, axis):
        n = x.shape[axis] // 2
        return lax.dynamic_slice_in_dim(x, core * n, n, axis)

    ends = lambda k: jnp.broadcast_to(rel_buckets[k : k + 1], (RMAX,))
    ext = jnp.concatenate([ends(0), rel_buckets, ends(2 * RMAX)])
    ext, ext1 = ext[None, :512], ext[None, 1:513]

    def exchange(x):
        return lax.all_to_all(x, "ctx", split_axis=0, concat_axis=0, tiled=True)

    small_ins = (embedding, conv_weight, conv_bias, score_weight, attn_gain, mlp_gain, rel_bias.T)
    small = call(p_kernel, "p", 1, small_ins, [VM] * 7, sds((SROWS, wloc), bf16), [pltpu.VMEM((SROWS, wloc), f32)])
    ids = exchange(jnp.broadcast_to(byte_ids.reshape(-1, 2).T[None], (ccount, 2, byte_ids.shape[0] // 2)))
    if split:
        small_other = across(small)
        small_parts = (small, small_other)
        attn = core_half(jnp.stack([query_weight, key_weight, value_weight, out_weight]), 1)
        mine = across(once(attn, small_other, ids))
        d_mine = across(once(core_half(down_weight, 0), small_other, ids))
    else:
        gather = lambda x, axis: lax.all_gather(x, "fsdp", axis=axis, tiled=True)
        full = gather(small, 1)
        bias_all = jnp.pad(gather(rel_bias, 0).T, ((0, 16 - heads), (0, D - NB)))
        small_parts = (jnp.concatenate([full[:BIAS_ROW], bias_all], axis=0),)
        attn_parts = (gather(query_weight, 0), gather(key_weight, 0), gather(value_weight, 0), gather(out_weight, 1))
        mlp_parts = (gather(gate_weight, 0), gather(up_weight, 0), gather(down_weight, 1))
    shards_at = (0, wloc) if split else (0,)
    teach = exchange(once(teacher.reshape(ccount, unit, D), ids))

    nw = total // (2 * BLK)
    tab, hid, n1, conv, rows = call(
        functools.partial(g_kernel, total, split),
        "g",
        8,
        (meta, seq_tokens, pad_bytes, ids) + small_parts,
        [SM, SM, SM, VM] + [ANY] * len(small_parts),
        (
            sds((VP, D), bf16),
            sds((nw, BLK, D), bf16),
            sds((nw, BLK, D), bf16),
            sds((2, nw, WIN, D), bf16),
            sds((16, total), f32),
        ),
        [
            pltpu.VMEM((VP, D), bf16),
            pltpu.VMEM((2 * WIN, VP), bf16),
            pltpu.VMEM((WIN, D), f32),
            pltpu.VMEM((WIN, D), f32),
            pltpu.VMEM((8, total), f32),
            pltpu.VMEM((8, total), f32),
            pltpu.VMEM((8, total), f32),
            pltpu.VMEM((8, total), f32),
            pltpu.SemaphoreType.DMA((2,)),
        ],
    )
    if split:
        n1_twin, hid_twin = twin(once(n1, mine, d_mine, teach)), twin(once(hid, mine))
        attn_parts = (query_weight, key_weight, value_weight, out_weight, mine, twin(mine))
        gu_mine = across(once(core_half(jnp.stack([gate_weight, up_weight]), 1), mine))
    else:
        n1_twin, hid_twin = twin(n1), twin(hid)
    na = len(attn_parts)
    attn_scratch = [
        pltpu.VMEM((D, 3 * hl), bf16),
        pltpu.VMEM((hl, D), bf16),
        pltpu.VMEM((BLK, total + 2 * BLK), f32),
        pltpu.VMEM((BLK, total), f32),
        pltpu.VMEM((16, 512), f32),
    ]
    q, k, v, att, lse, part, n1_full = call(
        functools.partial(a_kernel, total, split, shards_at),
        "a",
        10,
        (meta, seq_tokens, pad_bytes, ext, tab, n1, n1_twin) + attn_parts,
        [SM, SM, SM, VM, VM, VM, VM] + [ANY] * na,
        (
            sds((BLK, hl), bf16),
            sds((total, hl), bf16),
            sds((total, hl), bf16),
            sds((BLK, hl), bf16),
            sds((BLK, LANES), f32),
            sds((BLK, D), bf16),
            sds((total, D), bf16),
        ),
        attn_scratch + [pltpu.SemaphoreType.DMA((12,))],
    )
    part_other = tp_other(part)
    if split:
        gu_mine = once(gu_mine, part_other)
        d_mine = once(d_mine, part)
        mlp_parts = (gate_weight, up_weight, down_weight, gu_mine, twin(gu_mine), d_mine, twin(d_mine))
    nm = len(mlp_parts)
    mlp_scratch = [pltpu.VMEM((D, ffl), bf16), pltpu.VMEM((D, ffl), bf16), pltpu.VMEM((ffl, D), bf16)]
    res, act1, gate, up, part2 = call(
        functools.partial(b_kernel, split),
        "b",
        6,
        (meta, tab, hid, part, part_other) + mlp_parts,
        [SM, VM, VM, VM, VM] + [ANY] * nm,
        (
            sds((BLK, D), f32),
            sds((BLK, D + ffl), bf16),
            sds((BLK, ffl), f32),
            sds((BLK, ffl), f32),
            sds((BLK, D), bf16),
        ),
        mlp_scratch + [pltpu.SemaphoreType.DMA((9,))],
    )
    part2_other = tp_other(part2)
    if split:
        act1_t = twin(act1)
        part2_other = once(part2_other, act1_t)
    output, loss, gres, act2, part3 = call(
        functools.partial(c_kernel, split),
        "c",
        7,
        (meta, seq_tokens, pad_bytes, deal_targets, teach, res, part2, part2_other, gate, up) + mlp_parts,
        [SM, SM, SM, SM, VM, VM, VM, VM, VM, VM] + [ANY] * nm,
        (
            sds((BLK, D // tps), bf16),
            sds((8, LANES), f32),
            sds((BLK, D), f32),
            sds((BLK, D + 2 * ffl), bf16),
            sds((BLK, D), bf16),
        ),
        mlp_scratch + [pltpu.VMEM((BLK, D), f32), pltpu.SemaphoreType.DMA((9,))],
    )
    part3_other = tp_other(part3)
    quarter = D // 4
    half = ffl // 2
    if split:
        mlp_ins = (act1, act1_t, act2, twin(act2))
        mlp_shape = (sds((2, wloc, half), bf16),) * 2 + (sds((half, wloc), bf16),) * 2
        mlp_tmp = [pltpu.VMEM((D, half), bf16), pltpu.VMEM((half, D), bf16)]
    else:
        mlp_ins = (act1, act2)
        mlp_shape = (sds((2, D, ffl), bf16), sds((ffl, D), bf16))
        mlp_tmp = []
    mlp_pack = call(
        functools.partial(m_kernel, split, ffl), "m", 4, (meta,) + mlp_ins, [SM] + [VM] * len(mlp_ins), mlp_shape, mlp_tmp
    )
    if split:
        part3_other, *mlp_pack = lax.optimization_barrier((part3_other, *mlp_pack))
        gu_own, gu_oth, d_own, d_oth = mlp_pack
        gu_near, d_near = across(gu_oth), across(d_oth)
    attn_shape = (sds((2, 4, quarter, hl), bf16),) * 2 if split else (sds((3, D, hl), bf16), sds((hl, D), bf16))
    *attn_pack, dh_keep, dh_send, extra = call(
        functools.partial(d_kernel, total, split, shards_at, tps),
        "d",
        15,
        (meta, seq_tokens, pad_bytes, ext, ext1, tab, n1_full, q, k, v, att, lse, res, gres, hid, hid_twin, part3, part3_other) + attn_parts,
        [SM, SM, SM] + [VM] * 15 + [ANY] * na,
        attn_shape + (sds((nw, WIN, D), bf16),) * 2 + (sds((24, D), f32),),
        attn_scratch
        + [
            pltpu.VMEM((BLK, total + 3 * BLK), f32),
            pltpu.VMEM((2, 2 * BLK, total), bf16),
            pltpu.VMEM((BLK, hl), bf16),
            pltpu.VMEM((BLK, hl), bf16),
            pltpu.VMEM((total, 2 * hl), bf16),
            pltpu.VMEM((3, D, hl), bf16),
            pltpu.VMEM((hl, D), bf16),
            pltpu.VMEM((total + 2 * HALO, D), f32),
            pltpu.SemaphoreType.DMA((12,)),
        ],
    )
    if split:
        dh_send, attn_send = once(dh_send, gu_near, d_near), once(attn_pack[1], gu_near, d_near)
    def ctx_perm(x, bit):
        return lax.ppermute(x, "ctx", [(i, i ^ bit) for i in range(ccount)])

    odd = (cx // 2) % 2

    def add_halves(own, near):
        n = own.shape[0] // 2
        part = lambda x, k: lax.dynamic_slice_in_dim(x, k * n, n, 0)
        return tuple(add2(part(own, k), part(near, k)) for k in (odd, 1 - odd))

    dh_recv = twin(dh_send)
    if split:
        gu_keep, gu_send = add_halves(gu_own, gu_near)
        gu_got = ctx_perm(gu_send, 2)
        attn_own = add2(attn_pack[0], twin(attn_send))
        d_keep, d_send = add_halves(d_own, once(d_near, gu_send))
        d_got = ctx_perm(d_send, 2)
        attn_near = across(attn_own[1])
        dh_recv = once(dh_recv, attn_own, d_send)
    small_shape = (sds((2, SROWS // 2, wloc), bf16),) * 2 if split else (sds((SROWS, D), bf16),)
    small_pack = call(
        functools.partial(e_kernel, total, split, ccount),
        "e",
        9,
        (meta, seq_tokens, pad_bytes, ids, tab, conv, rows, dh_keep, dh_recv, extra, loss),
        [SM, SM, SM] + [VM] * 8,
        small_shape,
        [
            pltpu.VMEM((6, 8, total), f32),
            pltpu.VMEM((8, total), f32),
            pltpu.VMEM((8, total), f32),
            pltpu.VMEM((nw, WIN, D), bf16),
            pltpu.VMEM((2, total // 2, D), bf16),
            pltpu.VMEM((5 * SROWS, total // 2), bf16),
            pltpu.VMEM((SROWS + 8, D), f32),
        ],
    )

    if split:
        small_keep, small_send = small_pack
        gu = add2(gu_keep, once(gu_got, small_send))
        d = add2(d_keep, once(d_got, small_send))
        small_send = once(small_send, gu, d, attn_near)
        sums = add2(small_keep, twin(small_send))
        t = add2(sums[0], across(sums[1]))
        t = add2(t, tp_other(t))
        x = add2(attn_own[0], attn_near).reshape(4 * quarter, hl)
        part = lambda k: jnp.concatenate(
            [lax.dynamic_slice_in_dim(a, k * (a.shape[0] // 2), a.shape[0] // 2, 0) for a in (x, t)], axis=0
        )
        x_keep, x_send = part(odd), part(1 - odd)
        x_got = ctx_perm(x_send, 2)
        d = add2(d, once(ctx_perm(d, 4), x_send))
        gu = add2(gu, once(ctx_perm(gu, 4), x_send))
        d_o, gu_o = ctx_perm(d, 2), ctx_perm(gu, 2)
        x = add2(x_keep, once(x_got, gu))
        x = add2(x, ctx_perm(x, 4))
        x_o = ctx_perm(x, 2)
        gu_parts = [a.reshape(wloc, half) for a in (gu, gu_o, twin(gu), twin(gu_o))]
        d_parts = (d, d_o, twin(d), twin(d_o))
        gate_grad, up_grad, down_grad = call(
            f_mlp_kernel,
            "f",
            5,
            (meta, *gu_parts, *d_parts),
            [SM] + [VM] * 8,
            (sds((wloc, ffl), f32), sds((wloc, ffl), f32), sds((ffl, wloc), f32)),
            [],
        )
        attn_out = (x, x_o, twin(x), twin(once(x_o, gate_grad)))
        *attn_grads, loss, table_grad, taps_grad, shift_grad, score_grad, gain1_grad, gain2_grad, bias_grad = call(
            f_attn_kernel,
            "h",
            4,
            (meta, *attn_out),
            [SM] + [VM] * 4,
            (sds((wloc, hl), f32),) * 3
            + (
                sds((hl, wloc), f32),
                sds((1, 1), f32),
                sds((VOCAB, wloc), f32),
                sds((CONV, wloc), f32),
                sds((wloc,), f32),
                sds((wloc,), f32),
                sds((wloc,), f32),
                sds((wloc,), f32),
                sds((heads, bloc), f32),
            ),
            [pltpu.VMEM((SROWS, wloc), f32)],
            (VM,) * 4 + (SM,) + (VM,) * 7,
        )
        bias_grad = bias_grad.T
    else:

        def owner_sum(x, axis, axes="ctx"):
            return lax.psum(lax.psum_scatter(x, "fsdp", scatter_dimension=axis, tiled=True), axes).astype(f32)

        gu, down = mlp_pack
        gate_grad, up_grad = owner_sum(gu, 1)
        down_grad = owner_sum(down, 1)
        qkv, wo = attn_pack
        attn_grads = tuple(owner_sum(qkv, 1)) + (owner_sum(wo, 1),)
        (x,) = small_pack
        t = owner_sum(x, 1, ("ctx", "tp"))
        table_grad, taps_grad, shift_grad, score_grad = t[:VOCAB], t[TAP_ROW : TAP_ROW + CONV], t[SHIFT_ROW], t[SCORE_ROW]
        gain1_grad, gain2_grad = t[GAIN1_ROW], t[GAIN2_ROW]
        x = lax.dynamic_slice_in_dim(x, BIAS_ROW + 8 * tp, 8, 0)[:heads, :NB].T
        bias_grad = lax.dynamic_slice_in_dim(lax.psum(x, ("fsdp", "ctx")).astype(f32), fs * bloc, bloc, 0)
        loss = lax.psum(loss, ("fsdp", "ctx"))
    query_grad, key_grad, value_grad, out_grad = attn_grads
    return (
        output,
        table_grad,
        taps_grad,
        shift_grad,
        score_grad,
        gain1_grad,
        query_grad,
        key_grad,
        value_grad,
        bias_grad,
        out_grad,
        gain2_grad,
        gate_grad,
        up_grad,
        down_grad,
        loss[0, 0],
    )


def solution(mesh):
    both = ("fsdp", "ctx")
    in_specs = (
        P(both),
        P(),
        P(),
        P(),
        P(),
        P(None, "fsdp"),
        P(None, "fsdp"),
        P("fsdp"),
        P("fsdp"),
        P("fsdp"),
        P("fsdp", "tp"),
        P("fsdp", "tp"),
        P("fsdp", "tp"),
        P("fsdp", "tp"),
        P("tp", "fsdp"),
        P("fsdp"),
        P("fsdp", "tp"),
        P("fsdp", "tp"),
        P("tp", "fsdp"),
        P(both, None),
    )
    out_specs = (
        P(both, "tp"),
        P(None, "fsdp"),
        P(None, "fsdp"),
        P("fsdp"),
        P("fsdp"),
        P("fsdp"),
        P("fsdp", "tp"),
        P("fsdp", "tp"),
        P("fsdp", "tp"),
        P("fsdp", "tp"),
        P("tp", "fsdp"),
        P("fsdp"),
        P("fsdp", "tp"),
        P("fsdp", "tp"),
        P("tp", "fsdp"),
        P(),
    )
    return jax.shard_map(shards, mesh=mesh, in_specs=in_specs, out_specs=out_specs, check_vma=False)
```
